32 devices in a mesh: dp: 8 (over z, x), tp: 4 (over y, core).
Axes of the slice: x: 2, y: 2, z: 4, core: 2. Of those that a mesh axis runs over, the one named last changes fastest.
Arguments:
- inputs: bfloat16 [2, 4096, 768], P(None, 'dp'), may hold values from -6 to 6
- cotangent: bfloat16 [2, 4096, 768], P(None, 'dp'), may hold values from -6 to 6
- item_ids: int32 [2, 4096], P(None, 'dp'), may hold values from 0 to 3584, as said below
- timestep: int32 [2, 8], P(None, 'dp'), may hold values from 0 to 999
- qkv_weight: float32 [768, 3, 768], P('dp', None, 'tp'), may hold values from -0.21875 to 0.21875
- out_weight: float32 [768, 768], P('tp', 'dp'), may hold values from -0.625 to 0.625
- up_weight: float32 [768, 3072], P('dp', 'tp'), may hold values from -0.21875 to 0.21875
- down_weight: float32 [3072, 768], P('tp', 'dp'), may hold values from -0.109375 to 0.109375
- norm_params: float32 [4, 768], P(None, 'dp')
- qkv_first: float32 [768, 3, 768], P('dp', None, 'tp'), may hold values from -0.00061035156 to 0.00061035156
- out_first: float32 [768, 768], P('tp', 'dp'), may hold values from -0.00061035156 to 0.00061035156
- up_first: float32 [768, 3072], P('dp', 'tp'), may hold values from -0.00061035156 to 0.00061035156
- down_first: float32 [3072, 768], P('tp', 'dp'), may hold values from -0.00061035156 to 0.00061035156
- norm_first: float32 [4, 768], P(None, 'dp'), may hold values from -0.001953125 to 0.001953125
- qkv_second: float32 [768, 3, 768], P('dp', None, 'tp'), may hold values from 1.4122378e-10 to 5.6489513e-10
- out_second: float32 [768, 768], P('tp', 'dp'), may hold values from 1.4122378e-10 to 5.6489513e-10
- up_second: float32 [768, 3072], P('dp', 'tp'), may hold values from 1.4122378e-10 to 5.6489513e-10
- down_second: float32 [3072, 768], P('tp', 'dp'), may hold values from 1.4122378e-10 to 5.6489513e-10
- norm_second: float32 [4, 768], P(None, 'dp'), may hold values from 1.4122379e-09 to 5.6489515e-09
Outputs:
- block_out: bfloat16 [2, 4096, 768], P(None, 'dp')
- input_grad: float32 [2, 4096, 768], P(None, 'dp')
- grad_norm: float32 [], replicated
- qkv_new: float32 [768, 3, 768], P('dp', None, 'tp')
- qkv_first_new: float32 [768, 3, 768], P('dp', None, 'tp')
- qkv_second_new: float32 [768, 3, 768], P('dp', None, 'tp')
- out_new: float32 [768, 768], P('tp', 'dp')
- out_first_new: float32 [768, 768], P('tp', 'dp')
- out_second_new: float32 [768, 768], P('tp', 'dp')
- up_new: float32 [768, 3072], P('dp', 'tp')
- up_first_new: float32 [768, 3072], P('dp', 'tp')
- up_second_new: float32 [768, 3072], P('dp', 'tp')
- down_new: float32 [3072, 768], P('tp', 'dp')
- down_first_new: float32 [3072, 768], P('tp', 'dp')
- down_second_new: float32 [3072, 768], P('tp', 'dp')
- norm_new: float32 [4, 768], P(None, 'dp')
- norm_first_new: float32 [4, 768], P(None, 'dp')
- norm_second_new: float32 [4, 768], P(None, 'dp')
The draws below stay inside these ranges and needn't reach their ends.
Inputs may be any that keep to these rules, and one draw needn't show every extreme that they name: `item_ids`: A token's id is the index, within its micro-batch, of its item's first token, so ids never decrease along a micro-batch; every block of 512 tokens of one index of dp starts a new item, so no item spans two blocks; an item has 1 to 512 tokens and in every draw some item has exactly 512.
All inputs are finite; a program needn't handle non-finite values.
Results may differ from the reference program's by a relative error of at most 0.009.
Values may be sent and summed in bfloat16 or wider, within the bound.
A program may use at most 128 MiB of HBM per device.

```python
import math
import jax
import jax.numpy as jnp
from jax import lax

D = 768
HEADS = 12
HEAD_DIM = 64
FF = 3072
TOK_MB = 512
MB = 2
STEP = 10
HDALL = 768
TOKENS_MB = 4096
PARAMS = 7080960
N_DP = 8


def draw_item_ids(key, part):
    key_long, key_cut = jax.random.split(key)
    blocks = TOKENS_MB // TOK_MB
    whole_block = jax.random.randint(key_long, (MB, blocks), 0, 4) == 0
    first_block = (jnp.arange(MB)[:, None] == 0) & (jnp.arange(blocks)[None, :] == 0)
    last_block = jnp.arange(blocks)[None, :] == blocks - 1
    whole_block = whole_block | first_block | last_block
    whole_rows = jnp.repeat(whole_block, TOK_MB, axis=1)
    cut_marks = jax.random.randint(key_cut, (MB, TOKENS_MB), 0, 24) == 0
    position = jnp.broadcast_to(jnp.arange(TOKENS_MB, dtype=jnp.int32)[None, :], (MB, TOKENS_MB))
    starts = (position % TOK_MB == 0) | cut_marks & jnp.logical_not(whole_rows)
    marked = jnp.where(starts, position, jnp.zeros_like(position))
    return lax.cummax(marked, axis=1).astype(jnp.int32)


def draw_norm_params(key, part):
    noise_draw = jax.random.normal(key, (4, D), jnp.float32)
    row_index = jnp.arange(4)[:, None]
    return jnp.where(row_index % 2 == 0, 0.02 * noise_draw, 0.03 * noise_draw)


def place_ends(array, stream_key, low, high):
    place = [jax.random.randint(jax.random.fold_in(stream_key, axis), (), 0, length) for axis, length in enumerate(array.shape)]
    widest = array.shape.index(max(array.shape))
    beside = place[:widest] + [(place[widest] + 1) % array.shape[widest]] + place[widest + 1:]
    return array.at[tuple(place)].set(low).at[tuple(beside)].set(high)


def block_scale(own_key, dims, cuts, least, high):
    def one(dim, shards_of):
        steps = jax.random.uniform(jax.random.fold_in(jax.random.fold_in(own_key, 6), dim), (shards_of,), jnp.float32, least / len(cuts), high / len(cuts))
        return jnp.repeat(jnp.exp(steps), dims[dim] // shards_of).reshape((-1,) + (1,) * (len(dims) - dim - 1))

    gain = one(*cuts[0])
    for cut in cuts[1:]:
        gain = gain * one(*cut)
    return gain


def centred(stream_key, dims, scale, reach, pieces=(), held_as=jnp.bfloat16):
    factor_of = block_scale(stream_key, dims, pieces, -0.22, 0.18) if pieces else 1.0
    values = jax.random.normal(stream_key, dims, jnp.float32) * scale * factor_of
    return jnp.minimum(jnp.maximum(values, -reach), reach).astype(held_as)


def setup_inputs(seed: int = 0) -> dict:
    keys = jax.random.split(jax.random.key(seed), 20)
    inputs = centred(keys[0], (MB, TOKENS_MB, D), 1.0, 6.0, ((1, 8),))
    cotangent = centred(keys[1], (MB, TOKENS_MB, D), 1.0, 6.0, ((1, 8),))
    item_ids = draw_item_ids(jax.random.fold_in(keys[19], 71), 0)
    timestep = place_ends(jax.random.randint(keys[3], (MB, N_DP), 0, 1000), jax.random.fold_in(keys[3], 1), 0, 999).astype(jnp.int32)
    qkv_weight = centred(keys[4], (D, 3, HDALL), D ** -0.5, 0.21875, ((0, 8), (2, 4)), jnp.float32)
    out_weight = centred(keys[5], (HDALL, D), (HDALL // 8) ** -0.5, 0.625, ((0, 4), (1, 8)), jnp.float32)
    up_weight = centred(keys[6], (D, FF), D ** -0.5, 0.21875, ((0, 8), (1, 4)), jnp.float32)
    down_weight = centred(keys[7], (FF, D), FF ** -0.5, 0.109375, ((0, 4), (1, 8)), jnp.float32)
    norm_params = draw_norm_params(jax.random.fold_in(keys[19], 71), 0)
    qkv_first = centred(keys[9], (D, 3, HDALL), (0.11 * PARAMS ** -0.5), 0.00061035156, ((0, 8), (2, 4)), jnp.float32)
    out_first = centred(keys[10], (HDALL, D), (0.11 * PARAMS ** -0.5), 0.00061035156, ((0, 4), (1, 8)), jnp.float32)
    up_first = centred(keys[11], (D, FF), (0.11 * PARAMS ** -0.5), 0.00061035156, ((0, 8), (1, 4)), jnp.float32)
    down_first = centred(keys[12], (FF, D), (0.11 * PARAMS ** -0.5), 0.00061035156, ((0, 4), (1, 8)), jnp.float32)
    norm_first = centred(keys[13], (4, D), (0.35 * PARAMS ** -0.5), 0.001953125, ((1, 8),), jnp.float32)
    qkv_second = jnp.clip(jnp.exp(math.log(5.648951306724825e-10) - 1.3862944 * jax.random.uniform(keys[14], (D, 3, HDALL), jnp.float32) ** block_scale(keys[14], (D, 3, HDALL), ((0, 8), (2, 4)), -0.2, 0.2)), 1.4122378266812063e-10, 5.648951306724825e-10)
    out_second = jnp.clip(jnp.exp(math.log(5.648951306724825e-10) - 1.3862944 * jax.random.uniform(keys[15], (HDALL, D), jnp.float32) ** block_scale(keys[15], (HDALL, D), ((0, 4), (1, 8)), -0.2, 0.2)), 1.4122378266812063e-10, 5.648951306724825e-10)
    up_second = jnp.clip(jnp.exp(math.log(5.648951306724825e-10) - 1.3862944 * jax.random.uniform(keys[16], (D, FF), jnp.float32) ** block_scale(keys[16], (D, FF), ((0, 8), (1, 4)), -0.2, 0.2)), 1.4122378266812063e-10, 5.648951306724825e-10)
    down_second = jnp.clip(jnp.exp(math.log(5.648951306724825e-10) - 1.3862944 * jax.random.uniform(keys[17], (FF, D), jnp.float32) ** block_scale(keys[17], (FF, D), ((0, 4), (1, 8)), -0.2, 0.2)), 1.4122378266812063e-10, 5.648951306724825e-10)
    norm_second = jnp.clip(jnp.exp(math.log(5.64895152876943e-09) - 1.3862944 * jax.random.uniform(keys[18], (4, D), jnp.float32) ** block_scale(keys[18], (4, D), ((1, 8),), -0.2, 0.2)), 1.4122378821923576e-09, 5.64895152876943e-09)
    return {"inputs": inputs, "cotangent": cotangent, "item_ids": item_ids, "timestep": timestep, "qkv_weight": qkv_weight, "out_weight": out_weight, "up_weight": up_weight, "down_weight": down_weight, "norm_params": norm_params, "qkv_first": qkv_first, "out_first": out_first, "up_first": up_first, "down_first": down_first, "norm_first": norm_first, "qkv_second": qkv_second, "out_second": out_second, "up_second": up_second, "down_second": down_second, "norm_second": norm_second}


@jax.custom_vjp
def low(v):
    return lax.optimization_barrier(v.astype(jnp.bfloat16)).astype(jnp.float32)

@jax.custom_vjp
def low_back(v):
    return v

def low_keep(v):
    return (low(v), None)

def low_pass(kept, grad):
    return (grad,)

def back_keep(v):
    return (v, None)

def back_low(kept, grad):
    return (low(grad),)
low.defvjp(low_keep, low_pass)
low_back.defvjp(back_keep, back_low)
norm_eps = 1e-05
clip_limit = 1.0
learn_rate = 0.02
beta_one = 0.9
beta_two = 0.999
adam_eps = 1e-08
weight_decay = 0.01
highest = lax.Precision.HIGHEST

def time_embed(step_values):
    half_width = D // 2
    frequency = jnp.exp(jnp.arange(half_width, dtype=jnp.float32) * (-math.log(10000.0) / half_width))
    angles = step_values.astype(jnp.float32)[..., None] * frequency
    return jnp.concatenate([jnp.sin(angles), jnp.cos(angles)], axis=-1)

def layer_norm(values, gain_row, bias_row):
    centre = values - lax.optimization_barrier(jnp.mean(values, axis=-1, keepdims=True))
    spread = lax.optimization_barrier(jnp.mean(centre * centre, axis=-1, keepdims=True))
    return centre * lax.rsqrt(spread + norm_eps) * gain_row + bias_row

def attend(packed):
    triple, labels = packed
    split_shape = (TOK_MB, HEADS, HEAD_DIM)
    query_rows = triple[0].reshape(split_shape)
    key_rows = triple[1].reshape(split_shape)
    value_rows = triple[2].reshape(split_shape)
    scores = low_back(jnp.einsum('thd,shd->hts', query_rows, key_rows, precision=highest) * (1.0 / math.sqrt(HEAD_DIM)))
    same_item = labels[:, None] == labels[None, :]
    scores = jnp.where(same_item[None], scores, -1e+30)
    probs_soft = low(jax.nn.softmax(scores, axis=-1))
    context = jnp.einsum('hts,shd->thd', probs_soft, value_rows, precision=highest)
    return low_back(low(context.reshape(TOK_MB, HDALL)))

def forward(inputs_f, qkv_mat, out_mat, up_mat, down_mat, norm_rows, embeds, labels):
    micro_count = MB * N_DP
    qkv_low = low(qkv_mat)
    out_low = low(out_mat)
    up_low = low(up_mat)
    down_low = low(down_mat)
    norm_gains = low(norm_rows)
    stream = inputs_f.reshape(micro_count, TOK_MB, D) + embeds.reshape(micro_count, 1, D)
    normed = low(layer_norm(stream, 1.0 + norm_gains[0], norm_gains[1]))
    triple = low_back(low(jnp.einsum('btd,dje->bjte', normed, qkv_low, precision=highest)))
    context = lax.map(jax.checkpoint(attend), (triple, labels.reshape(micro_count, TOK_MB)))
    attn_out = low_back(jnp.einsum('btc,cd->btd', context, out_low, precision=highest))
    middle = stream + attn_out
    normed_two = low(layer_norm(middle, 1.0 + norm_gains[2], norm_gains[3]))
    hidden_pre = low_back(jnp.einsum('btd,df->btf', normed_two, up_low, precision=highest))
    hidden = low(jax.nn.gelu(hidden_pre, approximate=False))
    branch = low_back(jnp.einsum('btf,fd->btd', hidden, down_low, precision=highest))
    return (middle + branch).reshape(MB, N_DP * TOK_MB, D)

def adam_step(weight, gradient, first_old, second_old):
    first_new = beta_one * first_old + (1.0 - beta_one) * gradient
    second_new = beta_two * second_old + (1.0 - beta_two) * gradient * gradient
    moment_one = first_new / (1.0 - beta_one ** STEP)
    moment_two = second_new / (1.0 - beta_two ** STEP)
    weight_new = weight - learn_rate * (moment_one / (jnp.sqrt(moment_two) + adam_eps) + weight_decay * weight)
    return (weight_new, first_new, second_new)

def reference(inputs, cotangent, item_ids, timestep, qkv_weight, out_weight, up_weight, down_weight, norm_params, qkv_first, out_first, up_first, down_first, norm_first, qkv_second, out_second, up_second, down_second, norm_second):
    embeds = time_embed(timestep)

    def run_layer(inputs_f, qkv_mat, out_mat, up_mat, down_mat, norm_rows):
        return forward(inputs_f, qkv_mat, out_mat, up_mat, down_mat, norm_rows, embeds, item_ids)
    block_out, pullback = jax.vjp(run_layer, inputs.astype(jnp.float32), qkv_weight, out_weight, up_weight, down_weight, norm_params)
    grad_list = pullback(cotangent.astype(jnp.float32))
    input_grad = grad_list[0]
    weight_grads = grad_list[1:]
    squares = jnp.sum(weight_grads[0] * weight_grads[0])
    for gradient in weight_grads[1:]:
        squares = squares + jnp.sum(gradient * gradient)
    grad_norm = jnp.sqrt(squares)
    factor = jnp.minimum(1.0, clip_limit / (grad_norm + 1e-06))
    weights = (qkv_weight, out_weight, up_weight, down_weight, norm_params)
    firsts = (qkv_first, out_first, up_first, down_first, norm_first)
    seconds = (qkv_second, out_second, up_second, down_second, norm_second)
    result = [adam_step(weights[index], weight_grads[index] * factor, firsts[index], seconds[index]) for index in range(5)]
    return (block_out.astype(jnp.bfloat16), input_grad, grad_norm, result[0][0], result[0][1], result[0][2], result[1][0], result[1][1], result[1][2], result[2][0], result[2][1], result[2][2], result[3][0], result[3][1], result[3][2], result[4][0], result[4][1], result[4][2])
```

```python
from functools import partial
import math

import jax
import jax.numpy as jnp
from jax import lax
from jax.experimental import pallas as pl
from jax.experimental.pallas import tpu as pltpu
from jax.sharding import PartitionSpec as P

HEAD_DIM = 64
STEP = 10

norm_eps = 1e-05
clip_limit = 1.0
learn_rate = 0.02
beta_one = 0.9
beta_two = 0.999
adam_eps = 1e-08
weight_decay = 0.01

BF = jnp.bfloat16
F32 = jnp.float32
MESH = pl.DeviceIdType.MESH


def time_embed(step_values, model_width):
    half_width = model_width // 2
    frequency = jnp.exp(
        jnp.arange(half_width, dtype=jnp.float32) * (-math.log(10000.0) / half_width)
    )
    angles = step_values.astype(jnp.float32)[..., None] * frequency
    return jnp.concatenate([jnp.sin(angles), jnp.cos(angles)], axis=-1)


def adam_step(weight, gradient, first_old, second_old):
    first_new = beta_one * first_old + (1.0 - beta_one) * gradient
    second_new = beta_two * second_old + (1.0 - beta_two) * gradient * gradient
    moment_one = first_new / (1.0 - beta_one**STEP)
    moment_two = second_new / (1.0 - beta_two**STEP)
    weight_new = weight - learn_rate * (
        moment_one / (jnp.sqrt(moment_two) + adam_eps) + weight_decay * weight
    )
    return (weight_new, first_new, second_new)


def mm(a, b, ca, cb):
    return lax.dot_general(a, b, (((ca,), (cb,)), ((), ())), preferred_element_type=F32)


def layer_kernel(
    dims,
    x_ref, cot_ref, emb_ref, lc_ref, lr_ref, ain_ref, bin_ref, npin_ref,
    bo_ref, ig_ref, ga_ref, gb_ref, gn_ref, gs_ref,
    wa, wb, npg, npt, normed, qkv, probs, ctx, n2, hid, dpre, mid, dmid, bo_own, dattn, dqkv,
    csend, crecv, own, ysend, yrecv,
    rax_s, rax_r, rao, raz_s, raz_r,
    rbx_s, rbx_r, rbo, rbz_s, rbz_r,
    nacc, ncore, nsum, sqd, sqt,
    ag_zs, ag_zr, ag_xs, ag_xr, np_s, np_r,
    c_s, c_r, y_s, y_r, g_s, g_r, o_l,
    rx_s, rx_r, rz_s, rz_r, nc_s, nc_r, nd_s, nd_r, qd_s, qd_r, qt_s, qt_r,
):
    micro, tok, width, n_dp, n_tp, heads = dims
    n_z = n_dp // 2
    half = tok // 2
    own_rows = width // n_dp
    local = heads * HEAD_DIM
    scale = 1.0 / math.sqrt(HEAD_DIM)

    dp = lax.axis_index("dp")
    tp = lax.axis_index("tp")
    z, xx = lax.div(dp, 2), lax.rem(dp, 2)
    yy, cc = lax.div(tp, 2), lax.rem(tp, 2)
    x_peer = (2 * z + 1 - xx, tp)
    c_peer = (dp, 2 * yy + 1 - cc)
    y_peer = (dp, 2 * (1 - yy) + cc)

    def z_of(k):
        return lax.rem(z + k, n_z)

    def z_peer(k):
        return (2 * z_of(k) + xx, tp)

    def dp_of(k):
        return lax.rem(dp + k, n_dp)

    def tp_of(k):
        return lax.rem(tp + k, n_tp)

    sent = []

    def copy(src, dst, s_sem, r_sem, peer):
        return pltpu.make_async_remote_copy(
            src_ref=src, dst_ref=dst, send_sem=s_sem, recv_sem=r_sem, device_id=peer, device_id_type=MESH
        )

    def send(src, dst, s_sem, r_sem, peer):
        item = copy(src, dst, s_sem, r_sem, peer)
        item.start()
        sent.append(item)

    def arrive(dst, s_sem, r_sem, peer):
        copy(dst, dst, s_sem, r_sem, peer).wait_recv()

    barrier = pltpu.get_barrier_semaphore()
    for k in range(1, n_dp):
        pl.semaphore_signal(barrier, inc=1, device_id=(dp_of(k), tp), device_id_type=MESH)
    for k in range(1, n_tp):
        pl.semaphore_signal(barrier, inc=1, device_id=(dp, tp_of(k)), device_id_type=MESH)
    pl.semaphore_wait(barrier, n_dp + n_tp - 2)

    def rows_of(j):
        return pl.ds(pl.multiple_of(j * own_rows, own_rows), own_rows)

    def half_rows(h):
        return pl.ds(pl.multiple_of(h * half, half), half)

    mine = half_rows(cc)
    other = half_rows(1 - cc)

    def ag_src(g):
        return (ain_ref.at[pl.ds(0, 3)], ain_ref.at[3], bin_ref.at[0], bin_ref.at[1])[g]

    def ag_at(g, j):
        r = rows_of(j)
        return (wa.at[pl.ds(0, 3), r], wa.at[3, r], wb.at[0, r], wb.at[1, r])[g]

    for k in range(1, n_dp):
        send(npin_ref, npg.at[rows_of(dp)], np_s.at[k], np_r.at[k], (dp_of(k), tp))
    for g in range(4):
        for k in range(1, n_z):
            send(ag_src(g), ag_at(g, dp), ag_zs.at[g, k], ag_zr.at[g, k], z_peer(k))
        send(ag_src(g), ag_at(g, dp), ag_xs.at[g, 0], ag_xr.at[g, 0], x_peer)
    npg[rows_of(dp), :] = npin_ref[...]
    wa[:, rows_of(dp), :] = ain_ref[...]
    wb[:, rows_of(dp), :] = bin_ref[...]

    def ag_forward(g):
        for k in range(1, n_z):
            j = 2 * lax.rem(z + n_z - k, n_z) + xx
            arrive(ag_at(g, j), ag_zs.at[g, k], ag_zr.at[g, k], z_peer(k))
            send(ag_at(g, j), ag_at(g, j), ag_xs.at[g, k], ag_xr.at[g, k], x_peer)

    def ag_finish(g):
        for k in range(n_z):
            j = 2 * lax.rem(z + n_z - k, n_z) + 1 - xx
            arrive(ag_at(g, j), ag_xs.at[g, k], ag_xr.at[g, k], x_peer)

    def ar_start(kind, m, part):
        slot = kind % 2
        csend[kind, m] = part(other).astype(BF)
        send(csend.at[kind, m], crecv.at[kind, m], c_s.at[kind, m], c_r.at[kind, m], c_peer)
        own[slot, m] = part(mine)

    def ar_cross(kind, m):
        arrive(crecv.at[kind, m], c_s.at[kind, m], c_r.at[kind, m], c_peer)
        ysend[kind, m] = (own[kind % 2, m] + crecv[kind, m].astype(F32)).astype(BF)
        send(ysend.at[kind, m], yrecv.at[kind, m], y_s.at[kind, m], y_r.at[kind, m], y_peer)

    def ar_total(kind, m):
        arrive(yrecv.at[kind, m], y_s.at[kind, m], y_r.at[kind, m], y_peer)
        return ysend[kind, m].astype(F32) + yrecv[kind, m].astype(F32)

    def share(kind, m, ref):
        send(ref.at[m, mine], ref.at[m, mine], g_s.at[kind, m], g_r.at[kind, m], c_peer)

    def shared(kind, m, ref):
        arrive(ref.at[m, other], g_s.at[kind, m], g_r.at[kind, m], c_peer)

    def centred(v):
        c0 = v - jnp.mean(v, axis=-1, keepdims=True)
        return c0, lax.rsqrt(jnp.mean(c0 * c0, axis=-1, keepdims=True) + norm_eps)

    def norm_back(grad, hat, inv, gain):
        dhat = grad * gain
        return inv * (
            dhat
            - jnp.mean(dhat, axis=-1, keepdims=True)
            - hat * jnp.mean(dhat * hat, axis=-1, keepdims=True)
        )

    def gain_row(i):
        return 1.0 + npt[pl.ds(i, 1), :]

    def bias_row(i):
        return npt[pl.ds(i, 1), :]

    def stream_of(m, rows):
        return x_ref[m, rows, :].astype(F32) + emb_ref[m]

    def first_norm(m):
        c0, inv = centred(stream_of(m, pl.ds(0, tok)))
        normed[m] = (c0 * inv * gain_row(0) + bias_row(1)).astype(BF)

    def project(m):
        for i in range(3):
            qkv[i, m] = mm(normed[m], wa[i], 1, 0).astype(BF)

    lane = lax.broadcasted_iota(jnp.int32, (1, local), 1)

    def head_mask(h, value):
        here = (lane >= h * HEAD_DIM) & (lane < (h + 1) * HEAD_DIM)
        return jnp.where(here, value, 0.0).astype(BF)

    def attend(m):
        same = lc_ref[m] == lr_ref[m]
        total = None
        for h in range(heads):
            s = mm(qkv[0, m] * head_mask(h, scale), qkv[1, m], 1, 1)
            s = jnp.where(same, s, -1e30)
            e = jnp.exp(s - jnp.max(s, axis=-1, keepdims=True))
            p = e * (1.0 / jnp.sum(e, axis=-1, keepdims=True))
            probs[m, h] = p
            part = mm(p.astype(BF), qkv[2, m] * head_mask(h, 1.0), 1, 0)
            total = part if total is None else total + part
        ctx[m] = total.astype(BF)

    def attn_part(m):
        return lambda rows: mm(ctx[m, rows, :], wa[3], 1, 1)

    def second_norm(m):
        middle = stream_of(m, mine) + ar_total(0, m)
        mid[m] = middle
        c0, inv = centred(middle)
        n2[m, mine, :] = (c0 * inv * gain_row(2) + bias_row(3)).astype(BF)
        share(0, m, n2)

    def feed(m):
        shared(0, m, n2)
        pre = mm(n2[m], wb[0], 1, 0)
        cdf = 0.5 * (1.0 + lax.erf(pre * math.sqrt(0.5)))
        hid[m] = (pre * cdf).astype(BF)
        slope = cdf + pre * (jnp.exp(-0.5 * pre * pre) * (1.0 / math.sqrt(2.0 * math.pi)))
        dpre[m] = (mm(cot_ref[m], wb[1], 1, 0) * slope).astype(BF)

    def dn2_part(m):
        return lambda rows: mm(dpre[m, rows, :], wb[0], 1, 1)

    def branch_part(m):
        return lambda rows: mm(hid[m, rows, :], wb[1], 1, 1)

    def col_sum(v):
        return jnp.sum(v, axis=0, keepdims=True)

    def second_back(m):
        grad = ar_total(1, m)
        c0, inv = centred(mid[m])
        hat = c0 * inv
        nacc[m, pl.ds(0, 1), :] = col_sum(grad * hat)
        nacc[m, pl.ds(1, 1), :] = col_sum(grad)
        grad_middle = cot_ref[m, mine, :].astype(F32) + norm_back(grad, hat, inv, gain_row(2))
        dmid[m] = grad_middle
        dattn[m, mine, :] = grad_middle.astype(BF)
        share(1, m, dattn)

    def finish_block(m):
        bo_own[m] = (mid[m] + ar_total(2, m)).astype(BF)
        send(bo_own.at[m], bo_ref.at[m, mine], g_s.at[2, m], g_r.at[2, m], c_peer)
        pltpu.make_async_copy(bo_own.at[m], bo_ref.at[m, mine], o_l.at[0, m]).start()

    def attend_back(m):
        shared(1, m, dattn)
        dctx = mm(dattn[m], wa[3], 1, 0).astype(BF)
        dq = dk = dv = None
        for h in range(heads):
            dch = dctx * head_mask(h, 1.0)
            p = probs[m, h]
            dp_ = mm(dch, qkv[2, m], 1, 1)
            inner = jnp.sum(dp_ * p, axis=-1, keepdims=True)
            ds = (p * (dp_ - inner)).astype(BF)
            mask = head_mask(h, scale)
            a = mm(ds, qkv[1, m] * mask, 1, 0)
            b = mm(ds, qkv[0, m] * mask, 0, 0)
            c = mm(p.astype(BF), dch, 0, 0)
            dq = a if dq is None else dq + a
            dk = b if dk is None else dk + b
            dv = c if dv is None else dv + c
        dqkv[0, m] = dq.astype(BF)
        dqkv[1, m] = dk.astype(BF)
        dqkv[2, m] = dv.astype(BF)

    def dn1_part(m):
        def part(rows):
            total = mm(dqkv[0, m, rows, :], wa[0], 1, 1)
            for i in range(1, 3):
                total = total + mm(dqkv[i, m, rows, :], wa[i], 1, 1)
            return total

        return part

    def first_back(m):
        grad = ar_total(3, m)
        c0, inv = centred(stream_of(m, mine))
        hat = c0 * inv
        nacc[m, pl.ds(2, 1), :] = col_sum(grad * hat)
        nacc[m, pl.ds(3, 1), :] = col_sum(grad)
        dmid[m] = dmid[m] + norm_back(grad, hat, inv, gain_row(0))
        send(dmid.at[m], ig_ref.at[m, mine], g_s.at[3, m], g_r.at[3, m], c_peer)
        pltpu.make_async_copy(dmid.at[m], ig_ref.at[m, mine], o_l.at[1, m]).start()

    def rs_refs(g):
        if g < 4:
            return rax_s.at[g], rax_r.at[g], rao.at[g], raz_s.at[g], raz_r.at[g]
        return rbx_s.at[g - 4], rbx_r.at[g - 4], rbo.at[g - 4], rbz_s.at[g - 4], rbz_r.at[g - 4]

    def rs_start(g, grad):
        xs, xr, keep, _, _ = rs_refs(g)
        blocks = grad.reshape(n_z, 2, own_rows, grad.shape[-1])
        left = xx == 0
        xs[...] = jnp.where(left, blocks[:, 1], blocks[:, 0]).astype(BF)
        send(xs, xr, rx_s.at[g], rx_r.at[g], x_peer)
        keep[...] = jnp.where(left, blocks[:, 0], blocks[:, 1])

    def rs_cross(g):
        xs, xr, keep, zs, zr = rs_refs(g)
        arrive(xr, rx_s.at[g], rx_r.at[g], x_peer)
        both = keep[...] + xr[...].astype(F32)
        keep[...] = both
        zs[...] = both.astype(BF)
        for k in range(1, n_z):
            send(zs.at[z_of(k)], zr.at[k], rz_s.at[g, k], rz_r.at[g, k], z_peer(k))

    def rs_finish(g):
        _, _, keep, _, zr = rs_refs(g)
        total = keep[z]
        for k in range(1, n_z):
            arrive(zr.at[k], rz_s.at[g, k], rz_r.at[g, k], z_peer(k))
            total = total + zr[k].astype(F32)
        if g < 4:
            ga_ref[g] = total
        else:
            gb_ref[g - 4] = total
        return jnp.sum(jnp.sum(total * total, axis=0, keepdims=True), axis=1, keepdims=True)

    def flat(ref):
        return ref[...].reshape(micro * tok, ref.shape[-1])

    def norm_start(e):
        both = nacc[0, pl.ds(2 * e, 2), :]
        for m in range(1, micro):
            both = both + nacc[m, pl.ds(2 * e, 2), :]
        ncore[e, 0] = both
        send(ncore.at[e, 0], ncore.at[e, 1], nc_s.at[e], nc_r.at[e], c_peer)

    def norm_cross(e):
        arrive(ncore.at[e, 1], nc_s.at[e], nc_r.at[e], c_peer)
        nsum[e, dp] = ncore[e, 0] + ncore[e, 1]
        for k in range(1, n_dp):
            send(nsum.at[e, dp], nsum.at[e, dp], nd_s.at[e, k], nd_r.at[e, k], (dp_of(k), tp))

    def norm_finish(e):
        for k in range(1, n_dp):
            j = lax.rem(dp + n_dp - k, n_dp)
            arrive(nsum.at[e, j], nd_s.at[e, k], nd_r.at[e, k], (dp_of(k), tp))
        total = nsum[e, 0]
        for j in range(1, n_dp):
            total = total + nsum[e, j]
        gn_ref[e] = total
        return jnp.sum(jnp.sum(total * total, axis=0, keepdims=True), axis=1, keepdims=True)

    for k in range(1, n_dp):
        j = lax.rem(dp + n_dp - k, n_dp)
        arrive(npg.at[rows_of(j)], np_s.at[k], np_r.at[k], (dp_of(k), tp))
    npt[...] = npg[...].T
    first_norm(0)
    first_norm(1)
    ag_forward(0)
    ag_finish(0)
    project(0)
    ag_forward(1)
    attend(0)
    ag_finish(1)
    ar_start(0, 0, attn_part(0))
    project(1)
    ar_cross(0, 0)
    ag_forward(2)
    attend(1)
    ar_start(0, 1, attn_part(1))
    second_norm(0)
    ag_forward(3)
    ar_cross(0, 1)
    ag_finish(2)
    ag_finish(3)
    feed(0)
    ar_start(1, 0, dn2_part(0))
    second_norm(1)
    ar_cross(1, 0)
    ar_start(2, 0, branch_part(0))
    feed(1)
    ar_cross(2, 0)
    ar_start(1, 1, dn2_part(1))
    second_back(0)
    ar_cross(1, 1)
    ar_start(2, 1, branch_part(1))
    rs_start(5, mm(flat(cot_ref), flat(hid), 0, 0))
    rs_start(4, mm(flat(n2), flat(dpre), 0, 0))
    finish_block(0)
    ar_cross(2, 1)
    attend_back(0)
    rs_cross(5)
    ar_start(3, 0, dn1_part(0))
    second_back(1)
    ar_cross(3, 0)
    norm_start(0)
    finish_block(1)
    attend_back(1)
    rs_cross(4)
    ar_start(3, 1, dn1_part(1))
    norm_cross(0)
    rs_start(0, mm(flat(normed), flat(dqkv.at[0]), 0, 0))
    ar_cross(3, 1)
    rs_start(1, mm(flat(normed), flat(dqkv.at[1]), 0, 0))
    rs_start(2, mm(flat(normed), flat(dqkv.at[2]), 0, 0))
    rs_start(3, mm(flat(dattn), flat(ctx), 0, 0))
    first_back(0)
    rs_cross(0)
    rs_cross(1)
    rs_cross(2)
    rs_cross(3)
    first_back(1)
    norm_start(1)
    squares = rs_finish(5) + rs_finish(4)
    norm_cross(1)
    for g in range(4):
        squares = squares + rs_finish(g)
    sqd[dp] = jnp.broadcast_to(squares, (8, 128))
    for k in range(1, n_dp):
        send(sqd.at[dp], sqd.at[dp], qd_s.at[k], qd_r.at[k], (dp_of(k), tp))
    extra = norm_finish(0) + norm_finish(1)
    for k in range(1, n_dp):
        j = lax.rem(dp + n_dp - k, n_dp)
        arrive(sqd.at[j], qd_s.at[k], qd_r.at[k], (dp_of(k), tp))
    mesh_row = sqd[0]
    for j in range(1, n_dp):
        mesh_row = mesh_row + sqd[j]
    sqt[tp] = mesh_row
    for k in range(1, n_tp):
        send(sqt.at[tp], sqt.at[tp], qt_s.at[k], qt_r.at[k], (dp, tp_of(k)))
    for k in range(1, n_tp):
        j = lax.rem(tp + n_tp - k, n_tp)
        arrive(sqt.at[j], qt_s.at[k], qt_r.at[k], (dp, tp_of(k)))
    everything = sqt[0]
    for j in range(1, n_tp):
        everything = everything + sqt[j]
    gs_ref[...] = jnp.sqrt(everything + extra)

    for m in range(micro):
        arrive(bo_ref.at[m, other], g_s.at[2, m], g_r.at[2, m], c_peer)
        arrive(ig_ref.at[m, other], g_s.at[3, m], g_r.at[3, m], c_peer)
        pltpu.make_async_copy(bo_own.at[m], bo_ref.at[m, mine], o_l.at[0, m]).wait()
        pltpu.make_async_copy(dmid.at[m], ig_ref.at[m, mine], o_l.at[1, m]).wait()
    for item in sent:
        item.wait_send()


def layer_call(n_dp, n_tp, inputs, cotangent, item_ids, embeds, a_in, b_in, np_in):
    micro, tok, width = inputs.shape
    _, own_rows, local = a_in.shape
    ff = b_in.shape[2]
    heads = local // HEAD_DIM
    half = tok // 2
    n_z = n_dp // 2
    dims = (micro, tok, width, n_dp, n_tp, heads)
    V = pltpu.VMEM
    DMA = pltpu.SemaphoreType.DMA
    scratch = [
        V((4, width, local), BF), V((2, width, ff), BF), V((width, 128), F32), V((128, width), F32),
        V((micro, tok, width), BF), V((3, micro, tok, local), BF), V((micro, heads, tok, tok), F32),
        V((micro, tok, local), BF), V((micro, tok, width), BF), V((micro, tok, ff), BF), V((micro, tok, ff), BF),
        V((micro, half, width), F32), V((micro, half, width), F32), V((micro, half, width), BF),
        V((micro, tok, width), BF), V((3, micro, tok, local), BF),
        V((4, micro, half, width), BF), V((4, micro, half, width), BF), V((2, micro, half, width), F32),
        V((4, micro, half, width), BF), V((4, micro, half, width), BF),
        V((4, n_z, own_rows, local), BF), V((4, n_z, own_rows, local), BF), V((4, n_z, own_rows, local), F32),
        V((4, n_z, own_rows, local), BF), V((4, n_z, own_rows, local), BF),
        V((2, n_z, own_rows, ff), BF), V((2, n_z, own_rows, ff), BF), V((2, n_z, own_rows, ff), F32),
        V((2, n_z, own_rows, ff), BF), V((2, n_z, own_rows, ff), BF),
        V((micro, 8, width), F32), V((2, 2, 2, width), F32), V((2, n_dp, 2, width), F32),
        V((n_dp, 8, 128), F32), V((n_tp, 8, 128), F32),
        DMA((4, n_z)), DMA((4, n_z)), DMA((4, n_z)), DMA((4, n_z)), DMA((n_dp,)), DMA((n_dp,)),
        DMA((4, micro)), DMA((4, micro)), DMA((4, micro)), DMA((4, micro)), DMA((4, micro)), DMA((4, micro)),
        DMA((2, micro)),
        DMA((6,)), DMA((6,)), DMA((6, n_z)), DMA((6, n_z)), DMA((2,)), DMA((2,)), DMA((2, n_dp)), DMA((2, n_dp)),
        DMA((n_dp,)), DMA((n_dp,)), DMA((n_tp,)), DMA((n_tp,)),
    ]
    vm = pl.BlockSpec(memory_space=pltpu.VMEM)
    anywhere = pl.BlockSpec(memory_space=pl.ANY)
    S = jax.ShapeDtypeStruct
    return pl.pallas_call(
        partial(layer_kernel, dims),
        out_shape=(
            S((micro, tok, width), BF), S((micro, tok, width), F32),
            S((4, own_rows, local), F32), S((2, own_rows, ff), F32), S((2, 2, width), F32), S((8, 128), F32),
        ),
        in_specs=[vm] * 8,
        out_specs=(anywhere, anywhere, vm, vm, vm, vm),
        scratch_shapes=scratch,
        compiler_params=pltpu.CompilerParams(
            collective_id=0, has_side_effects=True, vmem_limit_bytes=63 << 20
        ),
        name="layer",
    )(
        inputs, cotangent, embeds[:, None, :],
        item_ids[:, :, None], item_ids[:, None, :], a_in, b_in, np_in,
    )


def fast_local(
    n_dp, n_tp,
    inputs, cotangent, item_ids, timestep, qkv_weight, out_weight, up_weight, down_weight, norm_params,
    qkv_first, out_first, up_first, down_first, norm_first,
    qkv_second, out_second, up_second, down_second, norm_second,
):
    embeds = time_embed(timestep[:, 0], inputs.shape[2])
    a_in = jnp.concatenate(
        [jnp.moveaxis(qkv_weight, 1, 0).astype(BF), out_weight.T[None].astype(BF)], axis=0
    )
    b_in = jnp.stack([up_weight.astype(BF), down_weight.T.astype(BF)])
    np_in = jnp.pad(norm_params.astype(BF).astype(F32).T, ((0, 0), (0, 124)))
    block_out, grad_input, ga, gb, gn, gs = layer_call(
        n_dp, n_tp, inputs, cotangent, item_ids, embeds, a_in, b_in, np_in
    )
    grad_norm = gs[0, 0]
    factor = jnp.minimum(1.0, clip_limit / (grad_norm + 1e-06))
    own = norm_params.shape[1]
    gnorm_rows = jnp.concatenate([gn[1], gn[0]], axis=0)
    gnorm_own = lax.dynamic_slice_in_dim(gnorm_rows, lax.axis_index("dp") * own, own, axis=1)
    grads = (jnp.moveaxis(ga[:3], 0, 1), ga[3].T, gb[0], gb[1].T, gnorm_own)
    weights = (qkv_weight, out_weight, up_weight, down_weight, norm_params)
    firsts = (qkv_first, out_first, up_first, down_first, norm_first)
    seconds = (qkv_second, out_second, up_second, down_second, norm_second)
    result = [
        adam_step(weights[index], grads[index] * factor, firsts[index], seconds[index]) for index in range(5)
    ]
    flat = [item for triple in result for item in triple]
    return (block_out, grad_input, grad_norm, *flat)


def layer_norm(values, gain_row, bias_row):
    centre = values - jnp.mean(values, axis=-1, keepdims=True)
    spread = jnp.mean(centre * centre, axis=-1, keepdims=True)
    return centre * lax.rsqrt(spread + norm_eps) * gain_row + bias_row


def masked_scores(query_rows, key_rows, same_item, score_scale):
    scores = (
        jnp.einsum("thd,shd->hts", query_rows, key_rows, preferred_element_type=jnp.float32)
        * score_scale
    )
    return jnp.where(same_item, scores, -1e30)


def one_micro(gathered, stream_in, upstream, labels, embed_row):
    qkv_mat, out_mat, up_mat, down_mat, norm_rows = gathered
    tokens_here = stream_in.shape[0]
    local_width = out_mat.shape[0]
    heads_here = local_width // HEAD_DIM
    score_scale = 1.0 / math.sqrt(HEAD_DIM)
    split_shape = (tokens_here, heads_here, HEAD_DIM)
    norm_gains = norm_rows.astype(jnp.float32)
    gain_one = 1.0 + norm_gains[0]
    gain_two = 1.0 + norm_gains[2]
    stream = stream_in.astype(jnp.float32) + embed_row[None, :]
    normed_f, norm_one_back = jax.vjp(layer_norm, stream, gain_one, norm_gains[1])
    normed = normed_f.astype(jnp.bfloat16)
    triple = jnp.einsum("td,dje->jte", normed, qkv_mat, preferred_element_type=jnp.float32).astype(
        jnp.bfloat16
    )
    query_rows = triple[0].reshape(split_shape)
    key_rows = triple[1].reshape(split_shape)
    value_rows = triple[2].reshape(split_shape)
    same_item = (labels[:, None] == labels[None, :])[None]
    scores = masked_scores(query_rows, key_rows, same_item, score_scale)
    row_top = jnp.max(scores, axis=-1, keepdims=True)
    exp_scores = jnp.exp(scores - row_top)
    row_total = jnp.sum(exp_scores, axis=-1, keepdims=True)
    probs_soft = exp_scores / row_total
    log_total = row_top + jnp.log(row_total)
    context = (
        jnp.einsum(
            "hts,shd->thd",
            probs_soft.astype(jnp.bfloat16),
            value_rows,
            preferred_element_type=jnp.float32,
        )
        .reshape(tokens_here, local_width)
        .astype(jnp.bfloat16)
    )
    attn_out = lax.psum(jnp.dot(context, out_mat, preferred_element_type=jnp.float32), "tp")
    middle = stream + attn_out
    normed_two_f, norm_two_back = jax.vjp(layer_norm, middle, gain_two, norm_gains[3])
    normed_two = normed_two_f.astype(jnp.bfloat16)
    hidden_pre = jnp.dot(normed_two, up_mat, preferred_element_type=jnp.float32)
    hidden_f, gelu_back = jax.vjp(partial(jax.nn.gelu, approximate=False), hidden_pre)
    hidden = hidden_f.astype(jnp.bfloat16)
    branch = lax.psum(
        jnp.dot(hidden, down_mat, preferred_element_type=jnp.float32).astype(jnp.bfloat16), "tp"
    ).astype(jnp.float32)
    block_out = (middle + branch).astype(jnp.bfloat16)
    grad_down = jnp.einsum("tf,td->fd", hidden, upstream, preferred_element_type=jnp.float32)
    grad_hidden = jnp.einsum("td,fd->tf", upstream, down_mat, preferred_element_type=jnp.float32)
    grad_pre = gelu_back(grad_hidden)[0].astype(jnp.bfloat16)
    grad_up = jnp.einsum("td,tf->df", normed_two, grad_pre, preferred_element_type=jnp.float32)
    grad_normed_two = lax.psum(
        jnp.einsum("tf,df->td", grad_pre, up_mat, preferred_element_type=jnp.float32), "tp"
    )
    grad_middle_norm, grad_gain_two, grad_bias_two = norm_two_back(grad_normed_two)
    grad_middle = upstream.astype(jnp.float32) + grad_middle_norm
    grad_attn = grad_middle.astype(jnp.bfloat16)
    grad_outmat = jnp.einsum("tc,td->cd", context, grad_attn, preferred_element_type=jnp.float32)
    grad_context = (
        jnp.einsum("td,cd->tc", grad_attn, out_mat, preferred_element_type=jnp.float32)
        .astype(jnp.bfloat16)
        .reshape(split_shape)
    )
    probs_again = jnp.exp(masked_scores(query_rows, key_rows, same_item, score_scale) - log_total)
    grad_values = jnp.einsum(
        "hts,thd->shd",
        probs_again.astype(jnp.bfloat16),
        grad_context,
        preferred_element_type=jnp.float32,
    )
    grad_probs = jnp.einsum(
        "thd,shd->hts", grad_context, value_rows, preferred_element_type=jnp.float32
    )
    inner_sum = jnp.sum(grad_probs * probs_again, axis=-1, keepdims=True)
    grad_scores = (probs_again * (grad_probs - inner_sum)).astype(jnp.bfloat16)
    grad_query = (
        jnp.einsum("hts,shd->thd", grad_scores, key_rows, preferred_element_type=jnp.float32)
        * score_scale
    )
    grad_key = (
        jnp.einsum("hts,thd->shd", grad_scores, query_rows, preferred_element_type=jnp.float32)
        * score_scale
    )
    grad_triple = (
        jnp.stack([grad_query, grad_key, grad_values])
        .reshape(3, tokens_here, local_width)
        .astype(jnp.bfloat16)
    )
    grad_qkv = jnp.einsum("td,jte->dje", normed, grad_triple, preferred_element_type=jnp.float32)
    grad_normed = lax.psum(
        jnp.einsum("jte,dje->td", grad_triple, qkv_mat, preferred_element_type=jnp.float32).astype(
            jnp.bfloat16
        ),
        "tp",
    ).astype(jnp.float32)
    grad_stream_norm, grad_gain_one, grad_bias_one = norm_one_back(grad_normed)
    grad_input = grad_middle + grad_stream_norm
    grad_norms = jnp.stack([grad_gain_one, grad_bias_one, grad_gain_two, grad_bias_two])
    return (block_out, grad_input, (grad_qkv, grad_outmat, grad_up, grad_down, grad_norms))


def local(
    inputs,
    cotangent,
    item_ids,
    timestep,
    qkv_weight,
    out_weight,
    up_weight,
    down_weight,
    norm_params,
    qkv_first,
    out_first,
    up_first,
    down_first,
    norm_first,
    qkv_second,
    out_second,
    up_second,
    down_second,
    norm_second,
):
    micro_count = inputs.shape[0]
    embeds = time_embed(timestep[:, 0], inputs.shape[2])
    qkv_low = qkv_weight.astype(jnp.bfloat16)
    out_low = out_weight.astype(jnp.bfloat16)
    up_low = up_weight.astype(jnp.bfloat16)
    down_low = down_weight.astype(jnp.bfloat16)
    norm_low = norm_params.astype(jnp.bfloat16)
    block_list = []
    input_list = []
    for number in range(micro_count):
        gathered = (
            lax.all_gather(qkv_low, "dp", axis=0, tiled=True),
            lax.all_gather(out_low, "dp", axis=1, tiled=True),
            lax.all_gather(up_low, "dp", axis=0, tiled=True),
            lax.all_gather(down_low, "dp", axis=1, tiled=True),
            lax.all_gather(norm_low, "dp", axis=1, tiled=True),
        )
        block_out, grad_input, grad_list = one_micro(
            gathered, inputs[number], cotangent[number], item_ids[number], embeds[number]
        )
        owned_grads = (
            lax.psum_scatter(grad_list[0], "dp", scatter_dimension=0, tiled=True),
            lax.psum_scatter(grad_list[1], "dp", scatter_dimension=1, tiled=True),
            lax.psum_scatter(grad_list[2], "dp", scatter_dimension=0, tiled=True),
            lax.psum_scatter(grad_list[3], "dp", scatter_dimension=1, tiled=True),
            lax.psum_scatter(grad_list[4], "dp", scatter_dimension=1, tiled=True),
        )
        if number == 0:
            totals = tuple(owned_grads)
        else:
            totals = tuple((left + right for left, right in zip(totals, owned_grads)))
        block_list.append(block_out)
        input_list.append(grad_input)
    own_squares = jnp.sum(totals[0] * totals[0]) + jnp.sum(totals[1] * totals[1])
    own_squares = own_squares + jnp.sum(totals[2] * totals[2]) + jnp.sum(totals[3] * totals[3])
    norm_squares = jnp.sum(totals[4] * totals[4])
    own_squares = own_squares + jnp.where(
        lax.axis_index("tp") == 0, norm_squares, jnp.zeros_like(norm_squares)
    )
    grad_norm = jnp.sqrt(lax.psum(own_squares, ("dp", "tp")))
    factor = jnp.minimum(1.0, clip_limit / (grad_norm + 1e-06))
    weights = (qkv_weight, out_weight, up_weight, down_weight, norm_params)
    firsts = (qkv_first, out_first, up_first, down_first, norm_first)
    seconds = (qkv_second, out_second, up_second, down_second, norm_second)
    result = [
        adam_step(weights[index], totals[index] * factor, firsts[index], seconds[index])
        for index in range(5)
    ]
    return (
        jnp.stack(block_list),
        jnp.stack(input_list),
        grad_norm,
        result[0][0],
        result[0][1],
        result[0][2],
        result[1][0],
        result[1][1],
        result[1][2],
        result[2][0],
        result[2][1],
        result[2][2],
        result[3][0],
        result[3][1],
        result[3][2],
        result[4][0],
        result[4][1],
        result[4][2],
    )


def solution(mesh):
    n_dp, n_tp = mesh.shape["dp"], mesh.shape["tp"]

    def step(*args):
        own_rows = args[4].shape[0]
        fits = n_tp == 4 and n_dp % 2 == 0 and own_rows % 16 == 0 and args[0].shape[0] == 2
        if fits and args[0].shape[1] % 256 == 0 and args[4].shape[2] % HEAD_DIM == 0:
            return fast_local(n_dp, n_tp, *args)
        return local(*args)

    return jax.shard_map(
        step,
        mesh=mesh,
        in_specs=(
            P(None, "dp", None),
            P(None, "dp", None),
            P(None, "dp"),
            P(None, "dp"),
            P("dp", None, "tp"),
            P("tp", "dp"),
            P("dp", "tp"),
            P("tp", "dp"),
            P(None, "dp"),
            P("dp", None, "tp"),
            P("tp", "dp"),
            P("dp", "tp"),
            P("tp", "dp"),
            P(None, "dp"),
            P("dp", None, "tp"),
            P("tp", "dp"),
            P("dp", "tp"),
            P("tp", "dp"),
            P(None, "dp"),
        ),
        out_specs=(
            P(None, "dp", None),
            P(None, "dp", None),
            P(),
            P("dp", None, "tp"),
            P("dp", None, "tp"),
            P("dp", None, "tp"),
            P("tp", "dp"),
            P("tp", "dp"),
            P("tp", "dp"),
            P("dp", "tp"),
            P("dp", "tp"),
            P("dp", "tp"),
            P("tp", "dp"),
            P("tp", "dp"),
            P("tp", "dp"),
            P(None, "dp"),
            P(None, "dp"),
            P(None, "dp"),
        ),
        check_vma=False,
    )
```

```python
from functools import partial
import math

import jax
import jax.numpy as jnp
from jax import lax
from jax.experimental import pallas as pl
from jax.experimental.pallas import tpu as pltpu
from jax.sharding import PartitionSpec as P

HEAD_DIM = 64
STEP = 10

norm_eps = 1e-05
clip_limit = 1.0
learn_rate = 0.02
beta_one = 0.9
beta_two = 0.999
adam_eps = 1e-08
weight_decay = 0.01

BF = jnp.bfloat16
F32 = jnp.float32
MESH = pl.DeviceIdType.MESH


def time_embed(step_values, model_width):
    half_width = model_width // 2
    frequency = jnp.exp(
        jnp.arange(half_width, dtype=jnp.float32) * (-math.log(10000.0) / half_width)
    )
    angles = step_values.astype(jnp.float32)[..., None] * frequency
    return jnp.concatenate([jnp.sin(angles), jnp.cos(angles)], axis=-1)


def adam_step(weight, gradient, first_old, second_old):
    first_new = beta_one * first_old + (1.0 - beta_one) * gradient
    second_new = beta_two * second_old + (1.0 - beta_two) * gradient * gradient
    moment_one = first_new / (1.0 - beta_one**STEP)
    moment_two = second_new / (1.0 - beta_two**STEP)
    weight_new = weight - learn_rate * (
        moment_one / (jnp.sqrt(moment_two) + adam_eps) + weight_decay * weight
    )
    return (weight_new, first_new, second_new)


def mm(a, b, ca, cb):
    return lax.dot_general(a, b, (((ca,), (cb,)), ((), ())), preferred_element_type=F32)


def fold(v):
    cut = v.shape[-2] // 2
    low = jnp.concatenate([v[..., :cut, 128:], v[..., cut:, 128:]], axis=-1)
    return jnp.concatenate([v[..., :128], low], axis=-2)


def unfold(p):
    rows = 2 * p.shape[-2] // 3
    low = p[..., rows:, :]
    right = jnp.concatenate([low[..., :64], low[..., 64:]], axis=-2)
    return jnp.concatenate([p[..., :rows, :], right], axis=-1)


def layer_kernel(
    dims,
    x_ref, cot_ref, emb_ref, lc_ref, lr_ref, ain_ref, bin_ref, npin_ref,
    bo_ref, ig_ref, ga_ref, go_ref, gb_ref, gn_ref, gs_ref,
    wag, wqkv, woall, wo4, wb, npg, npt,
    normed, qkv, probs, ctx, ctxp, ctxr, n2, hid, dpre, mid, dmid, bo_own, dattn, dqkv,
    csend, crecv, own, ysend, yrecv,
    gfo, gfb, rax_s, rax_r, raz_s, raz_r, rbx_s, rbx_r, rbz_s, rbz_r,
    nacc, ncore, nsum, sqd, sqt,
    az_s, az_r, ax_s, ax_r, np_s, np_r, oy_s, oy_r, oc_s, oc_r, cx_s, cx_r,
    c_s, c_r, y_s, y_r, g_s, g_r, o_l,
    rx_s, rx_r, rz_s, rz_r, nc_s, nc_r, nd_s, nd_r, qd_s, qd_r, qt_s, qt_r,
):
    micro, tok, width, n_dp, n_tp, heads = dims
    n_z = n_dp // 2
    half = tok // 2
    own_rows = width // n_dp
    fold_rows = 3 * own_rows // 2
    local = heads * HEAD_DIM
    scale = 1.0 / math.sqrt(HEAD_DIM)

    dp = lax.axis_index("dp")
    tp = lax.axis_index("tp")
    z, xx = lax.div(dp, 2), lax.rem(dp, 2)
    yy, cc = lax.div(tp, 2), lax.rem(tp, 2)
    across_tp = 2 * (1 - yy) + cc
    x_peer = (2 * z + 1 - xx, tp)
    c_peer = (dp, 2 * yy + 1 - cc)
    y_peer = (dp, across_tp)
    d_peer = (dp, 2 * (1 - yy) + 1 - cc)

    far = lax.div(z, 2)
    column = (z + 1 - 2 * lax.rem(z, 2), 2 - far, 3 - 3 * far)
    flip = 1 - xx

    def dp_of(k):
        return lax.rem(dp + k, n_dp)

    def tp_of(k):
        return lax.rem(tp + k, n_tp)

    sent = []

    def copy(src, dst, s_sem, r_sem, peer):
        return pltpu.make_async_remote_copy(
            src_ref=src, dst_ref=dst, send_sem=s_sem, recv_sem=r_sem, device_id=peer, device_id_type=MESH
        )

    def send(src, dst, s_sem, r_sem, peer):
        item = copy(src, dst, s_sem, r_sem, peer)
        item.start()
        sent.append(item)

    def arrive(dst, s_sem, r_sem, peer):
        copy(dst, dst, s_sem, r_sem, peer).wait_recv()

    barrier = pltpu.get_barrier_semaphore()
    for k in range(1, n_dp):
        pl.semaphore_signal(barrier, inc=1, device_id=(dp_of(k), tp), device_id_type=MESH)
    for k in range(1, n_tp):
        pl.semaphore_signal(barrier, inc=1, device_id=(dp, tp_of(k)), device_id_type=MESH)
    pl.semaphore_wait(barrier, n_dp + n_tp - 2)

    def rows_of(j):
        return pl.ds(pl.multiple_of(j * own_rows, own_rows), own_rows)

    def half_rows(h):
        return pl.ds(pl.multiple_of(h * half, half), half)

    mine = half_rows(cc)
    other = half_rows(1 - cc)

    def ag_src(g):
        if g < 2:
            return ain_ref.at[:, pl.ds(384 * g, 384 - 256 * g)]
        return bin_ref.at[g - 2]

    def ag_at(g, j):
        if g < 2:
            return wag.at[j, :, pl.ds(384 * g, 384 - 256 * g)]
        return wb.at[g - 2, j]

    def ag_column(g):
        for i in range(3):
            send(ag_src(g), ag_at(g, dp), az_s.at[g, i], az_r.at[g, z], (2 * column[i] + xx, tp))
        ag_at(g, dp)[...] = ag_src(g)[...]

    def ag_side(g):
        send(ag_src(g), ag_at(g, dp), ax_s.at[g, 3], ax_r.at[g, z], x_peer)

    def ag_pass(g, *which):
        for i in which:
            s = column[i]
            block = ag_at(g, 2 * s + xx)
            arrive(block, az_s.at[g, i], az_r.at[g, s], (2 * s + xx, tp))
            send(block, block, ax_s.at[g, i], ax_r.at[g, s], x_peer)

    def ag_done(g):
        for i, s in enumerate((*column, z)):
            arrive(ag_at(g, 2 * s + flip), ax_s.at[g, i], ax_r.at[g, s], x_peer)

    def o_send(col, which):
        for i in which:
            j = 2 * (*column, z)[i] + col
            part = ag_at(1, j)
            send(part, woall.at[tp, j], oy_s.at[j], oy_r.at[j], y_peer)

    def o_core():
        woall[tp] = wag[:, :, 384:512]
        send(woall.at[tp], woall.at[tp], oc_s.at[0], oc_r.at[0], c_peer)

    def o_across():
        for j in range(n_dp):
            arrive(woall.at[across_tp, j], oy_s.at[j], oy_r.at[j], y_peer)
        send(woall.at[across_tp], woall.at[across_tp], oc_s.at[1], oc_r.at[1], c_peer)

    def o_done():
        arrive(woall.at[2 * yy + 1 - cc], oc_s.at[0], oc_r.at[0], c_peer)
        arrive(woall.at[2 * (1 - yy) + 1 - cc], oc_s.at[1], oc_r.at[1], c_peer)
        for t in range(n_tp):
            wo4[t] = unfold(woall[t]).reshape(width, local)

    def ar_start(kind, m, part):
        csend[kind, m] = part(other).astype(BF)
        send(csend.at[kind, m], crecv.at[kind, m], c_s.at[kind, m], c_r.at[kind, m], c_peer)
        own[kind % 2, m] = part(mine)

    def ar_cross(kind, m):
        arrive(crecv.at[kind, m], c_s.at[kind, m], c_r.at[kind, m], c_peer)
        ysend[kind, m] = (own[kind % 2, m] + crecv[kind, m].astype(F32)).astype(BF)
        send(ysend.at[kind, m], yrecv.at[kind, m], y_s.at[kind, m], y_r.at[kind, m], y_peer)

    def ar_total(kind, m):
        arrive(yrecv.at[kind, m], y_s.at[kind, m], y_r.at[kind, m], y_peer)
        return ysend[kind, m].astype(F32) + yrecv[kind, m].astype(F32)

    def share(i, m, ref):
        send(ref.at[m, mine], ref.at[m, mine], g_s.at[i, m], g_r.at[i, m], c_peer)

    def shared(i, m, ref):
        arrive(ref.at[m, other], g_s.at[i, m], g_r.at[i, m], c_peer)

    def centred(v):
        c0 = v - jnp.mean(v, axis=-1, keepdims=True)
        return c0, lax.rsqrt(jnp.mean(c0 * c0, axis=-1, keepdims=True) + norm_eps)

    def norm_back(grad, hat, inv, gain):
        dhat = grad * gain
        return inv * (
            dhat
            - jnp.mean(dhat, axis=-1, keepdims=True)
            - hat * jnp.mean(dhat * hat, axis=-1, keepdims=True)
        )

    def open_norms():
        block = lax.broadcasted_iota(jnp.int32, (n_dp, 128, width), 0)
        row = lax.broadcasted_iota(jnp.int32, (n_dp, 128, width), 1)
        col = lax.broadcasted_iota(jnp.int32, (n_dp, 128, width), 2)
        place = ((col == block * own_rows + row) & (row < own_rows)).astype(F32).astype(BF)
        rows = npg[0]
        total = mm(rows, place[0], 1, 0)
        for j in range(1, n_dp):
            total = total + mm(npg[j], place[j], 1, 0)
        npt[...] = total

    def gain_row(i):
        return 1.0 + npt[pl.ds(i, 1), :]

    def bias_row(i):
        return npt[pl.ds(i, 1), :]

    def stream_of(m, rows):
        return x_ref[m, rows, :].astype(F32) + emb_ref[m]

    def first_norm(m):
        c0, inv = centred(stream_of(m, pl.ds(0, tok)))
        normed[m] = (c0 * inv * gain_row(0) + bias_row(1)).astype(BF)

    def open_qkv():
        for i in range(3):
            wqkv[i] = unfold(wag[:, :, 128 * i : 128 * (i + 1)]).reshape(width, local)

    def project(m):
        for i in range(3):
            qkv[i, m] = mm(normed[m], wqkv[i], 1, 0).astype(BF)

    lane = lax.broadcasted_iota(jnp.int32, (1, local), 1)

    def head_mask(h, value):
        here = (lane >= h * HEAD_DIM) & (lane < (h + 1) * HEAD_DIM)
        return jnp.where(here, value, 0.0).astype(BF)

    def attend(m, *between):
        same = lc_ref[m] == lr_ref[m]
        total = None
        for h in range(heads):
            s = mm(qkv[0, m] * head_mask(h, scale), qkv[1, m], 1, 1)
            s = jnp.where(same, s, -1e30)
            e = jnp.exp(s - jnp.max(s, axis=-1, keepdims=True))
            p = e * (1.0 / jnp.sum(e, axis=-1, keepdims=True))
            probs[m * heads + h] = p
            part = mm(p.astype(BF), qkv[2, m] * head_mask(h, 1.0), 1, 0)
            total = part if total is None else total + part
            for work in between[h] if h < len(between) else ():
                work()
        ctx[m] = total.astype(BF)
        for i in range(2):
            ctxp[m, i] = fold(total[i * half : (i + 1) * half]).astype(BF)
        send(ctxp.at[m, cc], ctxr.at[m, tp], cx_s.at[m, 1], cx_r.at[m, 1], y_peer)
        send(ctxp.at[m, 1 - cc], ctxr.at[m, tp], cx_s.at[m, 2], cx_r.at[m, 2], d_peer)
        send(ctxp.at[m, 1 - cc], ctxr.at[m, tp], cx_s.at[m, 0], cx_r.at[m, 0], c_peer)
        ctxr[m, tp] = ctxp[m, cc]

    def second_norm(m):
        arrive(ctxr.at[m, 2 * yy + 1 - cc], cx_s.at[m, 0], cx_r.at[m, 0], c_peer)
        arrive(ctxr.at[m, across_tp], cx_s.at[m, 1], cx_r.at[m, 1], y_peer)
        arrive(ctxr.at[m, 2 * (1 - yy) + 1 - cc], cx_s.at[m, 2], cx_r.at[m, 2], d_peer)
        middle = stream_of(m, mine)
        for t in range(n_tp):
            middle = middle + mm(unfold(ctxr[m, t]), wo4[t], 1, 1)
        mid[m] = middle
        c0, inv = centred(middle)
        n2[m, mine, :] = (c0 * inv * gain_row(2) + bias_row(3)).astype(BF)
        share(0, m, n2)

    def wide(g):
        return wb[g].reshape(width, wb.shape[-1])

    def feed(m):
        shared(0, m, n2)
        pre = mm(n2[m], wide(0), 1, 0)
        cdf = 0.5 * (1.0 + lax.erf(pre * math.sqrt(0.5)))
        hid[m] = (pre * cdf).astype(BF)
        slope = cdf + pre * (jnp.exp(-0.5 * pre * pre) * (1.0 / math.sqrt(2.0 * math.pi)))
        dpre[m] = (mm(cot_ref[m], wide(1), 1, 0) * slope).astype(BF)

    def dn2_part(m):
        return lambda rows: mm(dpre[m, rows, :], wide(0), 1, 1)

    def branch_part(m):
        return lambda rows: mm(hid[m, rows, :], wide(1), 1, 1)

    def col_sum(v):
        return jnp.sum(v, axis=0, keepdims=True)

    def second_back(m):
        grad = ar_total(0, m)
        c0, inv = centred(mid[m])
        hat = c0 * inv
        nacc[m, pl.ds(0, 1), :] = col_sum(grad * hat)
        nacc[m, pl.ds(1, 1), :] = col_sum(grad)
        grad_middle = cot_ref[m, mine, :].astype(F32) + norm_back(grad, hat, inv, gain_row(2))
        dmid[m] = grad_middle
        dattn[m, mine, :] = grad_middle.astype(BF)
        share(1, m, dattn)

    def finish_block(m):
        bo_own[m] = (mid[m] + ar_total(1, m)).astype(BF)
        send(bo_own.at[m], bo_ref.at[m, mine], g_s.at[2, m], g_r.at[2, m], c_peer)
        pltpu.make_async_copy(bo_own.at[m], bo_ref.at[m, mine], o_l.at[0, m]).start()

    def attend_back(m, *between):
        shared(1, m, dattn)
        wo_own = wo4[tp]
        dctx = mm(dattn[m], wo_own, 1, 0).astype(BF)
        dq = dk = dv = None
        for h in range(heads):
            dch = dctx * head_mask(h, 1.0)
            p = probs[m * heads + h]
            dp_ = mm(dch, qkv[2, m], 1, 1)
            inner = jnp.sum(dp_ * p, axis=-1, keepdims=True)
            ds = (p * (dp_ - inner)).astype(BF)
            mask = head_mask(h, scale)
            a = mm(ds, qkv[1, m] * mask, 1, 0)
            b = mm(ds, qkv[0, m] * mask, 0, 0)
            c = mm(p.astype(BF), dch, 0, 0)
            dq = a if dq is None else dq + a
            dk = b if dk is None else dk + b
            dv = c if dv is None else dv + c
            for work in between[h] if h < len(between) else ():
                work()
        dqkv[0, m] = dq.astype(BF)
        dqkv[1, m] = dk.astype(BF)
        dqkv[2, m] = dv.astype(BF)

    def dn1_part(m):
        def part(rows):
            total = mm(dqkv[0, m, rows, :], wqkv[0], 1, 1)
            for i in range(1, 3):
                total = total + mm(dqkv[i, m, rows, :], wqkv[i], 1, 1)
            return total

        return part

    def first_back(m):
        grad = ar_total(2, m)
        c0, inv = centred(stream_of(m, mine))
        hat = c0 * inv
        nacc[m, pl.ds(2, 1), :] = col_sum(grad * hat)
        nacc[m, pl.ds(3, 1), :] = col_sum(grad)
        dmid[m] = dmid[m] + norm_back(grad, hat, inv, gain_row(0))
        send(dmid.at[m], ig_ref.at[m, mine], g_s.at[3, m], g_r.at[3, m], c_peer)
        pltpu.make_async_copy(dmid.at[m], ig_ref.at[m, mine], o_l.at[1, m]).start()

    def gf(g, at, col):
        if g == 0:
            rows = pl.ds(pl.multiple_of(col * fold_rows, fold_rows), fold_rows)
            return probs.at[at, rows, pl.ds(0, 384)]
        return gfo.at[2 * at + col] if g == 1 else gfb.at[g - 2, 2 * at + col]

    def rs_slots(g, at):
        if g < 2:
            lanes = pl.ds(384 * g, 384 - 256 * g)
            return [r.at[at, :, lanes] for r in (rax_s, rax_r, raz_s, raz_r)]
        return [r.at[g - 2, at] for r in (rbx_s, rbx_r, rbz_s, rbz_r)]

    def flat(ref):
        return ref[...].reshape(micro * tok, ref.shape[-1])

    def rs_wide(g, left, right):
        gfb[g - 2] = mm(flat(left), flat(right), 0, 0).reshape(n_dp, own_rows, right.shape[-1])

    def rs_narrow(i, left, right):
        grad = fold(mm(flat(left), flat(right), 0, 0).reshape(n_dp, own_rows, local))
        if i == 3:
            gfo[...] = grad
            return
        for j in range(n_dp):
            rows = pl.ds((j % 2) * fold_rows, fold_rows)
            probs[j // 2, rows, 128 * i : 128 * (i + 1)] = grad[j]

    def rs_start(g):
        for i in (2, 1, 0, 3):
            at = (*column, z)[i]
            here, there, _, _ = rs_slots(g, at)
            here[...] = gf(g, at, flip)[...].astype(BF)
            send(here, there, rx_s.at[g, i], rx_r.at[g, at], x_peer)

    def rs_sum(g, i):
        at = (*column, z)[i]
        there = rs_slots(g, at)[1]
        arrive(there, rx_s.at[g, i], rx_r.at[g, at], x_peer)
        return gf(g, at, xx)[...] + there[...].astype(F32)

    def rs_pass(g, *which):
        for i in which:
            at = column[i]
            here = rs_slots(g, at)[2]
            here[...] = rs_sum(g, i).astype(BF)
            send(here, rs_slots(g, z)[3], rz_s.at[g, i], rz_r.at[g, z], (2 * at + xx, tp))

    def rs_finish(g):
        total = rs_sum(g, 3)
        for i in range(3):
            s = column[i]
            there = rs_slots(g, s)[3]
            arrive(there, rz_s.at[g, i], rz_r.at[g, s], (2 * s + xx, tp))
            total = total + there[...].astype(F32)
        if g == 0:
            for i in range(3):
                ga_ref[i] = unfold(total[:, 128 * i : 128 * (i + 1)])
        elif g == 1:
            go_ref[...] = unfold(total).T
        else:
            gb_ref[g - 2] = total
        return jnp.sum(col_sum(total * total), axis=1, keepdims=True)

    def norm_start(e):
        both = nacc[0, pl.ds(2 * e, 2), :]
        for m in range(1, micro):
            both = both + nacc[m, pl.ds(2 * e, 2), :]
        ncore[e, 0] = both
        send(ncore.at[e, 0], ncore.at[e, 1], nc_s.at[e], nc_r.at[e], c_peer)

    def norm_cross(e):
        arrive(ncore.at[e, 1], nc_s.at[e], nc_r.at[e], c_peer)
        nsum[e, dp] = ncore[e, 0] + ncore[e, 1]
        for k in range(1, n_dp):
            send(nsum.at[e, dp], nsum.at[e, dp], nd_s.at[e, k], nd_r.at[e, k], (dp_of(k), tp))

    def norm_finish(e):
        for k in range(1, n_dp):
            j = lax.rem(dp + n_dp - k, n_dp)
            arrive(nsum.at[e, j], nd_s.at[e, k], nd_r.at[e, k], (dp_of(k), tp))
        total = nsum[e, 0]
        for j in range(1, n_dp):
            total = total + nsum[e, j]
        gn_ref[e] = total
        return jnp.sum(col_sum(total * total), axis=1, keepdims=True)

    ag_side(0)
    ag_column(0)
    npg[dp] = npin_ref[...]
    for k in range(1, n_dp):
        send(npin_ref, npg.at[dp], np_s.at[k], np_r.at[k], (dp_of(k), tp))
    ag_column(1)
    o_send(xx, (3,))
    for k in range(1, n_dp):
        arrive(npg.at[lax.rem(dp + n_dp - k, n_dp)], np_s.at[k], np_r.at[k], (dp_of(k), tp))
    open_norms()
    first_norm(0)
    ag_pass(0, 0)
    first_norm(1)
    ag_pass(0, 1, 2)
    ag_side(1)
    ag_column(2)
    ag_pass(1, 0, 1, 2)
    o_send(xx, (0, 1, 2))
    ag_done(0)
    open_qkv()
    project(0)
    ag_side(2)

    def o_rest():
        ag_done(1)
        o_send(flip, (0, 1, 2, 3))
        o_core()

    attend(0, (o_rest,), (partial(ag_pass, 2, 0),), (partial(ag_pass, 2, 1), partial(ag_column, 3)))
    project(1)
    ag_pass(2, 2)
    ag_side(3)
    attend(1, (o_across,), (partial(ag_pass, 3, 0),), (partial(ag_pass, 3, 1),))
    o_done()
    second_norm(0)
    ag_done(2)
    ag_pass(3, 2)
    second_norm(1)
    ag_done(3)
    feed(0)
    ar_start(0, 0, dn2_part(0))
    feed(1)
    ar_cross(0, 0)
    ar_start(0, 1, dn2_part(1))
    rs_wide(3, cot_ref, hid)
    ar_cross(0, 1)
    rs_start(3)
    rs_wide(2, n2, dpre)
    ar_start(1, 0, branch_part(0))
    ar_start(1, 1, branch_part(1))
    second_back(0)
    rs_pass(3, 2, 1)
    attend_back(0, (partial(rs_pass, 3, 0),), (partial(rs_start, 2),))
    ar_start(2, 0, dn1_part(0))
    rs_pass(2, 2)
    ar_cross(2, 0)
    second_back(1)
    rs_pass(2, 1)
    norm_start(0)
    attend_back(
        1,
        (partial(rs_pass, 2, 0), partial(rs_narrow, 3, dattn, ctx), partial(rs_start, 1)),
        (partial(norm_cross, 0),),
    )
    ar_start(2, 1, dn1_part(1))
    rs_pass(1, 2, 1, 0)
    for i in range(3):
        rs_narrow(i, normed, dqkv.at[i])
    ar_cross(2, 1)
    rs_start(0)
    ar_cross(1, 0)
    ar_cross(1, 1)
    first_back(0)
    rs_pass(0, 2, 1)
    squares = rs_finish(3) + rs_finish(2)
    squares = squares + rs_finish(1)
    rs_pass(0, 0)
    first_back(1)
    norm_start(1)
    norm_cross(1)
    squares = squares + rs_finish(0)
    sqd[dp] = jnp.broadcast_to(squares, (8, 128))
    for k in range(1, n_dp):
        send(sqd.at[dp], sqd.at[dp], qd_s.at[k], qd_r.at[k], (dp_of(k), tp))
    extra = norm_finish(0) + norm_finish(1)
    for k in range(1, n_dp):
        j = lax.rem(dp + n_dp - k, n_dp)
        arrive(sqd.at[j], qd_s.at[k], qd_r.at[k], (dp_of(k), tp))
    mesh_row = sqd[0]
    for j in range(1, n_dp):
        mesh_row = mesh_row + sqd[j]
    sqt[tp] = mesh_row
    for k in range(1, n_tp):
        send(sqt.at[tp], sqt.at[tp], qt_s.at[k], qt_r.at[k], (dp, tp_of(k)))
    for k in range(1, n_tp):
        j = lax.rem(tp + n_tp - k, n_tp)
        arrive(sqt.at[j], qt_s.at[k], qt_r.at[k], (dp, tp_of(k)))
    everything = sqt[0]
    for j in range(1, n_tp):
        everything = everything + sqt[j]
    gs_ref[...] = jnp.sqrt(everything + extra)
    finish_block(0)
    finish_block(1)
    for m in range(micro):
        arrive(bo_ref.at[m, other], g_s.at[2, m], g_r.at[2, m], c_peer)
        arrive(ig_ref.at[m, other], g_s.at[3, m], g_r.at[3, m], c_peer)
        pltpu.make_async_copy(bo_own.at[m], bo_ref.at[m, mine], o_l.at[0, m]).wait()
        pltpu.make_async_copy(dmid.at[m], ig_ref.at[m, mine], o_l.at[1, m]).wait()
    for item in sent:
        item.wait_send()


def layer_call(n_dp, n_tp, inputs, cotangent, item_ids, embeds, a_in, b_in, np_in):
    micro, tok, width = inputs.shape
    _, own_rows, ff = b_in.shape
    fold_rows = a_in.shape[0]
    heads = 2 * a_in.shape[0] * a_in.shape[1] // (8 * own_rows * HEAD_DIM)
    local = heads * HEAD_DIM
    half = tok // 2
    fold_half = 3 * half // 2
    dims = (micro, tok, width, n_dp, n_tp, heads)
    V = pltpu.VMEM
    DMA = pltpu.SemaphoreType.DMA
    n_z = n_dp // 2
    room = max(micro * heads, n_z)
    scratch = [
        V((n_dp, fold_rows, 512), BF), V((3, width, local), BF), V((n_tp, n_dp, fold_rows, 128), BF),
        V((n_tp, width, local), BF), V((2, n_dp, own_rows, ff), BF), V((n_dp, 8, 128), BF), V((8, width), F32),
        V((micro, tok, width), BF), V((3, micro, tok, local), BF), V((room, tok, tok), F32),
        V((micro, tok, local), BF), V((micro, 2, fold_half, 128), BF), V((micro, n_tp, fold_half, 128), BF),
        V((micro, tok, width), BF), V((micro, tok, ff), BF), V((micro, tok, ff), BF),
        V((micro, half, width), F32), V((micro, half, width), F32), V((micro, half, width), BF),
        V((micro, tok, width), BF), V((3, micro, tok, local), BF),
        V((3, micro, half, width), BF), V((3, micro, half, width), BF), V((2, micro, half, width), F32),
        V((3, micro, half, width), BF), V((3, micro, half, width), BF),
        V((n_dp, fold_rows, 128), F32), V((2, n_dp, own_rows, ff), F32),
        V((n_z, fold_rows, 512), BF), V((n_z, fold_rows, 512), BF), V((n_z, fold_rows, 512), BF), V((n_z, fold_rows, 512), BF),
        V((2, n_z, own_rows, ff), BF), V((2, n_z, own_rows, ff), BF), V((2, n_z, own_rows, ff), BF), V((2, n_z, own_rows, ff), BF),
        V((micro, 8, width), F32), V((2, 2, 2, width), F32), V((2, n_dp, 2, width), F32),
        V((n_dp, 8, 128), F32), V((n_tp, 8, 128), F32),
        DMA((4, n_z)), DMA((4, n_z)), DMA((4, n_z)), DMA((4, n_z)), DMA((n_dp,)), DMA((n_dp,)), DMA((n_dp,)), DMA((n_dp,)), DMA((2,)), DMA((2,)),
        DMA((micro, 3)), DMA((micro, 3)),
        DMA((3, micro)), DMA((3, micro)), DMA((3, micro)), DMA((3, micro)), DMA((4, micro)), DMA((4, micro)),
        DMA((2, micro)),
        DMA((4, n_z)), DMA((4, n_z)), DMA((4, n_z)), DMA((4, n_z)), DMA((2,)), DMA((2,)), DMA((2, n_dp)), DMA((2, n_dp)),
        DMA((n_dp,)), DMA((n_dp,)), DMA((n_tp,)), DMA((n_tp,)),
    ]
    vm = pl.BlockSpec(memory_space=pltpu.VMEM)
    anywhere = pl.BlockSpec(memory_space=pl.ANY)
    S = jax.ShapeDtypeStruct
    return pl.pallas_call(
        partial(layer_kernel, dims),
        out_shape=(
            S((micro, tok, width), BF), S((micro, tok, width), F32),
            S((3, own_rows, local), F32), S((local, own_rows), F32), S((2, own_rows, ff), F32),
            S((2, 2, width), F32), S((8, 128), F32),
        ),
        in_specs=[vm] * 8,
        out_specs=(anywhere, anywhere, vm, vm, vm, vm, vm),
        scratch_shapes=scratch,
        compiler_params=pltpu.CompilerParams(
            collective_id=0, has_side_effects=True, vmem_limit_bytes=63 << 20
        ),
        name="layer",
    )(
        inputs, cotangent, embeds[:, None, :],
        item_ids[:, :, None], item_ids[:, None, :], a_in, b_in, np_in,
    )


def fast_local(
    n_dp, n_tp,
    inputs, cotangent, item_ids, timestep, qkv_weight, out_weight, up_weight, down_weight, norm_params,
    qkv_first, out_first, up_first, down_first, norm_first,
    qkv_second, out_second, up_second, down_second, norm_second,
):
    embeds = time_embed(timestep[:, 0], inputs.shape[2])
    narrow = [qkv_weight[:, i] for i in range(3)] + [out_weight.T]
    a_in = jnp.concatenate([fold(w.astype(BF)) for w in narrow], axis=1)
    b_in = jnp.stack([up_weight.astype(BF), down_weight.T.astype(BF)])
    np_in = jnp.pad(norm_params.astype(BF), ((0, 4), (0, 128 - norm_params.shape[1])))
    block_out, grad_input, ga, go, gb, gn, gs = layer_call(
        n_dp, n_tp, inputs, cotangent, item_ids, embeds, a_in, b_in, np_in
    )
    grad_norm = gs[0, 0]
    factor = jnp.minimum(1.0, clip_limit / (grad_norm + 1e-06))
    own = norm_params.shape[1]
    gnorm_rows = jnp.concatenate([gn[1], gn[0]], axis=0)
    gnorm_own = lax.dynamic_slice_in_dim(gnorm_rows, lax.axis_index("dp") * own, own, axis=1)
    grads = (jnp.moveaxis(ga, 0, 1), go, gb[0], gb[1].T, gnorm_own)
    weights = (qkv_weight, out_weight, up_weight, down_weight, norm_params)
    firsts = (qkv_first, out_first, up_first, down_first, norm_first)
    seconds = (qkv_second, out_second, up_second, down_second, norm_second)
    result = [
        adam_step(weights[index], grads[index] * factor, firsts[index], seconds[index]) for index in range(5)
    ]
    flat = [item for triple in result for item in triple]
    return (block_out, grad_input, grad_norm, *flat)


def layer_norm(values, gain_row, bias_row):
    centre = values - jnp.mean(values, axis=-1, keepdims=True)
    spread = jnp.mean(centre * centre, axis=-1, keepdims=True)
    return centre * lax.rsqrt(spread + norm_eps) * gain_row + bias_row


def masked_scores(query_rows, key_rows, same_item, score_scale):
    scores = (
        jnp.einsum("thd,shd->hts", query_rows, key_rows, preferred_element_type=jnp.float32)
        * score_scale
    )
    return jnp.where(same_item, scores, -1e30)


def one_micro(gathered, stream_in, upstream, labels, embed_row):
    qkv_mat, out_mat, up_mat, down_mat, norm_rows = gathered
    tokens_here = stream_in.shape[0]
    local_width = out_mat.shape[0]
    heads_here = local_width // HEAD_DIM
    score_scale = 1.0 / math.sqrt(HEAD_DIM)
    split_shape = (tokens_here, heads_here, HEAD_DIM)
    norm_gains = norm_rows.astype(jnp.float32)
    gain_one = 1.0 + norm_gains[0]
    gain_two = 1.0 + norm_gains[2]
    stream = stream_in.astype(jnp.float32) + embed_row[None, :]
    normed_f, norm_one_back = jax.vjp(layer_norm, stream, gain_one, norm_gains[1])
    normed = normed_f.astype(jnp.bfloat16)
    triple = jnp.einsum("td,dje->jte", normed, qkv_mat, preferred_element_type=jnp.float32).astype(
        jnp.bfloat16
    )
    query_rows = triple[0].reshape(split_shape)
    key_rows = triple[1].reshape(split_shape)
    value_rows = triple[2].reshape(split_shape)
    same_item = (labels[:, None] == labels[None, :])[None]
    scores = masked_scores(query_rows, key_rows, same_item, score_scale)
    row_top = jnp.max(scores, axis=-1, keepdims=True)
    exp_scores = jnp.exp(scores - row_top)
    row_total = jnp.sum(exp_scores, axis=-1, keepdims=True)
    probs_soft = exp_scores / row_total
    log_total = row_top + jnp.log(row_total)
    context = (
        jnp.einsum(
            "hts,shd->thd",
            probs_soft.astype(jnp.bfloat16),
            value_rows,
            preferred_element_type=jnp.float32,
        )
        .reshape(tokens_here, local_width)
        .astype(jnp.bfloat16)
    )
    attn_out = lax.psum(jnp.dot(context, out_mat, preferred_element_type=jnp.float32), "tp")
    middle = stream + attn_out
    normed_two_f, norm_two_back = jax.vjp(layer_norm, middle, gain_two, norm_gains[3])
    normed_two = normed_two_f.astype(jnp.bfloat16)
    hidden_pre = jnp.dot(normed_two, up_mat, preferred_element_type=jnp.float32)
    hidden_f, gelu_back = jax.vjp(partial(jax.nn.gelu, approximate=False), hidden_pre)
    hidden = hidden_f.astype(jnp.bfloat16)
    branch = lax.psum(
        jnp.dot(hidden, down_mat, preferred_element_type=jnp.float32).astype(jnp.bfloat16), "tp"
    ).astype(jnp.float32)
    block_out = (middle + branch).astype(jnp.bfloat16)
    grad_down = jnp.einsum("tf,td->fd", hidden, upstream, preferred_element_type=jnp.float32)
    grad_hidden = jnp.einsum("td,fd->tf", upstream, down_mat, preferred_element_type=jnp.float32)
    grad_pre = gelu_back(grad_hidden)[0].astype(jnp.bfloat16)
    grad_up = jnp.einsum("td,tf->df", normed_two, grad_pre, preferred_element_type=jnp.float32)
    grad_normed_two = lax.psum(
        jnp.einsum("tf,df->td", grad_pre, up_mat, preferred_element_type=jnp.float32), "tp"
    )
    grad_middle_norm, grad_gain_two, grad_bias_two = norm_two_back(grad_normed_two)
    grad_middle = upstream.astype(jnp.float32) + grad_middle_norm
    grad_attn = grad_middle.astype(jnp.bfloat16)
    grad_outmat = jnp.einsum("tc,td->cd", context, grad_attn, preferred_element_type=jnp.float32)
    grad_context = (
        jnp.einsum("td,cd->tc", grad_attn, out_mat, preferred_element_type=jnp.float32)
        .astype(jnp.bfloat16)
        .reshape(split_shape)
    )
    probs_again = jnp.exp(masked_scores(query_rows, key_rows, same_item, score_scale) - log_total)
    grad_values = jnp.einsum(
        "hts,thd->shd",
        probs_again.astype(jnp.bfloat16),
        grad_context,
        preferred_element_type=jnp.float32,
    )
    grad_probs = jnp.einsum(
        "thd,shd->hts", grad_context, value_rows, preferred_element_type=jnp.float32
    )
    inner_sum = jnp.sum(grad_probs * probs_again, axis=-1, keepdims=True)
    grad_scores = (probs_again * (grad_probs - inner_sum)).astype(jnp.bfloat16)
    grad_query = (
        jnp.einsum("hts,shd->thd", grad_scores, key_rows, preferred_element_type=jnp.float32)
        * score_scale
    )
    grad_key = (
        jnp.einsum("hts,thd->shd", grad_scores, query_rows, preferred_element_type=jnp.float32)
        * score_scale
    )
    grad_triple = (
        jnp.stack([grad_query, grad_key, grad_values])
        .reshape(3, tokens_here, local_width)
        .astype(jnp.bfloat16)
    )
    grad_qkv = jnp.einsum("td,jte->dje", normed, grad_triple, preferred_element_type=jnp.float32)
    grad_normed = lax.psum(
        jnp.einsum("jte,dje->td", grad_triple, qkv_mat, preferred_element_type=jnp.float32).astype(
            jnp.bfloat16
        ),
        "tp",
    ).astype(jnp.float32)
    grad_stream_norm, grad_gain_one, grad_bias_one = norm_one_back(grad_normed)
    grad_input = grad_middle + grad_stream_norm
    grad_norms = jnp.stack([grad_gain_one, grad_bias_one, grad_gain_two, grad_bias_two])
    return (block_out, grad_input, (grad_qkv, grad_outmat, grad_up, grad_down, grad_norms))


def local(
    inputs,
    cotangent,
    item_ids,
    timestep,
    qkv_weight,
    out_weight,
    up_weight,
    down_weight,
    norm_params,
    qkv_first,
    out_first,
    up_first,
    down_first,
    norm_first,
    qkv_second,
    out_second,
    up_second,
    down_second,
    norm_second,
):
    micro_count = inputs.shape[0]
    embeds = time_embed(timestep[:, 0], inputs.shape[2])
    qkv_low = qkv_weight.astype(jnp.bfloat16)
    out_low = out_weight.astype(jnp.bfloat16)
    up_low = up_weight.astype(jnp.bfloat16)
    down_low = down_weight.astype(jnp.bfloat16)
    norm_low = norm_params.astype(jnp.bfloat16)
    block_list = []
    input_list = []
    for number in range(micro_count):
        gathered = (
            lax.all_gather(qkv_low, "dp", axis=0, tiled=True),
            lax.all_gather(out_low, "dp", axis=1, tiled=True),
            lax.all_gather(up_low, "dp", axis=0, tiled=True),
            lax.all_gather(down_low, "dp", axis=1, tiled=True),
            lax.all_gather(norm_low, "dp", axis=1, tiled=True),
        )
        block_out, grad_input, grad_list = one_micro(
            gathered, inputs[number], cotangent[number], item_ids[number], embeds[number]
        )
        owned_grads = (
            lax.psum_scatter(grad_list[0], "dp", scatter_dimension=0, tiled=True),
            lax.psum_scatter(grad_list[1], "dp", scatter_dimension=1, tiled=True),
            lax.psum_scatter(grad_list[2], "dp", scatter_dimension=0, tiled=True),
            lax.psum_scatter(grad_list[3], "dp", scatter_dimension=1, tiled=True),
            lax.psum_scatter(grad_list[4], "dp", scatter_dimension=1, tiled=True),
        )
        if number == 0:
            totals = tuple(owned_grads)
        else:
            totals = tuple((left + right for left, right in zip(totals, owned_grads)))
        block_list.append(block_out)
        input_list.append(grad_input)
    own_squares = jnp.sum(totals[0] * totals[0]) + jnp.sum(totals[1] * totals[1])
    own_squares = own_squares + jnp.sum(totals[2] * totals[2]) + jnp.sum(totals[3] * totals[3])
    norm_squares = jnp.sum(totals[4] * totals[4])
    own_squares = own_squares + jnp.where(
        lax.axis_index("tp") == 0, norm_squares, jnp.zeros_like(norm_squares)
    )
    grad_norm = jnp.sqrt(lax.psum(own_squares, ("dp", "tp")))
    factor = jnp.minimum(1.0, clip_limit / (grad_norm + 1e-06))
    weights = (qkv_weight, out_weight, up_weight, down_weight, norm_params)
    firsts = (qkv_first, out_first, up_first, down_first, norm_first)
    seconds = (qkv_second, out_second, up_second, down_second, norm_second)
    result = [
        adam_step(weights[index], totals[index] * factor, firsts[index], seconds[index])
        for index in range(5)
    ]
    return (
        jnp.stack(block_list),
        jnp.stack(input_list),
        grad_norm,
        result[0][0],
        result[0][1],
        result[0][2],
        result[1][0],
        result[1][1],
        result[1][2],
        result[2][0],
        result[2][1],
        result[2][2],
        result[3][0],
        result[3][1],
        result[3][2],
        result[4][0],
        result[4][1],
        result[4][2],
    )


def solution(mesh):
    n_dp, n_tp = mesh.shape["dp"], mesh.shape["tp"]

    def step(*args):
        micro, tok, width = args[0].shape
        own_rows, _, local_width = args[4].shape
        fits = n_tp == 4 and n_dp == 8 and micro == 2 and tok == 512 and own_rows == 96
        if fits and local_width == 3 * HEAD_DIM and width % 256 == 0 and args[6].shape[1] % 256 == 0:
            return fast_local(n_dp, n_tp, *args)
        return local(*args)

    return jax.shard_map(
        step,
        mesh=mesh,
        in_specs=(
            P(None, "dp", None),
            P(None, "dp", None),
            P(None, "dp"),
            P(None, "dp"),
            P("dp", None, "tp"),
            P("tp", "dp"),
            P("dp", "tp"),
            P("tp", "dp"),
            P(None, "dp"),
            P("dp", None, "tp"),
            P("tp", "dp"),
            P("dp", "tp"),
            P("tp", "dp"),
            P(None, "dp"),
            P("dp", None, "tp"),
            P("tp", "dp"),
            P("dp", "tp"),
            P("tp", "dp"),
            P(None, "dp"),
        ),
        out_specs=(
            P(None, "dp", None),
            P(None, "dp", None),
            P(),
            P("dp", None, "tp"),
            P("dp", None, "tp"),
            P("dp", None, "tp"),
            P("tp", "dp"),
            P("tp", "dp"),
            P("tp", "dp"),
            P("dp", "tp"),
            P("dp", "tp"),
            P("dp", "tp"),
            P("tp", "dp"),
            P("tp", "dp"),
            P("tp", "dp"),
            P(None, "dp"),
            P(None, "dp"),
            P(None, "dp"),
        ),
        check_vma=False,
    )
```

```python
from functools import partial
import math

import jax
import jax.numpy as jnp
from jax import lax
from jax.experimental import pallas as pl
from jax.experimental.pallas import tpu as pltpu
from jax.sharding import PartitionSpec as P

HEAD_DIM = 64
STEP = 10

norm_eps = 1e-05
clip_limit = 1.0
learn_rate = 0.02
beta_one = 0.9
beta_two = 0.999
adam_eps = 1e-08
weight_decay = 0.01

BF = jnp.bfloat16
F32 = jnp.float32
MESH = pl.DeviceIdType.MESH


def time_embed(step_values, model_width):
    half_width = model_width // 2
    frequency = jnp.exp(
        jnp.arange(half_width, dtype=jnp.float32) * (-math.log(10000.0) / half_width)
    )
    angles = step_values.astype(jnp.float32)[..., None] * frequency
    return jnp.concatenate([jnp.sin(angles), jnp.cos(angles)], axis=-1)


def adam_step(weight, gradient, first_old, second_old):
    first_new = beta_one * first_old + (1.0 - beta_one) * gradient
    second_new = beta_two * second_old + (1.0 - beta_two) * gradient * gradient
    moment_one = first_new / (1.0 - beta_one**STEP)
    moment_two = second_new / (1.0 - beta_two**STEP)
    weight_new = weight - learn_rate * (
        moment_one / (jnp.sqrt(moment_two) + adam_eps) + weight_decay * weight
    )
    return (weight_new, first_new, second_new)


def mm(a, b, ca, cb):
    return lax.dot_general(a, b, (((ca,), (cb,)), ((), ())), preferred_element_type=F32)


def fold(v):
    cut = v.shape[-2] // 2
    low = jnp.concatenate([v[..., :cut, 128:], v[..., cut:, 128:]], axis=-1)
    return jnp.concatenate([v[..., :128], low], axis=-2)


def unfold(p):
    rows = 2 * p.shape[-2] // 3
    low = p[..., rows:, :]
    right = jnp.concatenate([low[..., :64], low[..., 64:]], axis=-2)
    return jnp.concatenate([p[..., :rows, :], right], axis=-1)


def layer_kernel(
    dims,
    x_in, cot_in, ids_ref, step_ref, wqkv_ref, wout_ref, wup_ref, wdown_ref, wnorm_ref,
    bo_ref, ig_ref, ga_ref, go_ref, gb_ref, gn_ref, gs_ref,
    x_ref, cot_ref, emb, lc, npin,
    wag, wqkv, woall, wo4, wb, npg, npt,
    normed, qkv, probs, ctx, ctxp, ctxr, n2, hid, dpre, mid, dmid, bo_own, dattn, dqkv,
    csend, crecv, own, ysend, yrecv, bsend, brecv, bown, bysend, byrecv,
    gfo, gfb, rax_s, rax_r, raz_s, raz_r, rbx_s, rbx_r, rbz_s, rbz_r,
    nacc, ncore, nsum, sqd, sqt,
    az_s, az_r, ax_s, ax_r, np_s, np_r, oy_s, oy_r, oc_s, oc_r, cx_s, cx_r,
    c_s, c_r, y_s, y_r, g_s, g_r, o_l, in_l,
    rx_s, rx_r, rz_s, rz_r, nc_s, nc_r, nd_s, nd_r, qd_s, qd_r, qt_s, qt_r,
):
    micro, tok, width, n_dp, n_tp, heads = dims
    n_z = n_dp // 2
    half = tok // 2
    own_rows = width // n_dp
    fold_rows = 3 * own_rows // 2
    local = heads * HEAD_DIM
    scale = 1.0 / math.sqrt(HEAD_DIM)

    dp = lax.axis_index("dp")
    tp = lax.axis_index("tp")
    z, xx = lax.div(dp, 2), lax.rem(dp, 2)
    yy, cc = lax.div(tp, 2), lax.rem(tp, 2)
    across_tp = 2 * (1 - yy) + cc
    x_peer = (2 * z + 1 - xx, tp)
    c_peer = (dp, 2 * yy + 1 - cc)
    y_peer = (dp, across_tp)
    d_peer = (dp, 2 * (1 - yy) + 1 - cc)

    far = lax.div(z, 2)
    column = (z + 1 - 2 * lax.rem(z, 2), 2 - far, 3 - 3 * far)
    inner = (z > 0) & (z < n_z - 1)
    near_peer = (2 * column[0] + xx, tp)
    mid_peer = (2 * column[1] + xx, tp)
    flip = 1 - xx

    def dp_of(k):
        return lax.rem(dp + k, n_dp)

    def tp_of(k):
        return lax.rem(tp + k, n_tp)

    sent, sent_inner = [], []

    def copy(src, dst, s_sem, r_sem, peer):
        return pltpu.make_async_remote_copy(
            src_ref=src, dst_ref=dst, send_sem=s_sem, recv_sem=r_sem, device_id=peer, device_id_type=MESH
        )

    def send(src, dst, s_sem, r_sem, peer):
        item = copy(src, dst, s_sem, r_sem, peer)
        item.start()
        sent.append(item)

    def send_inner(src, dst, s_sem, r_sem, peer):
        item = copy(src, dst, s_sem, r_sem, peer)
        pl.when(inner)(item.start)
        sent_inner.append(item)

    def arrive(dst, s_sem, r_sem, peer):
        copy(dst, dst, s_sem, r_sem, peer).wait_recv()

    loads = [
        pltpu.make_async_copy(x_in, x_ref, in_l.at[0]),
        pltpu.make_async_copy(cot_in, cot_ref, in_l.at[1]),
    ]
    for load in loads:
        load.start()
    for i in range(3):
        wag[dp, :, 128 * i : 128 * (i + 1)] = fold(wqkv_ref[i]).astype(BF)
    wag[dp, :, 384:512] = fold(wout_ref[...].T).astype(BF)
    wb[0, dp] = wup_ref[...].astype(BF)
    wb[1, dp] = wdown_ref[...].astype(BF)
    npin[...] = jnp.zeros_like(npin)
    npin[:4, :own_rows] = wnorm_ref[...].astype(BF)
    place = lax.broadcasted_iota(jnp.int32, (1, width // 2), 1).astype(F32)
    rates = jnp.exp(place * (-math.log(10000.0) / (width // 2)))
    for m in range(micro):
        angles = step_ref[:, m : m + 1].astype(F32) * rates
        emb[m : m + 1, : width // 2] = jnp.sin(angles)
        emb[m : m + 1, width // 2 :] = jnp.cos(angles)
    labels = ids_ref[...].astype(F32)
    columns = jnp.concatenate([labels] * (8 // micro), axis=0).T
    for m in range(micro):
        lc[m] = columns[:, m : m + 1]

    barrier = pltpu.get_barrier_semaphore()
    for k in range(1, n_dp):
        pl.semaphore_signal(barrier, inc=1, device_id=(dp_of(k), tp), device_id_type=MESH)
    for k in range(1, n_tp):
        pl.semaphore_signal(barrier, inc=1, device_id=(dp, tp_of(k)), device_id_type=MESH)
    pl.semaphore_wait(barrier, n_dp + n_tp - 2)

    def rows_of(j):
        return pl.ds(pl.multiple_of(j * own_rows, own_rows), own_rows)

    def half_rows(h):
        return pl.ds(pl.multiple_of(h * half, half), half)

    mine = half_rows(cc)
    other = half_rows(1 - cc)

    def ag_at(g, j):
        if g < 2:
            return wag.at[j, :, pl.ds(384 * g, 384 - 256 * g)]
        return wb.at[g - 2, j]

    def ag_column(g):
        block = ag_at(g, dp)
        send(block, block, az_s.at[g, 0], az_r.at[g, 0], near_peer)
        send_inner(block, block, az_s.at[g, 1], az_r.at[g, 1], mid_peer)

    def ag_side(g):
        send(ag_at(g, dp), ag_at(g, dp), ax_s.at[g, 3], ax_r.at[g, z], x_peer)

    def ag_pass(g, *which):
        for i in which:
            s = column[i]
            block = ag_at(g, 2 * s + xx)
            arrive(block, az_s.at[g, 0], az_r.at[g, i], near_peer)
            send_inner(block, block, az_s.at[g, 2 + i], az_r.at[g, i or 2], near_peer if i else mid_peer)
            send(block, block, ax_s.at[g, i], ax_r.at[g, s], x_peer)

    def ag_done(g):
        for i, s in enumerate((*column, z)):
            arrive(ag_at(g, 2 * s + flip), ax_s.at[g, i], ax_r.at[g, s], x_peer)

    def o_send(col, which):
        for i in which:
            j = 2 * (*column, z)[i] + col
            part = ag_at(1, j)
            send(part, woall.at[tp, j], oy_s.at[j], oy_r.at[j], y_peer)

    def o_core():
        woall[tp] = wag[:, :, 384:512]
        send(woall.at[tp], woall.at[tp], oc_s.at[0], oc_r.at[0], c_peer)

    def o_across():
        for j in range(n_dp):
            arrive(woall.at[across_tp, j], oy_s.at[j], oy_r.at[j], y_peer)
        send(woall.at[across_tp], woall.at[across_tp], oc_s.at[1], oc_r.at[1], c_peer)

    def o_done():
        arrive(woall.at[2 * yy + 1 - cc], oc_s.at[0], oc_r.at[0], c_peer)
        arrive(woall.at[2 * (1 - yy) + 1 - cc], oc_s.at[1], oc_r.at[1], c_peer)
        for t in range(n_tp):
            wo4[t] = unfold(woall[t]).reshape(width, local)

    def ar_refs(kind, m):
        if kind < 2:
            return csend.at[kind, m], crecv.at[kind, m], own.at[m], ysend.at[kind, m], yrecv.at[kind, m]
        return [r.at[kind - 2, m] for r in (bsend, brecv, bown, bysend, byrecv)]

    def ar_start(kind, m, part):
        here, there, keep, _, _ = ar_refs(kind, m)
        here[...] = part(other).astype(BF)
        send(here, there, c_s.at[kind, m], c_r.at[kind, m], c_peer)
        keep[...] = part(mine)

    def ar_cross(kind, m):
        _, there, keep, here, across = ar_refs(kind, m)
        arrive(there, c_s.at[kind, m], c_r.at[kind, m], c_peer)
        here[...] = (keep[...] + there[...].astype(F32)).astype(BF)
        send(here, across, y_s.at[kind, m], y_r.at[kind, m], y_peer)

    def ar_total(kind, m):
        _, _, _, here, across = ar_refs(kind, m)
        arrive(across, y_s.at[kind, m], y_r.at[kind, m], y_peer)
        return here[...].astype(F32) + across[...].astype(F32)

    def share(i, m, ref):
        send(ref.at[m, mine], ref.at[m, mine], g_s.at[i, m], g_r.at[i, m], c_peer)

    def shared(i, m, ref):
        arrive(ref.at[m, other], g_s.at[i, m], g_r.at[i, m], c_peer)

    def centred(v):
        c0 = v - jnp.mean(v, axis=-1, keepdims=True)
        return c0, lax.rsqrt(jnp.mean(c0 * c0, axis=-1, keepdims=True) + norm_eps)

    def norm_back(grad, hat, inv, gain):
        dhat = grad * gain
        return inv * (
            dhat
            - jnp.mean(dhat, axis=-1, keepdims=True)
            - hat * jnp.mean(dhat * hat, axis=-1, keepdims=True)
        )

    def open_norms():
        block = lax.broadcasted_iota(jnp.int32, (n_dp, 128, width), 0)
        row = lax.broadcasted_iota(jnp.int32, (n_dp, 128, width), 1)
        col = lax.broadcasted_iota(jnp.int32, (n_dp, 128, width), 2)
        place = ((col == block * own_rows + row) & (row < own_rows)).astype(F32).astype(BF)
        rows = npg[0]
        total = mm(rows, place[0], 1, 0)
        for j in range(1, n_dp):
            total = total + mm(npg[j], place[j], 1, 0)
        npt[...] = total

    def gain_row(i):
        return 1.0 + npt[pl.ds(i, 1), :]

    def bias_row(i):
        return npt[pl.ds(i, 1), :]

    def stream_of(m, rows):
        return x_ref[m, rows, :].astype(F32) + emb[pl.ds(m, 1), :]

    def first_norm(m):
        c0, inv = centred(stream_of(m, pl.ds(0, tok)))
        normed[m] = (c0 * inv * gain_row(0) + bias_row(1)).astype(BF)

    def open_qkv():
        for i in range(3):
            wqkv[i] = unfold(wag[:, :, 128 * i : 128 * (i + 1)]).reshape(width, local)

    def project(m):
        for i in range(3):
            qkv[i, m] = mm(normed[m], wqkv[i], 1, 0).astype(BF)

    lane = lax.broadcasted_iota(jnp.int32, (1, local), 1)

    def head_mask(h, value):
        here = (lane >= h * HEAD_DIM) & (lane < (h + 1) * HEAD_DIM)
        return jnp.where(here, value, 0.0).astype(BF)

    def attend(m, *between):
        same = lc[m] == ids_ref[pl.ds(m, 1), :].astype(F32)
        total = None
        for h in range(heads):
            s = mm(qkv[0, m] * head_mask(h, scale), qkv[1, m], 1, 1)
            s = jnp.where(same, s, -1e30)
            e = jnp.exp(s - jnp.max(s, axis=-1, keepdims=True))
            p = e * (1.0 / jnp.sum(e, axis=-1, keepdims=True))
            probs[m * heads + h] = p
            part = mm(p.astype(BF), qkv[2, m] * head_mask(h, 1.0), 1, 0)
            total = part if total is None else total + part
            for work in between[h] if h < len(between) else ():
                work()
        ctx[m] = total.astype(BF)
        for i in range(2):
            ctxp[m, i] = fold(total[i * half : (i + 1) * half]).astype(BF)
        send(ctxp.at[m, cc], ctxr.at[m, tp], cx_s.at[m, 1], cx_r.at[m, 1], y_peer)
        send(ctxp.at[m, 1 - cc], ctxr.at[m, tp], cx_s.at[m, 2], cx_r.at[m, 2], d_peer)
        send(ctxp.at[m, 1 - cc], ctxr.at[m, tp], cx_s.at[m, 0], cx_r.at[m, 0], c_peer)
        ctxr[m, tp] = ctxp[m, cc]

    def second_norm(m):
        arrive(ctxr.at[m, 2 * yy + 1 - cc], cx_s.at[m, 0], cx_r.at[m, 0], c_peer)
        arrive(ctxr.at[m, across_tp], cx_s.at[m, 1], cx_r.at[m, 1], y_peer)
        arrive(ctxr.at[m, 2 * (1 - yy) + 1 - cc], cx_s.at[m, 2], cx_r.at[m, 2], d_peer)
        middle = stream_of(m, mine)
        for t in range(n_tp):
            middle = middle + mm(unfold(ctxr[m, t]), wo4[t], 1, 1)
        mid[m] = middle
        c0, inv = centred(middle)
        n2[m, mine, :] = (c0 * inv * gain_row(2) + bias_row(3)).astype(BF)
        share(0, m, n2)

    def wide(g):
        return wb[g].reshape(width, wb.shape[-1])

    def feed(m):
        shared(0, m, n2)
        pre = mm(n2[m], wide(0), 1, 0)
        cdf = 0.5 * (1.0 + lax.erf(pre * math.sqrt(0.5)))
        hid[m] = (pre * cdf).astype(BF)
        slope = cdf + pre * (jnp.exp(-0.5 * pre * pre) * (1.0 / math.sqrt(2.0 * math.pi)))
        if m == 0:
            gfb[0, :tok, :] = slope
        else:
            dmid[...] = slope.reshape(2, half, slope.shape[-1])

    def feed_back(m):
        slope = gfb[0, :tok, :] if m == 0 else dmid[...].reshape(tok, dmid.shape[-1])
        dpre[m] = (mm(cot_ref[m], wide(1), 1, 0) * slope).astype(BF)

    def dn2_part(m):
        return lambda rows: mm(dpre[m, rows, :], wide(0), 1, 1)

    def branch_part(m, col):
        def part(rows):
            blocks = [wb[1, 2 * at + col] for at in range(n_z)]
            return mm(hid[m, rows, :], jnp.concatenate(blocks, axis=0), 1, 1)

        return part

    def col_sum(v):
        return jnp.sum(v, axis=0, keepdims=True)

    def second_back(m):
        grad = ar_total(0, m)
        c0, inv = centred(mid[m])
        hat = c0 * inv
        nacc[m, pl.ds(0, 1), :] = col_sum(grad * hat)
        nacc[m, pl.ds(1, 1), :] = col_sum(grad)
        grad_middle = cot_ref[m, mine, :].astype(F32) + norm_back(grad, hat, inv, gain_row(2))
        dmid[m] = grad_middle
        dattn[m, mine, :] = grad_middle.astype(BF)
        share(1, m, dattn)

    def finish_block(m):
        near, away = ar_total(2, m), ar_total(3, m)
        even = jnp.where(xx == 0, near, away)
        odd = jnp.where(xx == 0, away, near)
        pieces = []
        for at in range(n_z):
            cut = slice(at * own_rows, (at + 1) * own_rows)
            pieces += [even[:, cut], odd[:, cut]]
        bo_own[m] = (mid[m] + jnp.concatenate(pieces, axis=1)).astype(BF)
        send(bo_own.at[m], bo_ref.at[m, mine], g_s.at[2, m], g_r.at[2, m], c_peer)
        pltpu.make_async_copy(bo_own.at[m], bo_ref.at[m, mine], o_l.at[0, m]).start()

    def attend_back(m, *between):
        shared(1, m, dattn)
        wo_own = wo4[tp]
        dctx = mm(dattn[m], wo_own, 1, 0).astype(BF)
        dq = dk = dv = None
        for h in range(heads):
            dch = dctx * head_mask(h, 1.0)
            p = probs[m * heads + h]
            dp_ = mm(dch, qkv[2, m], 1, 1)
            inner = jnp.sum(dp_ * p, axis=-1, keepdims=True)
            ds = (p * (dp_ - inner)).astype(BF)
            mask = head_mask(h, scale)
            a = mm(ds, qkv[1, m] * mask, 1, 0)
            b = mm(ds, qkv[0, m] * mask, 0, 0)
            c = mm(p.astype(BF), dch, 0, 0)
            dq = a if dq is None else dq + a
            dk = b if dk is None else dk + b
            dv = c if dv is None else dv + c
            for work in between[h] if h < len(between) else ():
                work()
        dqkv[0, m] = dq.astype(BF)
        dqkv[1, m] = dk.astype(BF)
        dqkv[2, m] = dv.astype(BF)

    def dn1_part(m):
        def part(rows):
            total = mm(dqkv[0, m, rows, :], wqkv[0], 1, 1)
            for i in range(1, 3):
                total = total + mm(dqkv[i, m, rows, :], wqkv[i], 1, 1)
            return total

        return part

    def first_back(m):
        grad = ar_total(1, m)
        c0, inv = centred(stream_of(m, mine))
        hat = c0 * inv
        nacc[m, pl.ds(2, 1), :] = col_sum(grad * hat)
        nacc[m, pl.ds(3, 1), :] = col_sum(grad)
        dmid[m] = dmid[m] + norm_back(grad, hat, inv, gain_row(0))
        send(dmid.at[m], ig_ref.at[m, mine], g_s.at[3, m], g_r.at[3, m], c_peer)
        pltpu.make_async_copy(dmid.at[m], ig_ref.at[m, mine], o_l.at[1, m]).start()

    def gf(g, at, col):
        if g == 0:
            rows = pl.ds(pl.multiple_of(col * fold_rows, fold_rows), fold_rows)
            return probs.at[at, rows, pl.ds(0, 384)]
        return gfo.at[2 * at + col] if g == 1 else gfb.at[g - 2, rows_of(2 * at + col)]

    def rs_slots(g, at):
        if g < 2:
            lanes = pl.ds(384 * g, 384 - 256 * g)
            return [r.at[at, :, lanes] for r in (rax_s, rax_r, raz_s, raz_r)]
        return [r.at[g - 2, at] for r in (rbx_s, rbx_r, rbz_s, rbz_r)]

    def flat(ref):
        return ref[...].reshape(micro * tok, ref.shape[-1])

    def rs_wide(g, left, right):
        gfb[g - 2] = mm(flat(left), flat(right), 0, 0)

    def rs_narrow(i, left, right):
        grad = fold(mm(flat(left), flat(right), 0, 0).reshape(n_dp, own_rows, local))
        if i == 3:
            gfo[...] = grad
            return
        for j in range(n_dp):
            rows = pl.ds((j % 2) * fold_rows, fold_rows)
            probs[j // 2, rows, 128 * i : 128 * (i + 1)] = grad[j]

    def rs_start(g):
        for i in (2, 1, 0, 3):
            at = (*column, z)[i]
            here, there, _, _ = rs_slots(g, at)
            here[...] = gf(g, at, flip)[...].astype(BF)
            send(here, there, rx_s.at[g, i], rx_r.at[g, at], x_peer)

    def rs_sum(g, i):
        at = (*column, z)[i]
        there = rs_slots(g, at)[1]
        arrive(there, rx_s.at[g, i], rx_r.at[g, at], x_peer)
        return gf(g, at, xx)[...] + there[...].astype(F32)

    def rs_pass(g, *which):
        for i in which:
            at = column[i]
            here = rs_slots(g, at)[2]
            here[...] = rs_sum(g, i).astype(BF)
            send(here, rs_slots(g, z)[3], rz_s.at[g, i], rz_r.at[g, z], (2 * at + xx, tp))

    def rs_finish(g):
        total = rs_sum(g, 3)
        for i in range(3):
            s = column[i]
            there = rs_slots(g, s)[3]
            arrive(there, rz_s.at[g, i], rz_r.at[g, s], (2 * s + xx, tp))
            total = total + there[...].astype(F32)
        if g == 0:
            for i in range(3):
                ga_ref[i] = unfold(total[:, 128 * i : 128 * (i + 1)])
        elif g == 1:
            go_ref[...] = unfold(total).T
        else:
            gb_ref[g - 2] = total
        return jnp.sum(col_sum(total * total), axis=1, keepdims=True)

    def norm_start(e):
        both = nacc[0, pl.ds(2 * e, 2), :]
        for m in range(1, micro):
            both = both + nacc[m, pl.ds(2 * e, 2), :]
        ncore[e, 0] = both
        send(ncore.at[e, 0], ncore.at[e, 1], nc_s.at[e], nc_r.at[e], c_peer)

    def norm_cross(e):
        arrive(ncore.at[e, 1], nc_s.at[e], nc_r.at[e], c_peer)
        nsum[e, dp] = ncore[e, 0] + ncore[e, 1]
        for k in range(1, n_dp):
            send(nsum.at[e, dp], nsum.at[e, dp], nd_s.at[e, k], nd_r.at[e, k], (dp_of(k), tp))

    def norm_finish(e):
        for k in range(1, n_dp):
            j = lax.rem(dp + n_dp - k, n_dp)
            arrive(nsum.at[e, j], nd_s.at[e, k], nd_r.at[e, k], (dp_of(k), tp))
        total = nsum[e, 0]
        for j in range(1, n_dp):
            total = total + nsum[e, j]
        mine_only = jnp.zeros((2, own_rows), F32)
        for j in range(n_dp):
            mine_only = jnp.where(dp == j, total[:, j * own_rows : (j + 1) * own_rows], mine_only)
        gn_ref[pl.ds(2 - 2 * e, 2), :] = mine_only
        return jnp.sum(col_sum(total * total), axis=1, keepdims=True)

    ag_side(0)
    ag_column(0)
    ag_column(1)
    ag_side(1)
    npg[dp] = npin[...]
    for k in range(1, n_dp):
        send(npin, npg.at[dp], np_s.at[k], np_r.at[k], (dp_of(k), tp))
    o_send(xx, (3,))
    ag_side(2)
    ag_pass(0, 0)
    for k in range(1, n_dp):
        arrive(npg.at[lax.rem(dp + n_dp - k, n_dp)], np_s.at[k], np_r.at[k], (dp_of(k), tp))
    open_norms()
    loads[0].wait()
    ag_pass(0, 1)
    first_norm(0)
    ag_pass(0, 2)
    ag_pass(1, 0)
    ag_column(2)
    first_norm(1)
    ag_pass(1, 1, 2)
    ag_done(0)
    open_qkv()
    project(0)
    ag_column(3)
    o_send(xx, (0, 1, 2))
    project(1)
    ag_pass(2, 0)

    def o_rest():
        ag_done(1)
        o_send(flip, (0, 1, 2, 3))
        o_core()

    attend(0, (o_rest, partial(ag_pass, 2, 1)), (partial(ag_pass, 2, 2),), (partial(ag_side, 3),))
    attend(1, (partial(ag_pass, 3, 0),), (partial(ag_pass, 3, 1),), (o_across,))
    o_done()
    second_norm(0)
    second_norm(1)
    ag_pass(3, 2)
    ag_done(2)
    loads[1].wait()
    feed(0)
    ar_start(2, 0, branch_part(0, xx))
    feed(1)
    ar_cross(2, 0)
    ar_start(2, 1, branch_part(1, xx))
    rs_wide(3, cot_ref, hid)
    ar_cross(2, 1)
    ag_done(3)
    feed_back(0)
    ar_start(0, 0, dn2_part(0))
    rs_start(3)
    feed_back(1)
    ar_cross(0, 0)
    ar_start(0, 1, dn2_part(1))
    rs_wide(2, n2, dpre)
    ar_cross(0, 1)
    rs_start(2)
    rs_pass(3, 2, 1)
    second_back(0)
    rs_pass(3, 0)
    attend_back(0)
    ar_start(1, 0, dn1_part(0))
    rs_pass(2, 2)
    ar_cross(1, 0)
    second_back(1)
    rs_pass(2, 1)
    norm_start(0)
    attend_back(
        1,
        (partial(rs_narrow, 3, dattn, ctx), partial(rs_start, 1), partial(rs_pass, 2, 0)),
        (partial(norm_cross, 0),),
    )
    ar_start(1, 1, dn1_part(1))
    rs_narrow(0, normed, dqkv.at[0])
    ar_cross(1, 1)
    rs_narrow(1, normed, dqkv.at[1])
    rs_narrow(2, normed, dqkv.at[2])
    rs_start(0)
    rs_pass(1, 2, 1, 0)
    ar_start(3, 0, branch_part(0, flip))
    ar_start(3, 1, branch_part(1, flip))
    ar_cross(3, 0)
    ar_cross(3, 1)
    first_back(0)
    rs_pass(0, 2, 1)
    squares = rs_finish(3) + rs_finish(2)
    squares = squares + rs_finish(1)
    rs_pass(0, 0)
    first_back(1)
    norm_start(1)
    norm_cross(1)
    squares = squares + rs_finish(0)
    sqd[dp] = jnp.broadcast_to(squares, (8, 128))
    for k in range(1, n_dp):
        send(sqd.at[dp], sqd.at[dp], qd_s.at[k], qd_r.at[k], (dp_of(k), tp))
    extra = norm_finish(0) + norm_finish(1)
    for k in range(1, n_dp):
        j = lax.rem(dp + n_dp - k, n_dp)
        arrive(sqd.at[j], qd_s.at[k], qd_r.at[k], (dp_of(k), tp))
    mesh_row = sqd[0]
    for j in range(1, n_dp):
        mesh_row = mesh_row + sqd[j]
    sqt[tp] = mesh_row
    for k in range(1, n_tp):
        send(sqt.at[tp], sqt.at[tp], qt_s.at[k], qt_r.at[k], (dp, tp_of(k)))
    for k in range(1, n_tp):
        j = lax.rem(tp + n_tp - k, n_tp)
        arrive(sqt.at[j], qt_s.at[k], qt_r.at[k], (dp, tp_of(k)))
    everything = sqt[0]
    for j in range(1, n_tp):
        everything = everything + sqt[j]
    gs_ref[...] = jnp.sqrt(everything + extra)
    finish_block(0)
    finish_block(1)
    for m in range(micro):
        arrive(bo_ref.at[m, other], g_s.at[2, m], g_r.at[2, m], c_peer)
        arrive(ig_ref.at[m, other], g_s.at[3, m], g_r.at[3, m], c_peer)
        pltpu.make_async_copy(bo_own.at[m], bo_ref.at[m, mine], o_l.at[0, m]).wait()
        pltpu.make_async_copy(dmid.at[m], ig_ref.at[m, mine], o_l.at[1, m]).wait()
    for item in sent:
        item.wait_send()
    for item in sent_inner:
        pl.when(inner)(item.wait_send)


def layer_call(n_dp, n_tp, inputs, cotangent, item_ids, timestep, qkv, out, up, down, norms):
    micro, tok, width = inputs.shape
    own_rows, ff = up.shape
    local = qkv.shape[2]
    fold_rows = 3 * own_rows // 2
    heads = local // HEAD_DIM
    half = tok // 2
    fold_half = 3 * half // 2
    dims = (micro, tok, width, n_dp, n_tp, heads)
    V = pltpu.VMEM
    DMA = pltpu.SemaphoreType.DMA
    n_z = n_dp // 2
    room = max(micro * heads, n_z)
    scratch = [
        V((micro, tok, width), BF), V((micro, tok, width), BF), V((micro, width), F32), V((micro, tok, 1), F32), V((8, 128), BF),
        V((n_dp, fold_rows, 512), BF), V((3, width, local), BF), V((n_tp, n_dp, fold_rows, 128), BF),
        V((n_tp, width, local), BF), V((2, n_dp, own_rows, ff), BF), V((n_dp, 8, 128), BF), V((8, width), F32),
        V((micro, tok, width), BF), V((3, micro, tok, local), BF), V((room, tok, tok), F32),
        V((micro, tok, local), BF), V((micro, 2, fold_half, 128), BF), V((micro, n_tp, fold_half, 128), BF),
        V((micro, tok, width), BF), V((micro, tok, ff), BF), V((micro, tok, ff), BF),
        V((micro, half, width), F32), V((micro, half, width), F32), V((micro, half, width), BF),
        V((micro, tok, width), BF), V((3, micro, tok, local), BF),
        V((2, micro, half, width), BF), V((2, micro, half, width), BF), V((micro, half, width), F32),
        V((2, micro, half, width), BF), V((2, micro, half, width), BF),
        V((2, micro, half, width // 2), BF), V((2, micro, half, width // 2), BF), V((2, micro, half, width // 2), F32),
        V((2, micro, half, width // 2), BF), V((2, micro, half, width // 2), BF),
        V((n_dp, fold_rows, 128), F32), V((2, width, ff), F32),
        V((n_z, fold_rows, 512), BF), V((n_z, fold_rows, 512), BF), V((n_z, fold_rows, 512), BF), V((n_z, fold_rows, 512), BF),
        V((2, n_z, own_rows, ff), BF), V((2, n_z, own_rows, ff), BF), V((2, n_z, own_rows, ff), BF), V((2, n_z, own_rows, ff), BF),
        V((micro, 8, width), F32), V((2, 2, 2, width), F32), V((2, n_dp, 2, width), F32),
        V((n_dp, 8, 128), F32), V((n_tp, 8, 128), F32),
        DMA((4, 5)), DMA((4, 3)), DMA((4, n_z)), DMA((4, n_z)), DMA((n_dp,)), DMA((n_dp,)), DMA((n_dp,)), DMA((n_dp,)), DMA((2,)), DMA((2,)),
        DMA((micro, 3)), DMA((micro, 3)),
        DMA((4, micro)), DMA((4, micro)), DMA((4, micro)), DMA((4, micro)), DMA((4, micro)), DMA((4, micro)),
        DMA((2, micro)), DMA((2,)),
        DMA((4, n_z)), DMA((4, n_z)), DMA((4, n_z)), DMA((4, n_z)), DMA((2,)), DMA((2,)), DMA((2, n_dp)), DMA((2, n_dp)),
        DMA((n_dp,)), DMA((n_dp,)), DMA((n_tp,)), DMA((n_tp,)),
    ]
    vm = pl.BlockSpec(memory_space=pltpu.VMEM)
    anywhere = pl.BlockSpec(memory_space=pl.ANY)
    S = jax.ShapeDtypeStruct
    return pl.pallas_call(
        partial(layer_kernel, dims),
        out_shape=(
            S((micro, tok, width), BF), S((micro, tok, width), F32),
            S((3, own_rows, local), F32), S((local, own_rows), F32), S((2, own_rows, ff), F32),
            S((4, own_rows), F32), S((8, 128), F32),
        ),
        in_specs=[anywhere] * 2 + [vm] * 7,
        out_specs=(anywhere, anywhere, vm, vm, vm, vm, vm),
        scratch_shapes=scratch,
        compiler_params=pltpu.CompilerParams(
            collective_id=0, has_side_effects=True, vmem_limit_bytes=63 << 20
        ),
        name="layer",
    )(inputs, cotangent, item_ids, timestep, qkv, out, up, down, norms)


def adam_kernel(*refs):
    bo_in, ig_in, gs_ref = refs[:3]
    grads = (refs[3], refs[4], refs[5].at[0], refs[5].at[1], refs[6])
    olds = refs[7:22]
    bo_ref, ig_ref, norm_ref = refs[22:25]
    news = refs[25:40]
    loaded, stored = refs[40:55], refs[55:70]
    bo_held, ig_held, in_sem, out_sem, move_sem = refs[70:]
    takes = [
        pltpu.make_async_copy(bo_in, bo_held, move_sem.at[0]), pltpu.make_async_copy(ig_in, ig_held, move_sem.at[1])
    ]
    moves = [
        pltpu.make_async_copy(bo_held, bo_ref, move_sem.at[2]), pltpu.make_async_copy(ig_held, ig_ref, move_sem.at[3])
    ]
    loads = [pltpu.make_async_copy(olds[i], loaded[i], in_sem.at[i]) for i in range(15)]
    stores = [pltpu.make_async_copy(stored[i], news[i], out_sem.at[i]) for i in range(15)]
    for load in loads:
        load.start()
    for take in takes:
        take.start()
    grad_norm = gs_ref[pl.ds(0, 1), pl.ds(0, 1)]
    norm_ref[...] = grad_norm
    factor = jnp.minimum(1.0, clip_limit / (grad_norm + 1e-06))
    for p in range(5):
        for i in range(3):
            loads[3 * p + i].wait()
        weight, first, second = loaded[3 * p : 3 * p + 3]
        results = adam_step(weight[...], grads[p][...] * factor, first[...], second[...])
        for i in range(3):
            stored[3 * p + i][...] = results[i]
            stores[3 * p + i].start()
        if p in (1, 3):
            takes[p // 2].wait()
            moves[p // 2].start()
    for store in stores:
        store.wait()
    for move in moves:
        move.wait()


def adam_call(block_out, grad_input, gs, grads, olds):
    vm = pl.BlockSpec(memory_space=pltpu.VMEM)
    anywhere = pl.BlockSpec(memory_space=pl.ANY)
    S = jax.ShapeDtypeStruct
    like = [S(o.shape, o.dtype) for o in olds]
    return pl.pallas_call(
        adam_kernel,
        out_shape=(
            S(block_out.shape, block_out.dtype), S(grad_input.shape, grad_input.dtype), S((1, 1), F32), *like
        ),
        in_specs=[anywhere] * 2 + [vm] * 5 + [anywhere] * 15,
        out_specs=(anywhere, anywhere, vm, *[anywhere] * 15),
        scratch_shapes=[pltpu.VMEM(o.shape, o.dtype) for o in olds] * 2
        + [pltpu.VMEM(block_out.shape, block_out.dtype), pltpu.VMEM(grad_input.shape, grad_input.dtype)]
        + [pltpu.SemaphoreType.DMA((15,)), pltpu.SemaphoreType.DMA((15,)), pltpu.SemaphoreType.DMA((4,))],
        compiler_params=pltpu.CompilerParams(vmem_limit_bytes=63 << 20),
        name="adam",
    )(block_out, grad_input, gs, *grads, *olds)


def fast_local(
    n_dp, n_tp,
    inputs, cotangent, item_ids, timestep, qkv_weight, out_weight, up_weight, down_weight, norm_params,
    qkv_first, out_first, up_first, down_first, norm_first,
    qkv_second, out_second, up_second, down_second, norm_second,
):
    def turned(qkv, out, up, down, norms):
        return (jnp.moveaxis(qkv, 1, 0), out, up, down.T, norms)

    weights = turned(qkv_weight, out_weight, up_weight, down_weight, norm_params)
    firsts = turned(qkv_first, out_first, up_first, down_first, norm_first)
    seconds = turned(qkv_second, out_second, up_second, down_second, norm_second)
    block_out, grad_input, ga, go, gb, gn, gs = layer_call(
        n_dp, n_tp, inputs, cotangent, item_ids, timestep.T, *weights
    )
    olds = [item for p in range(5) for item in (weights[p], firsts[p], seconds[p])]
    block_out, grad_input, grad_norm, *news = adam_call(block_out, grad_input, gs, (ga, go, gb, gn), olds)
    for i in range(3):
        news[i] = jnp.moveaxis(news[i], 0, 1)
        news[9 + i] = news[9 + i].T
    return (block_out, grad_input, grad_norm[0, 0], *news)


def layer_norm(values, gain_row, bias_row):
    centre = values - jnp.mean(values, axis=-1, keepdims=True)
    spread = jnp.mean(centre * centre, axis=-1, keepdims=True)
    return centre * lax.rsqrt(spread + norm_eps) * gain_row + bias_row


def masked_scores(query_rows, key_rows, same_item, score_scale):
    scores = (
        jnp.einsum("thd,shd->hts", query_rows, key_rows, preferred_element_type=jnp.float32)
        * score_scale
    )
    return jnp.where(same_item, scores, -1e30)


def one_micro(gathered, stream_in, upstream, labels, embed_row):
    qkv_mat, out_mat, up_mat, down_mat, norm_rows = gathered
    tokens_here = stream_in.shape[0]
    local_width = out_mat.shape[0]
    heads_here = local_width // HEAD_DIM
    score_scale = 1.0 / math.sqrt(HEAD_DIM)
    split_shape = (tokens_here, heads_here, HEAD_DIM)
    norm_gains = norm_rows.astype(jnp.float32)
    gain_one = 1.0 + norm_gains[0]
    gain_two = 1.0 + norm_gains[2]
    stream = stream_in.astype(jnp.float32) + embed_row[None, :]
    normed_f, norm_one_back = jax.vjp(layer_norm, stream, gain_one, norm_gains[1])
    normed = normed_f.astype(jnp.bfloat16)
    triple = jnp.einsum("td,dje->jte", normed, qkv_mat, preferred_element_type=jnp.float32).astype(
        jnp.bfloat16
    )
    query_rows = triple[0].reshape(split_shape)
    key_rows = triple[1].reshape(split_shape)
    value_rows = triple[2].reshape(split_shape)
    same_item = (labels[:, None] == labels[None, :])[None]
    scores = masked_scores(query_rows, key_rows, same_item, score_scale)
    row_top = jnp.max(scores, axis=-1, keepdims=True)
    exp_scores = jnp.exp(scores - row_top)
    row_total = jnp.sum(exp_scores, axis=-1, keepdims=True)
    probs_soft = exp_scores / row_total
    log_total = row_top + jnp.log(row_total)
    context = (
        jnp.einsum(
            "hts,shd->thd",
            probs_soft.astype(jnp.bfloat16),
            value_rows,
            preferred_element_type=jnp.float32,
        )
        .reshape(tokens_here, local_width)
        .astype(jnp.bfloat16)
    )
    attn_out = lax.psum(jnp.dot(context, out_mat, preferred_element_type=jnp.float32), "tp")
    middle = stream + attn_out
    normed_two_f, norm_two_back = jax.vjp(layer_norm, middle, gain_two, norm_gains[3])
    normed_two = normed_two_f.astype(jnp.bfloat16)
    hidden_pre = jnp.dot(normed_two, up_mat, preferred_element_type=jnp.float32)
    hidden_f, gelu_back = jax.vjp(partial(jax.nn.gelu, approximate=False), hidden_pre)
    hidden = hidden_f.astype(jnp.bfloat16)
    branch = lax.psum(
        jnp.dot(hidden, down_mat, preferred_element_type=jnp.float32).astype(jnp.bfloat16), "tp"
    ).astype(jnp.float32)
    block_out = (middle + branch).astype(jnp.bfloat16)
    grad_down = jnp.einsum("tf,td->fd", hidden, upstream, preferred_element_type=jnp.float32)
    grad_hidden = jnp.einsum("td,fd->tf", upstream, down_mat, preferred_element_type=jnp.float32)
    grad_pre = gelu_back(grad_hidden)[0].astype(jnp.bfloat16)
    grad_up = jnp.einsum("td,tf->df", normed_two, grad_pre, preferred_element_type=jnp.float32)
    grad_normed_two = lax.psum(
        jnp.einsum("tf,df->td", grad_pre, up_mat, preferred_element_type=jnp.float32), "tp"
    )
    grad_middle_norm, grad_gain_two, grad_bias_two = norm_two_back(grad_normed_two)
    grad_middle = upstream.astype(jnp.float32) + grad_middle_norm
    grad_attn = grad_middle.astype(jnp.bfloat16)
    grad_outmat = jnp.einsum("tc,td->cd", context, grad_attn, preferred_element_type=jnp.float32)
    grad_context = (
        jnp.einsum("td,cd->tc", grad_attn, out_mat, preferred_element_type=jnp.float32)
        .astype(jnp.bfloat16)
        .reshape(split_shape)
    )
    probs_again = jnp.exp(masked_scores(query_rows, key_rows, same_item, score_scale) - log_total)
    grad_values = jnp.einsum(
        "hts,thd->shd",
        probs_again.astype(jnp.bfloat16),
        grad_context,
        preferred_element_type=jnp.float32,
    )
    grad_probs = jnp.einsum(
        "thd,shd->hts", grad_context, value_rows, preferred_element_type=jnp.float32
    )
    inner_sum = jnp.sum(grad_probs * probs_again, axis=-1, keepdims=True)
    grad_scores = (probs_again * (grad_probs - inner_sum)).astype(jnp.bfloat16)
    grad_query = (
        jnp.einsum("hts,shd->thd", grad_scores, key_rows, preferred_element_type=jnp.float32)
        * score_scale
    )
    grad_key = (
        jnp.einsum("hts,thd->shd", grad_scores, query_rows, preferred_element_type=jnp.float32)
        * score_scale
    )
    grad_triple = (
        jnp.stack([grad_query, grad_key, grad_values])
        .reshape(3, tokens_here, local_width)
        .astype(jnp.bfloat16)
    )
    grad_qkv = jnp.einsum("td,jte->dje", normed, grad_triple, preferred_element_type=jnp.float32)
    grad_normed = lax.psum(
        jnp.einsum("jte,dje->td", grad_triple, qkv_mat, preferred_element_type=jnp.float32).astype(
            jnp.bfloat16
        ),
        "tp",
    ).astype(jnp.float32)
    grad_stream_norm, grad_gain_one, grad_bias_one = norm_one_back(grad_normed)
    grad_input = grad_middle + grad_stream_norm
    grad_norms = jnp.stack([grad_gain_one, grad_bias_one, grad_gain_two, grad_bias_two])
    return (block_out, grad_input, (grad_qkv, grad_outmat, grad_up, grad_down, grad_norms))


def local(
    inputs,
    cotangent,
    item_ids,
    timestep,
    qkv_weight,
    out_weight,
    up_weight,
    down_weight,
    norm_params,
    qkv_first,
    out_first,
    up_first,
    down_first,
    norm_first,
    qkv_second,
    out_second,
    up_second,
    down_second,
    norm_second,
):
    micro_count = inputs.shape[0]
    embeds = time_embed(timestep[:, 0], inputs.shape[2])
    qkv_low = qkv_weight.astype(jnp.bfloat16)
    out_low = out_weight.astype(jnp.bfloat16)
    up_low = up_weight.astype(jnp.bfloat16)
    down_low = down_weight.astype(jnp.bfloat16)
    norm_low = norm_params.astype(jnp.bfloat16)
    block_list = []
    input_list = []
    for number in range(micro_count):
        gathered = (
            lax.all_gather(qkv_low, "dp", axis=0, tiled=True),
            lax.all_gather(out_low, "dp", axis=1, tiled=True),
            lax.all_gather(up_low, "dp", axis=0, tiled=True),
            lax.all_gather(down_low, "dp", axis=1, tiled=True),
            lax.all_gather(norm_low, "dp", axis=1, tiled=True),
        )
        block_out, grad_input, grad_list = one_micro(
            gathered, inputs[number], cotangent[number], item_ids[number], embeds[number]
        )
        owned_grads = (
            lax.psum_scatter(grad_list[0], "dp", scatter_dimension=0, tiled=True),
            lax.psum_scatter(grad_list[1], "dp", scatter_dimension=1, tiled=True),
            lax.psum_scatter(grad_list[2], "dp", scatter_dimension=0, tiled=True),
            lax.psum_scatter(grad_list[3], "dp", scatter_dimension=1, tiled=True),
            lax.psum_scatter(grad_list[4], "dp", scatter_dimension=1, tiled=True),
        )
        if number == 0:
            totals = tuple(owned_grads)
        else:
            totals = tuple((left + right for left, right in zip(totals, owned_grads)))
        block_list.append(block_out)
        input_list.append(grad_input)
    own_squares = jnp.sum(totals[0] * totals[0]) + jnp.sum(totals[1] * totals[1])
    own_squares = own_squares + jnp.sum(totals[2] * totals[2]) + jnp.sum(totals[3] * totals[3])
    norm_squares = jnp.sum(totals[4] * totals[4])
    own_squares = own_squares + jnp.where(
        lax.axis_index("tp") == 0, norm_squares, jnp.zeros_like(norm_squares)
    )
    grad_norm = jnp.sqrt(lax.psum(own_squares, ("dp", "tp")))
    factor = jnp.minimum(1.0, clip_limit / (grad_norm + 1e-06))
    weights = (qkv_weight, out_weight, up_weight, down_weight, norm_params)
    firsts = (qkv_first, out_first, up_first, down_first, norm_first)
    seconds = (qkv_second, out_second, up_second, down_second, norm_second)
    result = [
        adam_step(weights[index], totals[index] * factor, firsts[index], seconds[index])
        for index in range(5)
    ]
    return (
        jnp.stack(block_list),
        jnp.stack(input_list),
        grad_norm,
        result[0][0],
        result[0][1],
        result[0][2],
        result[1][0],
        result[1][1],
        result[1][2],
        result[2][0],
        result[2][1],
        result[2][2],
        result[3][0],
        result[3][1],
        result[3][2],
        result[4][0],
        result[4][1],
        result[4][2],
    )


def solution(mesh):
    n_dp, n_tp = mesh.shape["dp"], mesh.shape["tp"]

    def step(*args):
        micro, tok, width = args[0].shape
        own_rows, _, local_width = args[4].shape
        fits = n_tp == 4 and n_dp == 8 and micro == 2 and tok == 512 and own_rows == 96
        if fits and local_width == 3 * HEAD_DIM and width % 256 == 0 and args[6].shape[1] % 256 == 0:
            return fast_local(n_dp, n_tp, *args)
        return local(*args)

    return jax.shard_map(
        step,
        mesh=mesh,
        in_specs=(
            P(None, "dp", None),
            P(None, "dp", None),
            P(None, "dp"),
            P(None, "dp"),
            P("dp", None, "tp"),
            P("tp", "dp"),
            P("dp", "tp"),
            P("tp", "dp"),
            P(None, "dp"),
            P("dp", None, "tp"),
            P("tp", "dp"),
            P("dp", "tp"),
            P("tp", "dp"),
            P(None, "dp"),
            P("dp", None, "tp"),
            P("tp", "dp"),
            P("dp", "tp"),
            P("tp", "dp"),
            P(None, "dp"),
        ),
        out_specs=(
            P(None, "dp", None),
            P(None, "dp", None),
            P(),
            P("dp", None, "tp"),
            P("dp", None, "tp"),
            P("dp", None, "tp"),
            P("tp", "dp"),
            P("tp", "dp"),
            P("tp", "dp"),
            P("dp", "tp"),
            P("dp", "tp"),
            P("dp", "tp"),
            P("tp", "dp"),
            P("tp", "dp"),
            P("tp", "dp"),
            P(None, "dp"),
            P(None, "dp"),
            P(None, "dp"),
        ),
        check_vma=False,
    )
```

```python
from functools import partial
import math

import jax
import jax.numpy as jnp
from jax import lax
from jax.experimental import pallas as pl
from jax.experimental.pallas import tpu as pltpu
from jax.sharding import PartitionSpec as P

HEAD_DIM = 64
STEP = 10

norm_eps = 1e-05
clip_limit = 1.0
learn_rate = 0.02
beta_one = 0.9
beta_two = 0.999
adam_eps = 1e-08
weight_decay = 0.01

BF = jnp.bfloat16
F32 = jnp.float32
MESH = pl.DeviceIdType.MESH


def time_embed(step_values, model_width):
    half_width = model_width // 2
    frequency = jnp.exp(
        jnp.arange(half_width, dtype=jnp.float32) * (-math.log(10000.0) / half_width)
    )
    angles = step_values.astype(jnp.float32)[..., None] * frequency
    return jnp.concatenate([jnp.sin(angles), jnp.cos(angles)], axis=-1)


def adam_step(weight, gradient, first_old, second_old):
    first_new = beta_one * first_old + (1.0 - beta_one) * gradient
    second_new = beta_two * second_old + (1.0 - beta_two) * gradient * gradient
    moment_one = first_new / (1.0 - beta_one**STEP)
    moment_two = second_new / (1.0 - beta_two**STEP)
    weight_new = weight - learn_rate * (
        moment_one / (jnp.sqrt(moment_two) + adam_eps) + weight_decay * weight
    )
    return (weight_new, first_new, second_new)


def mm(a, b, ca, cb):
    return lax.dot_general(a, b, (((ca,), (cb,)), ((), ())), preferred_element_type=F32)


def fold(v):
    cut = v.shape[-2] // 2
    low = jnp.concatenate([v[..., :cut, 128:], v[..., cut:, 128:]], axis=-1)
    return jnp.concatenate([v[..., :128], low], axis=-2)


def unfold(p):
    rows = 2 * p.shape[-2] // 3
    low = p[..., rows:, :]
    right = jnp.concatenate([low[..., :64], low[..., 64:]], axis=-2)
    return jnp.concatenate([p[..., :rows, :], right], axis=-1)


def layer_kernel(
    dims,
    x_in, cot_in, ids_ref, step_ref, wqkv_ref, wout_ref, wup_ref, wdown_ref, wnorm_ref,
    bo_ref, ig_ref, ga_ref, go_ref, gb_ref, gn_ref, gs_ref,
    x_ref, cot_ref, emb, lc, npin, ga, go, gb, gn, gs,
    wag, wqkv, woall, wo4, wb, npg, npt,
    normed, qkv, probs, ctx, ctxp, ctxr, n2, hid, dpre, mid, dmid, bo_own, dattn, dqkv,
    csend, crecv, own, ysend, yrecv, bsend, brecv, bown, bysend, byrecv,
    gfa, gfo, gfb, rax_s, rax_r, raz_s, raz_r, rbx_s, rbx_r, rbz_s, rbz_r,
    nacc, ncore, nsum, sqd, sqt,
    az_s, az_r, ax_s, ax_r, np_s, np_r, oy_s, oy_r, oc_s, oc_r, cx_s, cx_r,
    c_s, c_r, y_s, y_r, g_s, g_r, o_l, in_l,
    rx_s, rx_r, rz_s, rz_r, nc_s, nc_r, nd_s, nd_r, qd_s, qd_r, qt_s, qt_r,
):
    micro, tok, width, n_dp, n_tp, heads = dims
    n_z = n_dp // 2
    half = tok // 2
    own_rows = width // n_dp
    fold_rows = 3 * own_rows // 2
    local = heads * HEAD_DIM
    scale = 1.0 / math.sqrt(HEAD_DIM)

    dp = lax.axis_index("dp")
    tp = lax.axis_index("tp")
    z, xx = lax.div(dp, 2), lax.rem(dp, 2)
    yy, cc = lax.div(tp, 2), lax.rem(tp, 2)
    across_tp = 2 * (1 - yy) + cc
    x_peer = (2 * z + 1 - xx, tp)
    c_peer = (dp, 2 * yy + 1 - cc)
    y_peer = (dp, across_tp)
    d_peer = (dp, 2 * (1 - yy) + 1 - cc)

    far = lax.div(z, 2)
    column = (z + 1 - 2 * lax.rem(z, 2), 2 - far, 3 - 3 * far)
    inner = (z > 0) & (z < n_z - 1)
    near_peer = (2 * column[0] + xx, tp)
    mid_peer = (2 * column[1] + xx, tp)
    flip = 1 - xx

    def dp_of(k):
        return lax.rem(dp + k, n_dp)

    def tp_of(k):
        return lax.rem(tp + k, n_tp)

    sent, sent_inner, puts = [], [], []

    def put(i, held, there):
        item = pltpu.make_async_copy(held, there, in_l.at[2 + i])
        item.start()
        puts.append(item)

    def copy(src, dst, s_sem, r_sem, peer):
        return pltpu.make_async_remote_copy(
            src_ref=src, dst_ref=dst, send_sem=s_sem, recv_sem=r_sem, device_id=peer, device_id_type=MESH
        )

    def send(src, dst, s_sem, r_sem, peer):
        item = copy(src, dst, s_sem, r_sem, peer)
        item.start()
        sent.append(item)

    def send_inner(src, dst, s_sem, r_sem, peer):
        item = copy(src, dst, s_sem, r_sem, peer)
        pl.when(inner)(item.start)
        sent_inner.append(item)

    def arrive(dst, s_sem, r_sem, peer):
        copy(dst, dst, s_sem, r_sem, peer).wait_recv()

    barrier = pltpu.get_barrier_semaphore()
    for k in range(1, n_dp):
        pl.semaphore_signal(barrier, inc=1, device_id=(dp_of(k), tp), device_id_type=MESH)
    for k in range(1, n_tp):
        pl.semaphore_signal(barrier, inc=1, device_id=(dp, tp_of(k)), device_id_type=MESH)
    loads = [
        pltpu.make_async_copy(x_in, x_ref, in_l.at[0]),
        pltpu.make_async_copy(cot_in, cot_ref, in_l.at[1]),
    ]
    for load in loads:
        load.start()
    for i in range(3):
        wag[dp, :, 128 * i : 128 * (i + 1)] = fold(wqkv_ref[i]).astype(BF)
    wag[dp, :, 384:512] = fold(wout_ref[...].T).astype(BF)
    wb[0, dp] = wup_ref[...].astype(BF)
    wb[1, dp] = wdown_ref[...].astype(BF)
    npin[...] = jnp.zeros_like(npin)
    npin[:4, :own_rows] = wnorm_ref[...].astype(BF)
    place = lax.broadcasted_iota(jnp.int32, (1, width // 2), 1).astype(F32)
    rates = jnp.exp(place * (-math.log(10000.0) / (width // 2)))
    for m in range(micro):
        angles = step_ref[:, m : m + 1].astype(F32) * rates
        emb[m : m + 1, : width // 2] = jnp.sin(angles)
        emb[m : m + 1, width // 2 :] = jnp.cos(angles)
    labels = ids_ref[...].astype(F32)
    columns = jnp.concatenate([labels] * (8 // micro), axis=0).T
    for m in range(micro):
        lc[m] = columns[:, m : m + 1]

    pl.semaphore_wait(barrier, n_dp + n_tp - 2)

    def rows_of(j):
        return pl.ds(pl.multiple_of(j * own_rows, own_rows), own_rows)

    def half_rows(h):
        return pl.ds(pl.multiple_of(h * half, half), half)

    mine = half_rows(cc)
    other = half_rows(1 - cc)

    def ag_at(g, j):
        if g < 2:
            return wag.at[j, :, pl.ds(384 * g, 384 - 256 * g)]
        return wb.at[g - 2, j]

    def ag_column(g):
        block = ag_at(g, dp)
        send(block, block, az_s.at[g, 0], az_r.at[g, 0], near_peer)
        send_inner(block, block, az_s.at[g, 1], az_r.at[g, 1], mid_peer)

    def ag_side(g):
        send(ag_at(g, dp), ag_at(g, dp), ax_s.at[g, 3], ax_r.at[g, z], x_peer)

    def ag_pass(g, *which):
        for i in which:
            s = column[i]
            block = ag_at(g, 2 * s + xx)
            arrive(block, az_s.at[g, 0], az_r.at[g, i], near_peer)
            send_inner(block, block, az_s.at[g, 2 + i], az_r.at[g, i or 2], near_peer if i else mid_peer)
            send(block, block, ax_s.at[g, i], ax_r.at[g, s], x_peer)

    def ag_done(g, *which):
        for i in which or range(4):
            s = (*column, z)[i]
            arrive(ag_at(g, 2 * s + flip), ax_s.at[g, i], ax_r.at[g, s], x_peer)

    def o_send(col, which):
        for i in which:
            j = 2 * (*column, z)[i] + col
            part = ag_at(1, j)
            send(part, woall.at[tp, j], oy_s.at[j], oy_r.at[j], y_peer)

    def o_core():
        woall[tp] = wag[:, :, 384:512]
        send(woall.at[tp], woall.at[tp], oc_s.at[0], oc_r.at[0], c_peer)

    def o_across():
        for j in range(n_dp):
            arrive(woall.at[across_tp, j], oy_s.at[j], oy_r.at[j], y_peer)
        send(woall.at[across_tp], woall.at[across_tp], oc_s.at[1], oc_r.at[1], c_peer)

    def o_done():
        arrive(woall.at[2 * yy + 1 - cc], oc_s.at[0], oc_r.at[0], c_peer)
        arrive(woall.at[2 * (1 - yy) + 1 - cc], oc_s.at[1], oc_r.at[1], c_peer)
        for t in range(n_tp):
            wo4[t] = unfold(woall[t]).reshape(width, local)

    def ar_refs(kind, m):
        if kind < 2:
            return csend.at[kind, m], crecv.at[kind, m], own.at[m], ysend.at[kind, m], yrecv.at[kind, m]
        return [r.at[kind - 2, m] for r in (bsend, brecv, bown, bysend, byrecv)]

    def ar_start(kind, m, part):
        here, there, keep, _, _ = ar_refs(kind, m)
        here[...] = part(other).astype(BF)
        send(here, there, c_s.at[kind, m], c_r.at[kind, m], c_peer)
        keep[...] = part(mine)

    def ar_cross(kind, m):
        _, there, keep, here, across = ar_refs(kind, m)
        arrive(there, c_s.at[kind, m], c_r.at[kind, m], c_peer)
        here[...] = (keep[...] + there[...].astype(F32)).astype(BF)
        send(here, across, y_s.at[kind, m], y_r.at[kind, m], y_peer)

    def ar_total(kind, m):
        _, _, _, here, across = ar_refs(kind, m)
        arrive(across, y_s.at[kind, m], y_r.at[kind, m], y_peer)
        return here[...].astype(F32) + across[...].astype(F32)

    def share(i, m, ref):
        send(ref.at[m, mine], ref.at[m, mine], g_s.at[i, m], g_r.at[i, m], c_peer)

    def shared(i, m, ref):
        arrive(ref.at[m, other], g_s.at[i, m], g_r.at[i, m], c_peer)

    def centred(v):
        c0 = v - jnp.mean(v, axis=-1, keepdims=True)
        return c0, lax.rsqrt(jnp.mean(c0 * c0, axis=-1, keepdims=True) + norm_eps)

    def norm_back(grad, hat, inv, gain):
        dhat = grad * gain
        return inv * (
            dhat
            - jnp.mean(dhat, axis=-1, keepdims=True)
            - hat * jnp.mean(dhat * hat, axis=-1, keepdims=True)
        )

    def open_norms():
        block = lax.broadcasted_iota(jnp.int32, (n_dp, 128, width), 0)
        row = lax.broadcasted_iota(jnp.int32, (n_dp, 128, width), 1)
        col = lax.broadcasted_iota(jnp.int32, (n_dp, 128, width), 2)
        place = ((col == block * own_rows + row) & (row < own_rows)).astype(F32).astype(BF)
        rows = npg[0]
        total = mm(rows, place[0], 1, 0)
        for j in range(1, n_dp):
            total = total + mm(npg[j], place[j], 1, 0)
        npt[...] = total

    def gain_row(i):
        return 1.0 + npt[pl.ds(i, 1), :]

    def bias_row(i):
        return npt[pl.ds(i, 1), :]

    def stream_of(m, rows):
        return x_ref[m, rows, :].astype(F32) + emb[pl.ds(m, 1), :]

    def first_norm(m):
        c0, inv = centred(stream_of(m, pl.ds(0, tok)))
        normed[m] = (c0 * inv * gain_row(0) + bias_row(1)).astype(BF)

    def open_qkv():
        for i in range(3):
            wqkv[i] = unfold(wag[:, :, 128 * i : 128 * (i + 1)]).reshape(width, local)

    def project(m):
        for i in range(3):
            qkv[i, m] = mm(normed[m], wqkv[i], 1, 0).astype(BF)

    lane = lax.broadcasted_iota(jnp.int32, (1, local), 1)

    def head_mask(h, value):
        here = (lane >= h * HEAD_DIM) & (lane < (h + 1) * HEAD_DIM)
        return jnp.where(here, value, 0.0).astype(BF)

    def attend(m, *between):
        same = lc[m] == ids_ref[pl.ds(m, 1), :].astype(F32)
        total = None
        for h in range(heads):
            s = mm(qkv[0, m] * head_mask(h, scale), qkv[1, m], 1, 1)
            s = jnp.where(same, s, -1e30)
            e = jnp.exp(s - jnp.max(s, axis=-1, keepdims=True))
            p = e * (1.0 / jnp.sum(e, axis=-1, keepdims=True))
            probs[m * heads + h] = p
            part = mm(p.astype(BF), qkv[2, m] * head_mask(h, 1.0), 1, 0)
            total = part if total is None else total + part
            for work in between[h] if h < len(between) else ():
                work()
        ctx[m] = total.astype(BF)
        for i in range(2):
            ctxp[m, i] = fold(total[i * half : (i + 1) * half]).astype(BF)
        send(ctxp.at[m, cc], ctxr.at[m, tp], cx_s.at[m, 1], cx_r.at[m, 1], y_peer)
        send(ctxp.at[m, 1 - cc], ctxr.at[m, tp], cx_s.at[m, 2], cx_r.at[m, 2], d_peer)
        send(ctxp.at[m, 1 - cc], ctxr.at[m, tp], cx_s.at[m, 0], cx_r.at[m, 0], c_peer)
        ctxr[m, tp] = ctxp[m, cc]

    def second_norm(m):
        arrive(ctxr.at[m, 2 * yy + 1 - cc], cx_s.at[m, 0], cx_r.at[m, 0], c_peer)
        arrive(ctxr.at[m, across_tp], cx_s.at[m, 1], cx_r.at[m, 1], y_peer)
        arrive(ctxr.at[m, 2 * (1 - yy) + 1 - cc], cx_s.at[m, 2], cx_r.at[m, 2], d_peer)
        middle = stream_of(m, mine)
        for t in range(n_tp):
            middle = middle + mm(unfold(ctxr[m, t]), wo4[t], 1, 1)
        mid[m] = middle
        c0, inv = centred(middle)
        n2[m, mine, :] = (c0 * inv * gain_row(2) + bias_row(3)).astype(BF)
        share(0, m, n2)

    def wide(g):
        return wb[g].reshape(width, wb.shape[-1])

    def feed(m):
        shared(0, m, n2)
        pre = mm(n2[m], wide(0), 1, 0)
        cdf = 0.5 * (1.0 + lax.erf(pre * math.sqrt(0.5)))
        hid[m] = (pre * cdf).astype(BF)
        slope = cdf + pre * (jnp.exp(-0.5 * pre * pre) * (1.0 / math.sqrt(2.0 * math.pi)))
        if m == 0:
            gfb[0, :tok, :] = slope
        else:
            dmid[...] = slope.reshape(2, half, slope.shape[-1])

    def dn2_part(m):
        def part(rows):
            at = 1 - cc if rows is other else cc
            slope = gfb[0, rows, :] if m == 0 else dmid[at]
            grad = (mm(cot_ref[m, rows, :], wide(1), 1, 0) * slope).astype(BF)
            dpre[m, rows, :] = grad
            return mm(grad, wide(0), 1, 1)

        return part

    def branch_part(m, side):
        def part(rows):
            blocks = wb[1, pl.ds(side * n_z, n_z)]
            return mm(hid[m, rows, :], blocks.reshape(width // 2, blocks.shape[-1]), 1, 1)

        return part

    def col_sum(v):
        return jnp.sum(v, axis=0, keepdims=True)

    def second_back(m):
        grad = ar_total(0, m)
        c0, inv = centred(mid[m])
        hat = c0 * inv
        nacc[m, pl.ds(0, 1), :] = col_sum(grad * hat)
        nacc[m, pl.ds(1, 1), :] = col_sum(grad)
        grad_middle = cot_ref[m, mine, :].astype(F32) + norm_back(grad, hat, inv, gain_row(2))
        dmid[m] = grad_middle
        dattn[m, mine, :] = grad_middle.astype(BF)
        share(1, m, dattn)

    def finish_block(m):
        near, away = ar_total(2, m), ar_total(3, m)
        left = jnp.where(far == 0, near, away)
        right = jnp.where(far == 0, away, near)
        bo_own[m] = (mid[m] + jnp.concatenate([left, right], axis=1)).astype(BF)
        send(bo_own.at[m], bo_ref.at[m, mine], g_s.at[2, m], g_r.at[2, m], c_peer)
        pltpu.make_async_copy(bo_own.at[m], bo_ref.at[m, mine], o_l.at[0, m]).start()

    def attend_back(m, *between):
        shared(1, m, dattn)
        wo_own = wo4[tp]
        dctx = mm(dattn[m], wo_own, 1, 0).astype(BF)
        dq = dk = dv = None
        for h in range(heads):
            dch = dctx * head_mask(h, 1.0)
            p = probs[m * heads + h]
            dp_ = mm(dch, qkv[2, m], 1, 1)
            inner = jnp.sum(dp_ * p, axis=-1, keepdims=True)
            ds = (p * (dp_ - inner)).astype(BF)
            mask = head_mask(h, scale)
            a = mm(ds, qkv[1, m] * mask, 1, 0)
            b = mm(ds, qkv[0, m] * mask, 0, 0)
            c = mm(p.astype(BF), dch, 0, 0)
            dq = a if dq is None else dq + a
            dk = b if dk is None else dk + b
            dv = c if dv is None else dv + c
            for work in between[h] if h < len(between) else ():
                work()
        dqkv[0, m] = dq.astype(BF)
        dqkv[1, m] = dk.astype(BF)
        dqkv[2, m] = dv.astype(BF)

    def dn1_part(m):
        def part(rows):
            total = mm(dqkv[0, m, rows, :], wqkv[0], 1, 1)
            for i in range(1, 3):
                total = total + mm(dqkv[i, m, rows, :], wqkv[i], 1, 1)
            return total

        return part

    def first_back(m):
        grad = ar_total(1, m)
        c0, inv = centred(stream_of(m, mine))
        hat = c0 * inv
        nacc[m, pl.ds(2, 1), :] = col_sum(grad * hat)
        nacc[m, pl.ds(3, 1), :] = col_sum(grad)
        dmid[m] = dmid[m] + norm_back(grad, hat, inv, gain_row(0))
        send(dmid.at[m], ig_ref.at[m, mine], g_s.at[3, m], g_r.at[3, m], c_peer)
        pltpu.make_async_copy(dmid.at[m], ig_ref.at[m, mine], o_l.at[1, m]).start()

    def gf(g, at, col):
        if g == 0:
            return gfa.at[2 * at + col]
        return gfo.at[2 * at + col] if g == 1 else gfb.at[g - 2, rows_of(2 * at + col)]

    def rs_slots(g, at):
        if g < 2:
            lanes = pl.ds(384 * g, 384 - 256 * g)
            return [r.at[at, :, lanes] for r in (rax_s, rax_r, raz_s, raz_r)]
        return [r.at[g - 2, at] for r in (rbx_s, rbx_r, rbz_s, rbz_r)]

    def flat(ref):
        return ref[...].reshape(micro * tok, ref.shape[-1])

    def rs_wide(g, left, right):
        gfb[g - 2] = mm(flat(left), flat(right), 0, 0)

    def folded(left, right):
        return fold(mm(left, right, 0, 0).reshape(n_dp, own_rows, local))

    def rs_out():
        gfo[...] = folded(flat(dattn), flat(ctx))

    def rs_qkv(m):
        for i in range(3):
            lanes = slice(128 * i, 128 * (i + 1))
            grad = folded(normed[m], dqkv[i, m])
            gfa[:, :, lanes] = grad if m == 0 else gfa[:, :, lanes] + grad

    def rs_start(g):
        for i in (2, 1, 0, 3):
            at = (*column, z)[i]
            here, there, _, _ = rs_slots(g, at)
            here[...] = gf(g, at, flip)[...].astype(BF)
            send(here, there, rx_s.at[g, i], rx_r.at[g, at], x_peer)

    def rs_sum(g, i):
        at = (*column, z)[i]
        there = rs_slots(g, at)[1]
        arrive(there, rx_s.at[g, i], rx_r.at[g, at], x_peer)
        return gf(g, at, xx)[...] + there[...].astype(F32)

    def rs_pass(g, *which):
        for i in which:
            at = column[i]
            here = rs_slots(g, at)[2]
            here[...] = rs_sum(g, i).astype(BF)
            send(here, rs_slots(g, z)[3], rz_s.at[g, i], rz_r.at[g, z], (2 * at + xx, tp))

    def rs_finish(g):
        total = rs_sum(g, 3)
        for i in range(3):
            s = column[i]
            there = rs_slots(g, s)[3]
            arrive(there, rz_s.at[g, i], rz_r.at[g, s], (2 * s + xx, tp))
            total = total + there[...].astype(F32)
        if g == 0:
            for i in range(3):
                ga[i] = unfold(total[:, 128 * i : 128 * (i + 1)])
            put(0, ga, ga_ref)
        elif g == 1:
            go[...] = unfold(total).T
            put(1, go, go_ref)
        else:
            gb[g - 2] = total
            put(g, gb.at[g - 2], gb_ref.at[g - 2])
        return jnp.sum(col_sum(total * total), axis=1, keepdims=True)

    def norm_start(e):
        both = nacc[0, pl.ds(2 * e, 2), :]
        for m in range(1, micro):
            both = both + nacc[m, pl.ds(2 * e, 2), :]
        ncore[e, 0] = both
        send(ncore.at[e, 0], ncore.at[e, 1], nc_s.at[e], nc_r.at[e], c_peer)

    def norm_cross(e):
        arrive(ncore.at[e, 1], nc_s.at[e], nc_r.at[e], c_peer)
        nsum[e, dp] = ncore[e, 0] + ncore[e, 1]
        for k in range(1, n_dp):
            send(nsum.at[e, dp], nsum.at[e, dp], nd_s.at[e, k], nd_r.at[e, k], (dp_of(k), tp))

    def norm_finish(e):
        for k in range(1, n_dp):
            j = lax.rem(dp + n_dp - k, n_dp)
            arrive(nsum.at[e, j], nd_s.at[e, k], nd_r.at[e, k], (dp_of(k), tp))
        total = nsum[e, 0]
        for j in range(1, n_dp):
            total = total + nsum[e, j]
        mine_only = jnp.zeros((2, own_rows), F32)
        for j in range(n_dp):
            mine_only = jnp.where(dp == j, total[:, j * own_rows : (j + 1) * own_rows], mine_only)
        gn[pl.ds(2 - 2 * e, 2), :] = mine_only
        return jnp.sum(col_sum(total * total), axis=1, keepdims=True)

    ag_side(0)
    ag_column(0)
    ag_column(1)
    ag_side(1)
    npg[dp] = npin[...]
    for k in range(1, n_dp):
        send(npin, npg.at[dp], np_s.at[k], np_r.at[k], (dp_of(k), tp))
    o_send(xx, (3,))
    ag_pass(0, 0)
    for k in range(1, n_dp):
        arrive(npg.at[lax.rem(dp + n_dp - k, n_dp)], np_s.at[k], np_r.at[k], (dp_of(k), tp))
    open_norms()
    loads[0].wait()
    ag_pass(0, 1)
    first_norm(0)
    ag_pass(0, 2)
    ag_pass(1, 0)
    ag_column(2)
    ag_side(2)
    first_norm(1)
    ag_pass(1, 1, 2)
    ag_done(0)
    open_qkv()
    project(0)
    ag_column(3)
    o_send(xx, (0, 1, 2))
    project(1)
    ag_pass(2, 0)

    def o_rest():
        ag_done(1)
        o_send(flip, (0, 1, 2, 3))
        o_core()

    attend(0, (o_rest,))
    ag_pass(2, 1, 2)
    ag_side(3)
    ag_pass(3, 0)
    attend(1)
    ag_pass(3, 1)
    o_across()
    o_done()
    second_norm(0)
    second_norm(1)
    ag_done(2)
    feed(0)
    ag_done(3, 0, 3)
    ar_start(2, 0, branch_part(0, far))
    ag_pass(3, 2)
    feed(1)
    ar_cross(2, 0)
    ar_start(2, 1, branch_part(1, far))
    loads[1].wait()
    rs_wide(3, cot_ref, hid)
    ar_cross(2, 1)
    ag_done(3, 1, 2)
    ar_start(0, 0, dn2_part(0))
    rs_start(3)
    ar_cross(0, 0)
    ar_start(0, 1, dn2_part(1))
    rs_wide(2, n2, dpre)
    ar_cross(0, 1)
    rs_start(2)
    rs_pass(3, 2, 1)
    second_back(0)
    rs_pass(3, 0)
    attend_back(0)
    ar_start(1, 0, dn1_part(0))
    rs_pass(2, 2)
    ar_cross(1, 0)
    rs_qkv(0)
    second_back(1)
    rs_pass(2, 1)
    norm_start(0)
    attend_back(1, (rs_out, partial(rs_start, 1), partial(rs_pass, 2, 0)), (partial(norm_cross, 0),))
    rs_qkv(1)
    rs_start(0)
    ar_start(1, 1, dn1_part(1))
    rs_pass(1, 2, 1, 0)
    ar_cross(1, 1)
    ar_start(3, 0, branch_part(0, 1 - far))
    ar_start(3, 1, branch_part(1, 1 - far))
    ar_cross(3, 0)
    ar_cross(3, 1)
    first_back(0)
    rs_pass(0, 2, 1)
    squares = rs_finish(3) + rs_finish(2)
    squares = squares + rs_finish(1)
    rs_pass(0, 0)
    first_back(1)
    norm_start(1)
    norm_cross(1)
    squares = squares + rs_finish(0)
    sqd[dp] = jnp.broadcast_to(squares, (8, 128))
    for k in range(1, n_dp):
        send(sqd.at[dp], sqd.at[dp], qd_s.at[k], qd_r.at[k], (dp_of(k), tp))
    finish_block(0)
    extra = norm_finish(0) + norm_finish(1)
    for k in range(1, n_dp):
        j = lax.rem(dp + n_dp - k, n_dp)
        arrive(sqd.at[j], qd_s.at[k], qd_r.at[k], (dp_of(k), tp))
    mesh_row = sqd[0]
    for j in range(1, n_dp):
        mesh_row = mesh_row + sqd[j]
    sqt[tp] = mesh_row
    for k in range(1, n_tp):
        send(sqt.at[tp], sqt.at[tp], qt_s.at[k], qt_r.at[k], (dp, tp_of(k)))
    finish_block(1)
    for k in range(1, n_tp):
        j = lax.rem(tp + n_tp - k, n_tp)
        arrive(sqt.at[j], qt_s.at[k], qt_r.at[k], (dp, tp_of(k)))
    everything = sqt[0]
    for j in range(1, n_tp):
        everything = everything + sqt[j]
    gs[...] = jnp.sqrt(everything + extra)
    put(4, gn, gn_ref)
    put(5, gs, gs_ref)
    for m in range(micro):
        arrive(bo_ref.at[m, other], g_s.at[2, m], g_r.at[2, m], c_peer)
        arrive(ig_ref.at[m, other], g_s.at[3, m], g_r.at[3, m], c_peer)
        pltpu.make_async_copy(bo_own.at[m], bo_ref.at[m, mine], o_l.at[0, m]).wait()
        pltpu.make_async_copy(dmid.at[m], ig_ref.at[m, mine], o_l.at[1, m]).wait()
    for item in puts:
        item.wait()
    for item in sent:
        item.wait_send()
    for item in sent_inner:
        pl.when(inner)(item.wait_send)


def layer_call(n_dp, n_tp, inputs, cotangent, item_ids, timestep, qkv, out, up, down, norms):
    micro, tok, width = inputs.shape
    own_rows, ff = up.shape
    local = qkv.shape[2]
    fold_rows = 3 * own_rows // 2
    heads = local // HEAD_DIM
    half = tok // 2
    fold_half = 3 * half // 2
    dims = (micro, tok, width, n_dp, n_tp, heads)
    V = pltpu.VMEM
    DMA = pltpu.SemaphoreType.DMA
    n_z = n_dp // 2
    scratch = [
        V((micro, tok, width), BF), V((micro, tok, width), BF), V((micro, width), F32), V((micro, tok, 1), F32), V((8, 128), BF),
        V((3, own_rows, local), F32), V((local, own_rows), F32), V((2, own_rows, ff), F32), V((4, own_rows), F32), V((8, 128), F32),
        V((n_dp, fold_rows, 512), BF), V((3, width, local), BF), V((n_tp, n_dp, fold_rows, 128), BF),
        V((n_tp, width, local), BF), V((2, n_dp, own_rows, ff), BF), V((n_dp, 8, 128), BF), V((8, width), F32),
        V((micro, tok, width), BF), V((3, micro, tok, local), BF), V((micro * heads, tok, tok), F32),
        V((micro, tok, local), BF), V((micro, 2, fold_half, 128), BF), V((micro, n_tp, fold_half, 128), BF),
        V((micro, tok, width), BF), V((micro, tok, ff), BF), V((micro, tok, ff), BF),
        V((micro, half, width), F32), V((micro, half, width), F32), V((micro, half, width), BF),
        V((micro, tok, width), BF), V((3, micro, tok, local), BF),
        V((2, micro, half, width), BF), V((2, micro, half, width), BF), V((micro, half, width), F32),
        V((2, micro, half, width), BF), V((2, micro, half, width), BF),
        V((2, micro, half, width // 2), BF), V((2, micro, half, width // 2), BF), V((2, micro, half, width // 2), F32),
        V((2, micro, half, width // 2), BF), V((2, micro, half, width // 2), BF),
        V((n_dp, fold_rows, 384), F32), V((n_dp, fold_rows, 128), F32), V((2, width, ff), F32),
        V((n_z, fold_rows, 512), BF), V((n_z, fold_rows, 512), BF), V((n_z, fold_rows, 512), BF), V((n_z, fold_rows, 512), BF),
        V((2, n_z, own_rows, ff), BF), V((2, n_z, own_rows, ff), BF), V((2, n_z, own_rows, ff), BF), V((2, n_z, own_rows, ff), BF),
        V((micro, 8, width), F32), V((2, 2, 2, width), F32), V((2, n_dp, 2, width), F32),
        V((n_dp, 8, 128), F32), V((n_tp, 8, 128), F32),
        DMA((4, 5)), DMA((4, 3)), DMA((4, n_z)), DMA((4, n_z)), DMA((n_dp,)), DMA((n_dp,)), DMA((n_dp,)), DMA((n_dp,)), DMA((2,)), DMA((2,)),
        DMA((micro, 3)), DMA((micro, 3)),
        DMA((4, micro)), DMA((4, micro)), DMA((4, micro)), DMA((4, micro)), DMA((4, micro)), DMA((4, micro)),
        DMA((2, micro)), DMA((8,)),
        DMA((4, n_z)), DMA((4, n_z)), DMA((4, n_z)), DMA((4, n_z)), DMA((2,)), DMA((2,)), DMA((2, n_dp)), DMA((2, n_dp)),
        DMA((n_dp,)), DMA((n_dp,)), DMA((n_tp,)), DMA((n_tp,)),
    ]
    vm = pl.BlockSpec(memory_space=pltpu.VMEM)
    anywhere = pl.BlockSpec(memory_space=pl.ANY)
    S = jax.ShapeDtypeStruct
    return pl.pallas_call(
        partial(layer_kernel, dims),
        out_shape=(
            S((micro, tok, width), BF), S((micro, tok, width), F32),
            S((3, own_rows, local), F32), S((local, own_rows), F32), S((2, own_rows, ff), F32),
            S((4, own_rows), F32), S((8, 128), F32),
        ),
        in_specs=[anywhere] * 2 + [vm] * 7,
        out_specs=[anywhere] * 7,
        scratch_shapes=scratch,
        compiler_params=pltpu.CompilerParams(
            collective_id=0, has_side_effects=True, vmem_limit_bytes=63 << 20
        ),
        name="layer",
    )(inputs, cotangent, item_ids, timestep, qkv, out, up, down, norms)


def adam_kernel(*refs):
    bo_in, ig_in, gs_ref = refs[:3]
    olds = refs[7:22]
    bo_ref, ig_ref, norm_ref = refs[22:25]
    news = refs[25:40]
    loaded, stored = refs[40:55], refs[55:70]
    bo_held, ig_held, ga, go, gb, gn, in_sem, out_sem, move_sem, grad_sem = refs[70:]
    grads = (ga, go, gb.at[0], gb.at[1], gn)
    held_grads = (ga, go, gb, gn)
    gets = [pltpu.make_async_copy(refs[3 + i], held_grads[i], grad_sem.at[i]) for i in range(4)]
    got = (0, 1, 2, None, 3)
    takes, moves = [], []
    for n, (there, held, here) in enumerate(((ig_in, ig_held, ig_ref), (bo_in, bo_held, bo_ref))):
        takes.append(pltpu.make_async_copy(there, held, move_sem.at[0, n]))
        moves.append(pltpu.make_async_copy(held, here, move_sem.at[1, n]))
    loads = [pltpu.make_async_copy(olds[i], loaded[i], in_sem.at[i]) for i in range(15)]
    stores = [pltpu.make_async_copy(stored[i], news[i], out_sem.at[i]) for i in range(15)]
    for item in (gets[0], *loads[:3], *gets[1:]):
        item.start()
    for take in takes:
        take.start()
    for load in loads[3:]:
        load.start()
    grad_norm = gs_ref[pl.ds(0, 1), pl.ds(0, 1)]
    norm_ref[...] = grad_norm
    factor = jnp.minimum(1.0, clip_limit / (grad_norm + 1e-06))
    for p in range(5):
        if got[p] is not None:
            gets[got[p]].wait()
        for i in range(3):
            loads[3 * p + i].wait()
        weight, first, second = loaded[3 * p : 3 * p + 3]
        results = adam_step(weight[...], grads[p][...] * factor, first[...], second[...])
        for i in range(3):
            stored[3 * p + i][...] = results[i]
            stores[3 * p + i].start()
        if p == 0:
            for take, move in zip(takes, moves):
                take.wait()
                move.start()
    for store in stores:
        store.wait()
    for move in moves:
        move.wait()


def adam_call(block_out, grad_input, gs, grads, olds):
    vm = pl.BlockSpec(memory_space=pltpu.VMEM)
    anywhere = pl.BlockSpec(memory_space=pl.ANY)
    S = jax.ShapeDtypeStruct
    like = [S(o.shape, o.dtype) for o in olds]
    return pl.pallas_call(
        adam_kernel,
        out_shape=(
            S(block_out.shape, block_out.dtype), S(grad_input.shape, grad_input.dtype), S((1, 1), F32), *like
        ),
        in_specs=[anywhere] * 2 + [vm] + [anywhere] * 19,
        out_specs=(anywhere, anywhere, vm, *[anywhere] * 15),
        scratch_shapes=[pltpu.VMEM(o.shape, o.dtype) for o in olds] * 2
        + [pltpu.VMEM(block_out.shape, block_out.dtype), pltpu.VMEM(grad_input.shape, grad_input.dtype)]
        + [pltpu.VMEM(g.shape, g.dtype) for g in grads]
        + [pltpu.SemaphoreType.DMA((15,)), pltpu.SemaphoreType.DMA((15,)), pltpu.SemaphoreType.DMA((2, 2)), pltpu.SemaphoreType.DMA((4,))],
        compiler_params=pltpu.CompilerParams(vmem_limit_bytes=63 << 20),
        name="adam",
    )(block_out, grad_input, gs, *grads, *olds)


def fast_local(
    n_dp, n_tp,
    inputs, cotangent, item_ids, timestep, qkv_weight, out_weight, up_weight, down_weight, norm_params,
    qkv_first, out_first, up_first, down_first, norm_first,
    qkv_second, out_second, up_second, down_second, norm_second,
):
    def turned(qkv, out, up, down, norms):
        return (jnp.moveaxis(qkv, 1, 0), out, up, down.T, norms)

    weights = turned(qkv_weight, out_weight, up_weight, down_weight, norm_params)
    firsts = turned(qkv_first, out_first, up_first, down_first, norm_first)
    seconds = turned(qkv_second, out_second, up_second, down_second, norm_second)
    block_out, grad_input, ga, go, gb, gn, gs = layer_call(
        n_dp, n_tp, inputs, cotangent, item_ids, timestep.T, *weights
    )
    olds = [item for p in range(5) for item in (weights[p], firsts[p], seconds[p])]
    block_out, grad_input, grad_norm, *news = adam_call(block_out, grad_input, gs, (ga, go, gb, gn), olds)
    for i in range(3):
        news[i] = jnp.moveaxis(news[i], 0, 1)
        news[9 + i] = news[9 + i].T
    return (block_out, grad_input, grad_norm[0, 0], *news)


def layer_norm(values, gain_row, bias_row):
    centre = values - jnp.mean(values, axis=-1, keepdims=True)
    spread = jnp.mean(centre * centre, axis=-1, keepdims=True)
    return centre * lax.rsqrt(spread + norm_eps) * gain_row + bias_row


def masked_scores(query_rows, key_rows, same_item, score_scale):
    scores = (
        jnp.einsum("thd,shd->hts", query_rows, key_rows, preferred_element_type=jnp.float32)
        * score_scale
    )
    return jnp.where(same_item, scores, -1e30)


def one_micro(gathered, stream_in, upstream, labels, embed_row):
    qkv_mat, out_mat, up_mat, down_mat, norm_rows = gathered
    tokens_here = stream_in.shape[0]
    local_width = out_mat.shape[0]
    heads_here = local_width // HEAD_DIM
    score_scale = 1.0 / math.sqrt(HEAD_DIM)
    split_shape = (tokens_here, heads_here, HEAD_DIM)
    norm_gains = norm_rows.astype(jnp.float32)
    gain_one = 1.0 + norm_gains[0]
    gain_two = 1.0 + norm_gains[2]
    stream = stream_in.astype(jnp.float32) + embed_row[None, :]
    normed_f, norm_one_back = jax.vjp(layer_norm, stream, gain_one, norm_gains[1])
    normed = normed_f.astype(jnp.bfloat16)
    triple = jnp.einsum("td,dje->jte", normed, qkv_mat, preferred_element_type=jnp.float32).astype(
        jnp.bfloat16
    )
    query_rows = triple[0].reshape(split_shape)
    key_rows = triple[1].reshape(split_shape)
    value_rows = triple[2].reshape(split_shape)
    same_item = (labels[:, None] == labels[None, :])[None]
    scores = masked_scores(query_rows, key_rows, same_item, score_scale)
    row_top = jnp.max(scores, axis=-1, keepdims=True)
    exp_scores = jnp.exp(scores - row_top)
    row_total = jnp.sum(exp_scores, axis=-1, keepdims=True)
    probs_soft = exp_scores / row_total
    log_total = row_top + jnp.log(row_total)
    context = (
        jnp.einsum(
            "hts,shd->thd",
            probs_soft.astype(jnp.bfloat16),
            value_rows,
            preferred_element_type=jnp.float32,
        )
        .reshape(tokens_here, local_width)
        .astype(jnp.bfloat16)
    )
    attn_out = lax.psum(jnp.dot(context, out_mat, preferred_element_type=jnp.float32), "tp")
    middle = stream + attn_out
    normed_two_f, norm_two_back = jax.vjp(layer_norm, middle, gain_two, norm_gains[3])
    normed_two = normed_two_f.astype(jnp.bfloat16)
    hidden_pre = jnp.dot(normed_two, up_mat, preferred_element_type=jnp.float32)
    hidden_f, gelu_back = jax.vjp(partial(jax.nn.gelu, approximate=False), hidden_pre)
    hidden = hidden_f.astype(jnp.bfloat16)
    branch = lax.psum(
        jnp.dot(hidden, down_mat, preferred_element_type=jnp.float32).astype(jnp.bfloat16), "tp"
    ).astype(jnp.float32)
    block_out = (middle + branch).astype(jnp.bfloat16)
    grad_down = jnp.einsum("tf,td->fd", hidden, upstream, preferred_element_type=jnp.float32)
    grad_hidden = jnp.einsum("td,fd->tf", upstream, down_mat, preferred_element_type=jnp.float32)
    grad_pre = gelu_back(grad_hidden)[0].astype(jnp.bfloat16)
    grad_up = jnp.einsum("td,tf->df", normed_two, grad_pre, preferred_element_type=jnp.float32)
    grad_normed_two = lax.psum(
        jnp.einsum("tf,df->td", grad_pre, up_mat, preferred_element_type=jnp.float32), "tp"
    )
    grad_middle_norm, grad_gain_two, grad_bias_two = norm_two_back(grad_normed_two)
    grad_middle = upstream.astype(jnp.float32) + grad_middle_norm
    grad_attn = grad_middle.astype(jnp.bfloat16)
    grad_outmat = jnp.einsum("tc,td->cd", context, grad_attn, preferred_element_type=jnp.float32)
    grad_context = (
        jnp.einsum("td,cd->tc", grad_attn, out_mat, preferred_element_type=jnp.float32)
        .astype(jnp.bfloat16)
        .reshape(split_shape)
    )
    probs_again = jnp.exp(masked_scores(query_rows, key_rows, same_item, score_scale) - log_total)
    grad_values = jnp.einsum(
        "hts,thd->shd",
        probs_again.astype(jnp.bfloat16),
        grad_context,
        preferred_element_type=jnp.float32,
    )
    grad_probs = jnp.einsum(
        "thd,shd->hts", grad_context, value_rows, preferred_element_type=jnp.float32
    )
    inner_sum = jnp.sum(grad_probs * probs_again, axis=-1, keepdims=True)
    grad_scores = (probs_again * (grad_probs - inner_sum)).astype(jnp.bfloat16)
    grad_query = (
        jnp.einsum("hts,shd->thd", grad_scores, key_rows, preferred_element_type=jnp.float32)
        * score_scale
    )
    grad_key = (
        jnp.einsum("hts,thd->shd", grad_scores, query_rows, preferred_element_type=jnp.float32)
        * score_scale
    )
    grad_triple = (
        jnp.stack([grad_query, grad_key, grad_values])
        .reshape(3, tokens_here, local_width)
        .astype(jnp.bfloat16)
    )
    grad_qkv = jnp.einsum("td,jte->dje", normed, grad_triple, preferred_element_type=jnp.float32)
    grad_normed = lax.psum(
        jnp.einsum("jte,dje->td", grad_triple, qkv_mat, preferred_element_type=jnp.float32).astype(
            jnp.bfloat16
        ),
        "tp",
    ).astype(jnp.float32)
    grad_stream_norm, grad_gain_one, grad_bias_one = norm_one_back(grad_normed)
    grad_input = grad_middle + grad_stream_norm
    grad_norms = jnp.stack([grad_gain_one, grad_bias_one, grad_gain_two, grad_bias_two])
    return (block_out, grad_input, (grad_qkv, grad_outmat, grad_up, grad_down, grad_norms))


def local(
    inputs,
    cotangent,
    item_ids,
    timestep,
    qkv_weight,
    out_weight,
    up_weight,
    down_weight,
    norm_params,
    qkv_first,
    out_first,
    up_first,
    down_first,
    norm_first,
    qkv_second,
    out_second,
    up_second,
    down_second,
    norm_second,
):
    micro_count = inputs.shape[0]
    embeds = time_embed(timestep[:, 0], inputs.shape[2])
    qkv_low = qkv_weight.astype(jnp.bfloat16)
    out_low = out_weight.astype(jnp.bfloat16)
    up_low = up_weight.astype(jnp.bfloat16)
    down_low = down_weight.astype(jnp.bfloat16)
    norm_low = norm_params.astype(jnp.bfloat16)
    block_list = []
    input_list = []
    for number in range(micro_count):
        gathered = (
            lax.all_gather(qkv_low, "dp", axis=0, tiled=True),
            lax.all_gather(out_low, "dp", axis=1, tiled=True),
            lax.all_gather(up_low, "dp", axis=0, tiled=True),
            lax.all_gather(down_low, "dp", axis=1, tiled=True),
            lax.all_gather(norm_low, "dp", axis=1, tiled=True),
        )
        block_out, grad_input, grad_list = one_micro(
            gathered, inputs[number], cotangent[number], item_ids[number], embeds[number]
        )
        owned_grads = (
            lax.psum_scatter(grad_list[0], "dp", scatter_dimension=0, tiled=True),
            lax.psum_scatter(grad_list[1], "dp", scatter_dimension=1, tiled=True),
            lax.psum_scatter(grad_list[2], "dp", scatter_dimension=0, tiled=True),
            lax.psum_scatter(grad_list[3], "dp", scatter_dimension=1, tiled=True),
            lax.psum_scatter(grad_list[4], "dp", scatter_dimension=1, tiled=True),
        )
        if number == 0:
            totals = tuple(owned_grads)
        else:
            totals = tuple((left + right for left, right in zip(totals, owned_grads)))
        block_list.append(block_out)
        input_list.append(grad_input)
    own_squares = jnp.sum(totals[0] * totals[0]) + jnp.sum(totals[1] * totals[1])
    own_squares = own_squares + jnp.sum(totals[2] * totals[2]) + jnp.sum(totals[3] * totals[3])
    norm_squares = jnp.sum(totals[4] * totals[4])
    own_squares = own_squares + jnp.where(
        lax.axis_index("tp") == 0, norm_squares, jnp.zeros_like(norm_squares)
    )
    grad_norm = jnp.sqrt(lax.psum(own_squares, ("dp", "tp")))
    factor = jnp.minimum(1.0, clip_limit / (grad_norm + 1e-06))
    weights = (qkv_weight, out_weight, up_weight, down_weight, norm_params)
    firsts = (qkv_first, out_first, up_first, down_first, norm_first)
    seconds = (qkv_second, out_second, up_second, down_second, norm_second)
    result = [
        adam_step(weights[index], totals[index] * factor, firsts[index], seconds[index])
        for index in range(5)
    ]
    return (
        jnp.stack(block_list),
        jnp.stack(input_list),
        grad_norm,
        result[0][0],
        result[0][1],
        result[0][2],
        result[1][0],
        result[1][1],
        result[1][2],
        result[2][0],
        result[2][1],
        result[2][2],
        result[3][0],
        result[3][1],
        result[3][2],
        result[4][0],
        result[4][1],
        result[4][2],
    )


def solution(mesh):
    n_dp, n_tp = mesh.shape["dp"], mesh.shape["tp"]

    def step(*args):
        micro, tok, width = args[0].shape
        own_rows, _, local_width = args[4].shape
        fits = n_tp == 4 and n_dp == 8 and micro == 2 and tok == 512 and own_rows == 96
        if fits and local_width == 3 * HEAD_DIM and width % 256 == 0 and args[6].shape[1] % 256 == 0:
            return fast_local(n_dp, n_tp, *args)
        return local(*args)

    return jax.shard_map(
        step,
        mesh=mesh,
        in_specs=(
            P(None, "dp", None),
            P(None, "dp", None),
            P(None, "dp"),
            P(None, "dp"),
            P("dp", None, "tp"),
            P("tp", "dp"),
            P("dp", "tp"),
            P("tp", "dp"),
            P(None, "dp"),
            P("dp", None, "tp"),
            P("tp", "dp"),
            P("dp", "tp"),
            P("tp", "dp"),
            P(None, "dp"),
            P("dp", None, "tp"),
            P("tp", "dp"),
            P("dp", "tp"),
            P("tp", "dp"),
            P(None, "dp"),
        ),
        out_specs=(
            P(None, "dp", None),
            P(None, "dp", None),
            P(),
            P("dp", None, "tp"),
            P("dp", None, "tp"),
            P("dp", None, "tp"),
            P("tp", "dp"),
            P("tp", "dp"),
            P("tp", "dp"),
            P("dp", "tp"),
            P("dp", "tp"),
            P("dp", "tp"),
            P("tp", "dp"),
            P("tp", "dp"),
            P("tp", "dp"),
            P(None, "dp"),
            P(None, "dp"),
            P(None, "dp"),
        ),
        check_vma=False,
    )
```

```python
from functools import partial
import math

import jax
import jax.numpy as jnp
from jax import lax
from jax.experimental import pallas as pl
from jax.experimental.pallas import tpu as pltpu
from jax.sharding import PartitionSpec as P

HEAD_DIM = 64
STEP = 10

norm_eps = 1e-05
clip_limit = 1.0
learn_rate = 0.02
beta_one = 0.9
beta_two = 0.999
adam_eps = 1e-08
weight_decay = 0.01

BF = jnp.bfloat16
F32 = jnp.float32
MESH = pl.DeviceIdType.MESH


def time_embed(step_values, model_width):
    half_width = model_width // 2
    frequency = jnp.exp(
        jnp.arange(half_width, dtype=jnp.float32) * (-math.log(10000.0) / half_width)
    )
    angles = step_values.astype(jnp.float32)[..., None] * frequency
    return jnp.concatenate([jnp.sin(angles), jnp.cos(angles)], axis=-1)


def adam_step(weight, gradient, first_old, second_old):
    first_new = beta_one * first_old + (1.0 - beta_one) * gradient
    second_new = beta_two * second_old + (1.0 - beta_two) * gradient * gradient
    moment_one = first_new / (1.0 - beta_one**STEP)
    moment_two = second_new / (1.0 - beta_two**STEP)
    weight_new = weight - learn_rate * (
        moment_one / (jnp.sqrt(moment_two) + adam_eps) + weight_decay * weight
    )
    return (weight_new, first_new, second_new)


def mm(a, b, ca, cb):
    return lax.dot_general(a, b, (((ca,), (cb,)), ((), ())), preferred_element_type=F32)


def fold(v):
    cut = v.shape[-2] // 2
    low = jnp.concatenate([v[..., :cut, 128:], v[..., cut:, 128:]], axis=-1)
    return jnp.concatenate([v[..., :128], low], axis=-2)


def unfold(p):
    rows = 2 * p.shape[-2] // 3
    low = p[..., rows:, :]
    right = jnp.concatenate([low[..., :64], low[..., 64:]], axis=-2)
    return jnp.concatenate([p[..., :rows, :], right], axis=-1)


def layer_kernel(
    dims,
    x_in, cot_in, ids_ref, step_ref, wqkv_ref, wout_ref, wup_ref, wdown_ref, wnorm_ref,
    bo_ref, ig_ref, ga_ref, go_ref, gb_ref, gn_ref, gs_ref,
    x_ref, cot_ref, emb, lc, npin, ga, go, gb, gn, gs,
    wag, wqkv, woall, wo4, wb, npg, npt,
    normed, qkv, probs, ctx, ctxp, ctxr, n2, hid, dpre, mid, dmid, bo_own, dattn, dqkv,
    csend, crecv, own, ysend, yrecv, bsend, brecv, bown, bysend, byrecv,
    gfa, gfo, gfb, rax_s, rax_r, raz_s, raz_r, rbx_s, rbx_r, rbz_s, rbz_r,
    nacc, ncore, nsum, sqd, sqt,
    az_s, az_r, ax_s, ax_r, np_s, np_r, oy_s, oy_r, oc_s, oc_r, cx_s, cx_r,
    c_s, c_r, y_s, y_r, g_s, g_r, o_l, in_l,
    rx_s, rx_r, rz_s, rz_r, nc_s, nc_r, nd_s, nd_r, qd_s, qd_r, qt_s, qt_r,
):
    micro, tok, width, n_dp, n_tp, heads = dims
    n_z = n_dp // 2
    half = tok // 2
    own_rows = width // n_dp
    fold_rows = 3 * own_rows // 2
    local = heads * HEAD_DIM
    scale = 1.0 / math.sqrt(HEAD_DIM)

    dp = lax.axis_index("dp")
    tp = lax.axis_index("tp")
    z, xx = lax.div(dp, 2), lax.rem(dp, 2)
    yy, cc = lax.div(tp, 2), lax.rem(tp, 2)
    across_tp = 2 * (1 - yy) + cc
    x_peer = (2 * z + 1 - xx, tp)
    c_peer = (dp, 2 * yy + 1 - cc)
    y_peer = (dp, across_tp)
    d_peer = (dp, 2 * (1 - yy) + 1 - cc)

    far = lax.div(z, 2)
    column = (z + 1 - 2 * lax.rem(z, 2), 2 - far, 3 - 3 * far)
    inner = (z > 0) & (z < n_z - 1)
    near_peer = (2 * column[0] + xx, tp)
    mid_peer = (2 * column[1] + xx, tp)
    flip = 1 - xx

    def dp_of(k):
        return lax.rem(dp + k, n_dp)

    def tp_of(k):
        return lax.rem(tp + k, n_tp)

    sent, sent_inner, puts = [], [], []

    def put(i, held, there):
        item = pltpu.make_async_copy(held, there, in_l.at[2 + i])
        item.start()
        puts.append(item)

    def copy(src, dst, s_sem, r_sem, peer):
        return pltpu.make_async_remote_copy(
            src_ref=src, dst_ref=dst, send_sem=s_sem, recv_sem=r_sem, device_id=peer, device_id_type=MESH
        )

    def send(src, dst, s_sem, r_sem, peer):
        item = copy(src, dst, s_sem, r_sem, peer)
        item.start()
        sent.append(item)

    def send_inner(src, dst, s_sem, r_sem, peer):
        item = copy(src, dst, s_sem, r_sem, peer)
        pl.when(inner)(item.start)
        sent_inner.append(item)

    def settle(count):
        for item in sent[:count]:
            item.wait_send()
        for item in sent_inner:
            pl.when(inner)(item.wait_send)
        del sent[:count]
        sent_inner.clear()

    def arrive(dst, s_sem, r_sem, peer):
        copy(dst, dst, s_sem, r_sem, peer).wait_recv()

    barrier = pltpu.get_barrier_semaphore()
    for k in range(1, n_dp):
        pl.semaphore_signal(barrier, inc=1, device_id=(dp_of(k), tp), device_id_type=MESH)
    for k in range(1, n_tp):
        pl.semaphore_signal(barrier, inc=1, device_id=(dp, tp_of(k)), device_id_type=MESH)
    loads = [
        pltpu.make_async_copy(x_in, x_ref, in_l.at[0]),
        pltpu.make_async_copy(cot_in, cot_ref, in_l.at[1]),
    ]
    for load in loads:
        load.start()
    for i in range(3):
        wag[dp, :, 128 * i : 128 * (i + 1)] = fold(wqkv_ref[i]).astype(BF)
    wag[dp, :, 384:512] = fold(wout_ref[...].T).astype(BF)
    wb[0, dp] = wup_ref[...].astype(BF)
    wb[1, dp] = wdown_ref[...].astype(BF)
    npin[...] = jnp.zeros_like(npin)
    npin[:4, :own_rows] = wnorm_ref[...].astype(BF)
    place = lax.broadcasted_iota(jnp.int32, (1, width // 2), 1).astype(F32)
    rates = jnp.exp(place * (-math.log(10000.0) / (width // 2)))
    for m in range(micro):
        angles = step_ref[:, m : m + 1].astype(F32) * rates
        emb[m : m + 1, : width // 2] = jnp.sin(angles)
        emb[m : m + 1, width // 2 :] = jnp.cos(angles)
    labels = ids_ref[...].astype(F32)
    columns = jnp.concatenate([labels] * (8 // micro), axis=0).T
    for m in range(micro):
        lc[m] = columns[:, m : m + 1]

    pl.semaphore_wait(barrier, n_dp + n_tp - 2)

    def rows_of(j):
        return pl.ds(pl.multiple_of(j * own_rows, own_rows), own_rows)

    def half_rows(h):
        return pl.ds(pl.multiple_of(h * half, half), half)

    mine = half_rows(cc)
    other = half_rows(1 - cc)

    def ag_at(g, j):
        if g < 2:
            return wag.at[j, :, pl.ds(384 * g, 384 - 256 * g)]
        return wb.at[g - 2, j]

    def ag_column(g):
        block = ag_at(g, dp)
        send(block, block, az_s.at[g, 0], az_r.at[g, 0], near_peer)
        send_inner(block, block, az_s.at[g, 1], az_r.at[g, 1], mid_peer)

    def ag_side(g):
        send(ag_at(g, dp), ag_at(g, dp), ax_s.at[g, 3], ax_r.at[g, z], x_peer)

    def ag_pass(g, *which):
        for i in which:
            s = column[i]
            block = ag_at(g, 2 * s + xx)
            arrive(block, az_s.at[g, 0], az_r.at[g, i], near_peer)
            send_inner(block, block, az_s.at[g, 2 + i], az_r.at[g, i or 2], near_peer if i else mid_peer)
            send(block, block, ax_s.at[g, i], ax_r.at[g, s], x_peer)

    def ag_done(g, *which):
        for i in which or range(4):
            s = (*column, z)[i]
            arrive(ag_at(g, 2 * s + flip), ax_s.at[g, i], ax_r.at[g, s], x_peer)

    def o_send(col, which):
        for i in which:
            j = 2 * (*column, z)[i] + col
            part = ag_at(1, j)
            send(part, woall.at[tp, j], oy_s.at[j], oy_r.at[j], y_peer)

    def o_core():
        woall[tp] = wag[:, :, 384:512]
        send(woall.at[tp], woall.at[tp], oc_s.at[0], oc_r.at[0], c_peer)

    def o_across():
        for j in range(n_dp):
            arrive(woall.at[across_tp, j], oy_s.at[j], oy_r.at[j], y_peer)
        send(woall.at[across_tp], woall.at[across_tp], oc_s.at[1], oc_r.at[1], c_peer)

    def o_done():
        arrive(woall.at[2 * yy + 1 - cc], oc_s.at[0], oc_r.at[0], c_peer)
        arrive(woall.at[2 * (1 - yy) + 1 - cc], oc_s.at[1], oc_r.at[1], c_peer)
        for t in range(n_tp):
            wo4[t] = unfold(woall[t]).reshape(width, local)

    def ar_refs(kind, m):
        if kind < 2:
            return csend.at[kind, m], crecv.at[kind, m], own.at[m], ysend.at[kind, m], yrecv.at[kind, m]
        return [r.at[kind - 2, m] for r in (bsend, brecv, bown, bysend, byrecv)]

    def ar_start(kind, m, part):
        here, there, keep, _, _ = ar_refs(kind, m)
        here[...] = part(other).astype(BF)
        send(here, there, c_s.at[kind, m], c_r.at[kind, m], c_peer)
        keep[...] = part(mine)

    def ar_cross(kind, m):
        _, there, keep, here, across = ar_refs(kind, m)
        arrive(there, c_s.at[kind, m], c_r.at[kind, m], c_peer)
        here[...] = (keep[...] + there[...].astype(F32)).astype(BF)
        send(here, across, y_s.at[kind, m], y_r.at[kind, m], y_peer)

    def ar_total(kind, m):
        _, _, _, here, across = ar_refs(kind, m)
        arrive(across, y_s.at[kind, m], y_r.at[kind, m], y_peer)
        return here[...].astype(F32) + across[...].astype(F32)

    def share(i, m, ref):
        send(ref.at[m, mine], ref.at[m, mine], g_s.at[i, m], g_r.at[i, m], c_peer)

    def shared(i, m, ref):
        arrive(ref.at[m, other], g_s.at[i, m], g_r.at[i, m], c_peer)

    def centred(v):
        c0 = v - jnp.mean(v, axis=-1, keepdims=True)
        return c0, lax.rsqrt(jnp.mean(c0 * c0, axis=-1, keepdims=True) + norm_eps)

    def norm_back(grad, hat, inv, gain):
        dhat = grad * gain
        return inv * (
            dhat
            - jnp.mean(dhat, axis=-1, keepdims=True)
            - hat * jnp.mean(dhat * hat, axis=-1, keepdims=True)
        )

    def open_norms():
        block = lax.broadcasted_iota(jnp.int32, (n_dp, 128, width), 0)
        row = lax.broadcasted_iota(jnp.int32, (n_dp, 128, width), 1)
        col = lax.broadcasted_iota(jnp.int32, (n_dp, 128, width), 2)
        place = ((col == block * own_rows + row) & (row < own_rows)).astype(F32).astype(BF)
        rows = npg[0]
        total = mm(rows, place[0], 1, 0)
        for j in range(1, n_dp):
            total = total + mm(npg[j], place[j], 1, 0)
        npt[...] = total

    def gain_row(i):
        return 1.0 + npt[pl.ds(i, 1), :]

    def bias_row(i):
        return npt[pl.ds(i, 1), :]

    def stream_of(m, rows):
        return x_ref[m, rows, :].astype(F32) + emb[pl.ds(m, 1), :]

    def first_norm(m):
        c0, inv = centred(stream_of(m, pl.ds(0, tok)))
        normed[m] = (c0 * inv * gain_row(0) + bias_row(1)).astype(BF)

    def open_qkv():
        for i in range(3):
            wqkv[i] = unfold(wag[:, :, 128 * i : 128 * (i + 1)]).reshape(width, local)

    def project(m):
        for i in range(3):
            qkv[i, m] = mm(normed[m], wqkv[i], 1, 0).astype(BF)

    lane = lax.broadcasted_iota(jnp.int32, (1, local), 1)

    def head_mask(h, value):
        here = (lane >= h * HEAD_DIM) & (lane < (h + 1) * HEAD_DIM)
        return jnp.where(here, value, 0.0).astype(BF)

    def attend(m, *between):
        same = lc[m] == ids_ref[pl.ds(m, 1), :].astype(F32)
        total = None
        for h in range(heads):
            s = mm(qkv[0, m] * head_mask(h, scale), qkv[1, m], 1, 1)
            s = jnp.where(same, s, -1e30)
            e = jnp.exp(s - jnp.max(s, axis=-1, keepdims=True))
            p = e * (1.0 / jnp.sum(e, axis=-1, keepdims=True))
            probs[m * heads + h] = p
            part = mm(p.astype(BF), qkv[2, m] * head_mask(h, 1.0), 1, 0)
            total = part if total is None else total + part
            for work in between[h] if h < len(between) else ():
                work()
        ctx[m] = total.astype(BF)
        for i in range(2):
            ctxp[m, i] = fold(total[i * half : (i + 1) * half]).astype(BF)
        send(ctxp.at[m, cc], ctxr.at[m, tp], cx_s.at[m, 1], cx_r.at[m, 1], y_peer)
        send(ctxp.at[m, 1 - cc], ctxr.at[m, tp], cx_s.at[m, 2], cx_r.at[m, 2], d_peer)
        send(ctxp.at[m, 1 - cc], ctxr.at[m, tp], cx_s.at[m, 0], cx_r.at[m, 0], c_peer)
        ctxr[m, tp] = ctxp[m, cc]

    def second_norm(m):
        arrive(ctxr.at[m, 2 * yy + 1 - cc], cx_s.at[m, 0], cx_r.at[m, 0], c_peer)
        arrive(ctxr.at[m, across_tp], cx_s.at[m, 1], cx_r.at[m, 1], y_peer)
        arrive(ctxr.at[m, 2 * (1 - yy) + 1 - cc], cx_s.at[m, 2], cx_r.at[m, 2], d_peer)
        middle = stream_of(m, mine)
        for t in range(n_tp):
            middle = middle + mm(unfold(ctxr[m, t]), wo4[t], 1, 1)
        mid[m] = middle
        c0, inv = centred(middle)
        n2[m, mine, :] = (c0 * inv * gain_row(2) + bias_row(3)).astype(BF)
        share(0, m, n2)

    def wide(g):
        return wb[g].reshape(width, wb.shape[-1])

    def feed(m):
        shared(0, m, n2)
        pre = mm(n2[m], wide(0), 1, 0)
        cdf = 0.5 * (1.0 + lax.erf(pre * math.sqrt(0.5)))
        hid[m] = (pre * cdf).astype(BF)
        slope = cdf + pre * (jnp.exp(-0.5 * pre * pre) * (1.0 / math.sqrt(2.0 * math.pi)))
        if m == 0:
            gfb[0, :tok, :] = slope
        else:
            dmid[...] = slope.reshape(2, half, slope.shape[-1])

    def dn2_part(m):
        def part(rows):
            at = 1 - cc if rows is other else cc
            slope = gfb[0, rows, :] if m == 0 else dmid[at]
            grad = (mm(cot_ref[m, rows, :], wide(1), 1, 0) * slope).astype(BF)
            dpre[m, rows, :] = grad
            return mm(grad, wide(0), 1, 1)

        return part

    def branch_part(m, side):
        def part(rows):
            blocks = wb[1, pl.ds(side * n_z, n_z)]
            return mm(hid[m, rows, :], blocks.reshape(width // 2, blocks.shape[-1]), 1, 1)

        return part

    def col_sum(v):
        return jnp.sum(v, axis=0, keepdims=True)

    def second_back(m):
        grad = ar_total(0, m)
        c0, inv = centred(mid[m])
        hat = c0 * inv
        nacc[m, pl.ds(0, 1), :] = col_sum(grad * hat)
        nacc[m, pl.ds(1, 1), :] = col_sum(grad)
        grad_middle = cot_ref[m, mine, :].astype(F32) + norm_back(grad, hat, inv, gain_row(2))
        dmid[m] = grad_middle
        dattn[m, mine, :] = grad_middle.astype(BF)
        share(1, m, dattn)

    def finish_block(m):
        near, away = ar_total(2, m), ar_total(3, m)
        left = jnp.where(far == 0, near, away)
        right = jnp.where(far == 0, away, near)
        bo_own[m] = (mid[m] + jnp.concatenate([left, right], axis=1)).astype(BF)
        send(bo_own.at[m], bo_ref.at[m, mine], g_s.at[2, m], g_r.at[2, m], c_peer)
        pltpu.make_async_copy(bo_own.at[m], bo_ref.at[m, mine], o_l.at[0, m]).start()

    def attend_back(m, *between):
        shared(1, m, dattn)
        wo_own = wo4[tp]
        dctx = mm(dattn[m], wo_own, 1, 0).astype(BF)
        dq = dk = dv = None
        for h in range(heads):
            dch = dctx * head_mask(h, 1.0)
            p = probs[m * heads + h]
            dp_ = mm(dch, qkv[2, m], 1, 1)
            inner = jnp.sum(dp_ * p, axis=-1, keepdims=True)
            ds = (p * (dp_ - inner)).astype(BF)
            mask = head_mask(h, scale)
            a = mm(ds, qkv[1, m] * mask, 1, 0)
            b = mm(ds, qkv[0, m] * mask, 0, 0)
            c = mm(p.astype(BF), dch, 0, 0)
            dq = a if dq is None else dq + a
            dk = b if dk is None else dk + b
            dv = c if dv is None else dv + c
            for work in between[h] if h < len(between) else ():
                work()
        dqkv[0, m] = dq.astype(BF)
        dqkv[1, m] = dk.astype(BF)
        dqkv[2, m] = dv.astype(BF)

    def dn1_part(m):
        def part(rows):
            total = mm(dqkv[0, m, rows, :], wqkv[0], 1, 1)
            for i in range(1, 3):
                total = total + mm(dqkv[i, m, rows, :], wqkv[i], 1, 1)
            return total

        return part

    def first_back(m):
        grad = ar_total(1, m)
        c0, inv = centred(stream_of(m, mine))
        hat = c0 * inv
        nacc[m, pl.ds(2, 1), :] = col_sum(grad * hat)
        nacc[m, pl.ds(3, 1), :] = col_sum(grad)
        dmid[m] = dmid[m] + norm_back(grad, hat, inv, gain_row(0))
        send(dmid.at[m], ig_ref.at[m, mine], g_s.at[3, m], g_r.at[3, m], c_peer)
        pltpu.make_async_copy(dmid.at[m], ig_ref.at[m, mine], o_l.at[1, m]).start()

    def gf(g, at, col):
        if g == 0:
            return gfa.at[2 * at + col]
        return gfo.at[2 * at + col] if g == 1 else gfb.at[g - 2, rows_of(2 * at + col)]

    def rs_slots(g, at):
        if g < 2:
            lanes = pl.ds(384 * g, 384 - 256 * g)
            return [r.at[at, :, lanes] for r in (rax_s, rax_r, raz_s, raz_r)]
        return [r.at[g - 2, at] for r in (rbx_s, rbx_r, rbz_s, rbz_r)]

    def flat(ref):
        return ref[...].reshape(micro * tok, ref.shape[-1])

    def rs_wide(g, left, right):
        gfb[g - 2] = mm(flat(left), flat(right), 0, 0)

    def folded(left, right):
        return fold(mm(left, right, 0, 0).reshape(n_dp, own_rows, local))

    def rs_out():
        gfo[...] = folded(flat(dattn), flat(ctx))

    def rs_qkv(m):
        for i in range(3):
            lanes = slice(128 * i, 128 * (i + 1))
            grad = folded(normed[m], dqkv[i, m])
            gfa[:, :, lanes] = grad if m == 0 else gfa[:, :, lanes] + grad

    def rs_start(g):
        for i in (2, 1, 0, 3):
            at = (*column, z)[i]
            here, there, _, _ = rs_slots(g, at)
            here[...] = gf(g, at, flip)[...].astype(BF)
            send(here, there, rx_s.at[g, i], rx_r.at[g, at], x_peer)

    def rs_sum(g, i):
        at = (*column, z)[i]
        there = rs_slots(g, at)[1]
        arrive(there, rx_s.at[g, i], rx_r.at[g, at], x_peer)
        return gf(g, at, xx)[...] + there[...].astype(F32)

    def rs_pass(g, *which):
        for i in which:
            at = column[i]
            here = rs_slots(g, at)[2]
            here[...] = rs_sum(g, i).astype(BF)
            send(here, rs_slots(g, z)[3], rz_s.at[g, i], rz_r.at[g, z], (2 * at + xx, tp))

    def rs_finish(g):
        total = rs_sum(g, 3)
        for i in range(3):
            s = column[i]
            there = rs_slots(g, s)[3]
            arrive(there, rz_s.at[g, i], rz_r.at[g, s], (2 * s + xx, tp))
            total = total + there[...].astype(F32)
        if g == 0:
            for i in range(3):
                ga[i] = unfold(total[:, 128 * i : 128 * (i + 1)])
            put(0, ga, ga_ref)
        elif g == 1:
            go[...] = unfold(total).T
            put(1, go, go_ref)
        else:
            gb[g - 2] = total
            put(g, gb.at[g - 2], gb_ref.at[g - 2])
        return jnp.sum(col_sum(total * total), axis=1, keepdims=True)

    def norm_start(e):
        both = nacc[0, pl.ds(2 * e, 2), :]
        for m in range(1, micro):
            both = both + nacc[m, pl.ds(2 * e, 2), :]
        ncore[e, 0] = both
        send(ncore.at[e, 0], ncore.at[e, 1], nc_s.at[e], nc_r.at[e], c_peer)

    def norm_cross(e):
        arrive(ncore.at[e, 1], nc_s.at[e], nc_r.at[e], c_peer)
        nsum[e, dp] = ncore[e, 0] + ncore[e, 1]
        for k in range(1, n_dp):
            send(nsum.at[e, dp], nsum.at[e, dp], nd_s.at[e, k], nd_r.at[e, k], (dp_of(k), tp))

    def norm_finish(e):
        for k in range(1, n_dp):
            j = lax.rem(dp + n_dp - k, n_dp)
            arrive(nsum.at[e, j], nd_s.at[e, k], nd_r.at[e, k], (dp_of(k), tp))
        total = nsum[e, 0]
        for j in range(1, n_dp):
            total = total + nsum[e, j]
        mine_only = jnp.zeros((2, own_rows), F32)
        for j in range(n_dp):
            mine_only = jnp.where(dp == j, total[:, j * own_rows : (j + 1) * own_rows], mine_only)
        gn[pl.ds(2 - 2 * e, 2), :] = mine_only
        return jnp.sum(col_sum(total * total), axis=1, keepdims=True)

    ag_side(0)
    ag_column(0)
    ag_column(1)
    ag_side(1)
    npg[dp] = npin[...]
    for k in range(1, n_dp):
        send(npin, npg.at[dp], np_s.at[k], np_r.at[k], (dp_of(k), tp))
    o_send(xx, (3,))
    ag_pass(0, 0)
    for k in range(1, n_dp):
        arrive(npg.at[lax.rem(dp + n_dp - k, n_dp)], np_s.at[k], np_r.at[k], (dp_of(k), tp))
    open_norms()
    loads[0].wait()
    ag_pass(0, 1)
    first_norm(0)
    ag_pass(0, 2)
    ag_pass(1, 0)
    ag_column(2)
    ag_side(2)
    first_norm(1)
    ag_pass(1, 1, 2)
    ag_done(0)
    open_qkv()
    project(0)
    ag_column(3)
    o_send(xx, (0, 1, 2))
    project(1)
    ag_pass(2, 0)

    def o_rest():
        ag_done(1)
        o_send(flip, (0, 1, 2, 3))
        o_core()

    attend(0, (o_rest,))
    ag_pass(2, 1, 2)
    ag_side(3)
    ag_pass(3, 0)
    attend(1)
    ag_pass(3, 1)
    o_across()
    o_done()
    second_norm(0)
    second_norm(1)
    ag_done(2)
    feed(0)
    ag_done(3, 0, 3)
    ar_start(2, 0, branch_part(0, far))
    ag_pass(3, 2)
    feed(1)
    ar_cross(2, 0)
    ar_start(2, 1, branch_part(1, far))
    loads[1].wait()
    rs_wide(3, cot_ref, hid)
    ar_cross(2, 1)
    ag_done(3, 1, 2)
    ar_start(0, 0, dn2_part(0))
    rs_start(3)
    ar_cross(0, 0)
    ar_start(0, 1, dn2_part(1))
    rs_wide(2, n2, dpre)
    ar_cross(0, 1)
    rs_start(2)
    rs_pass(3, 2, 1)
    second_back(0)
    rs_pass(3, 0)
    attend_back(0)
    ar_start(1, 0, dn1_part(0))
    rs_pass(2, 2)
    ar_cross(1, 0)
    rs_qkv(0)
    second_back(1)
    rs_pass(2, 1)
    norm_start(0)
    early = len(sent)
    attend_back(1, (rs_out, partial(rs_start, 1), partial(rs_pass, 2, 0)), (partial(norm_cross, 0),))
    rs_qkv(1)
    rs_start(0)
    ar_start(1, 1, dn1_part(1))
    rs_pass(1, 2, 1, 0)
    ar_cross(1, 1)
    ar_start(3, 0, branch_part(0, 1 - far))
    ar_start(3, 1, branch_part(1, 1 - far))
    ar_cross(3, 0)
    ar_cross(3, 1)
    first_back(0)
    rs_pass(0, 2, 1)
    squares = rs_finish(3) + rs_finish(2)
    squares = squares + rs_finish(1)
    rs_pass(0, 0)
    settle(early)
    first_back(1)
    norm_start(1)
    norm_cross(1)
    squares = squares + rs_finish(0)
    sqd[dp] = jnp.broadcast_to(squares, (8, 128))
    for k in range(1, n_dp):
        send(sqd.at[dp], sqd.at[dp], qd_s.at[k], qd_r.at[k], (dp_of(k), tp))
    finish_block(0)
    extra = norm_finish(0) + norm_finish(1)
    for k in range(1, n_dp):
        j = lax.rem(dp + n_dp - k, n_dp)
        arrive(sqd.at[j], qd_s.at[k], qd_r.at[k], (dp_of(k), tp))
    mesh_row = sqd[0]
    for j in range(1, n_dp):
        mesh_row = mesh_row + sqd[j]
    sqt[tp] = mesh_row
    for k in range(1, n_tp):
        send(sqt.at[tp], sqt.at[tp], qt_s.at[k], qt_r.at[k], (dp, tp_of(k)))
    finish_block(1)
    for k in range(1, n_tp):
        j = lax.rem(tp + n_tp - k, n_tp)
        arrive(sqt.at[j], qt_s.at[k], qt_r.at[k], (dp, tp_of(k)))
    everything = sqt[0]
    for j in range(1, n_tp):
        everything = everything + sqt[j]
    gs[...] = jnp.sqrt(everything + extra)
    put(4, gn, gn_ref)
    put(5, gs, gs_ref)
    for m in range(micro):
        arrive(bo_ref.at[m, other], g_s.at[2, m], g_r.at[2, m], c_peer)
        arrive(ig_ref.at[m, other], g_s.at[3, m], g_r.at[3, m], c_peer)
        pltpu.make_async_copy(bo_own.at[m], bo_ref.at[m, mine], o_l.at[0, m]).wait()
        pltpu.make_async_copy(dmid.at[m], ig_ref.at[m, mine], o_l.at[1, m]).wait()
    for item in puts:
        item.wait()
    settle(len(sent))


def layer_call(n_dp, n_tp, inputs, cotangent, item_ids, timestep, qkv, out, up, down, norms):
    micro, tok, width = inputs.shape
    own_rows, ff = up.shape
    local = qkv.shape[2]
    fold_rows = 3 * own_rows // 2
    heads = local // HEAD_DIM
    half = tok // 2
    fold_half = 3 * half // 2
    dims = (micro, tok, width, n_dp, n_tp, heads)
    V = pltpu.VMEM
    DMA = pltpu.SemaphoreType.DMA
    n_z = n_dp // 2
    scratch = [
        V((micro, tok, width), BF), V((micro, tok, width), BF), V((micro, width), F32), V((micro, tok, 1), F32), V((8, 128), BF),
        V((3, own_rows, local), F32), V((local, own_rows), F32), V((2, own_rows, ff), F32), V((4, own_rows), F32), V((8, 128), F32),
        V((n_dp, fold_rows, 512), BF), V((3, width, local), BF), V((n_tp, n_dp, fold_rows, 128), BF),
        V((n_tp, width, local), BF), V((2, n_dp, own_rows, ff), BF), V((n_dp, 8, 128), BF), V((8, width), F32),
        V((micro, tok, width), BF), V((3, micro, tok, local), BF), V((micro * heads, tok, tok), F32),
        V((micro, tok, local), BF), V((micro, 2, fold_half, 128), BF), V((micro, n_tp, fold_half, 128), BF),
        V((micro, tok, width), BF), V((micro, tok, ff), BF), V((micro, tok, ff), BF),
        V((micro, half, width), F32), V((micro, half, width), F32), V((micro, half, width), BF),
        V((micro, tok, width), BF), V((3, micro, tok, local), BF),
        V((2, micro, half, width), BF), V((2, micro, half, width), BF), V((micro, half, width), F32),
        V((2, micro, half, width), BF), V((2, micro, half, width), BF),
        V((2, micro, half, width // 2), BF), V((2, micro, half, width // 2), BF), V((2, micro, half, width // 2), F32),
        V((2, micro, half, width // 2), BF), V((2, micro, half, width // 2), BF),
        V((n_dp, fold_rows, 384), F32), V((n_dp, fold_rows, 128), F32), V((2, width, ff), F32),
        V((n_z, fold_rows, 512), BF), V((n_z, fold_rows, 512), BF), V((n_z, fold_rows, 512), BF), V((n_z, fold_rows, 512), BF),
        V((2, n_z, own_rows, ff), BF), V((2, n_z, own_rows, ff), BF), V((2, n_z, own_rows, ff), BF), V((2, n_z, own_rows, ff), BF),
        V((micro, 8, width), F32), V((2, 2, 2, width), F32), V((2, n_dp, 2, width), F32),
        V((n_dp, 8, 128), F32), V((n_tp, 8, 128), F32),
        DMA((4, 5)), DMA((4, 3)), DMA((4, n_z)), DMA((4, n_z)), DMA((n_dp,)), DMA((n_dp,)), DMA((n_dp,)), DMA((n_dp,)), DMA((2,)), DMA((2,)),
        DMA((micro, 3)), DMA((micro, 3)),
        DMA((4, micro)), DMA((4, micro)), DMA((4, micro)), DMA((4, micro)), DMA((4, micro)), DMA((4, micro)),
        DMA((2, micro)), DMA((8,)),
        DMA((4, n_z)), DMA((4, n_z)), DMA((4, n_z)), DMA((4, n_z)), DMA((2,)), DMA((2,)), DMA((2, n_dp)), DMA((2, n_dp)),
        DMA((n_dp,)), DMA((n_dp,)), DMA((n_tp,)), DMA((n_tp,)),
    ]
    vm = pl.BlockSpec(memory_space=pltpu.VMEM)
    anywhere = pl.BlockSpec(memory_space=pl.ANY)
    S = jax.ShapeDtypeStruct
    return pl.pallas_call(
        partial(layer_kernel, dims),
        out_shape=(
            S((micro, tok, width), BF), S((micro, tok, width), F32),
            S((3, own_rows, local), F32), S((local, own_rows), F32), S((2, own_rows, ff), F32),
            S((4, own_rows), F32), S((8, 128), F32),
        ),
        in_specs=[anywhere] * 2 + [vm] * 7,
        out_specs=[anywhere] * 7,
        scratch_shapes=scratch,
        compiler_params=pltpu.CompilerParams(
            collective_id=0, has_side_effects=True, vmem_limit_bytes=63 << 20
        ),
        name="layer",
    )(inputs, cotangent, item_ids, timestep, qkv, out, up, down, norms)


def adam_kernel(*refs):
    bo_in, ig_in, gs_ref = refs[:3]
    olds = refs[7:22]
    bo_ref, ig_ref, norm_ref = refs[22:25]
    news = refs[25:40]
    loaded, stored = refs[40:55], refs[55:70]
    bo_held, ig_held, ga, go, gb, gn, in_sem, out_sem, move_sem, grad_sem = refs[70:]
    grads = (ga, go, gb.at[0], gb.at[1], gn)
    held_grads = (ga, go, gb, gn)
    gets = [pltpu.make_async_copy(refs[3 + i], held_grads[i], grad_sem.at[i]) for i in range(4)]
    got = (0, 1, 2, None, 3)
    takes, moves = [], []
    for n, (there, held, here) in enumerate(((ig_in, ig_held, ig_ref), (bo_in, bo_held, bo_ref))):
        takes.append(pltpu.make_async_copy(there, held, move_sem.at[0, n]))
        moves.append(pltpu.make_async_copy(held, here, move_sem.at[1, n]))
    loads = [pltpu.make_async_copy(olds[i], loaded[i], in_sem.at[i]) for i in range(15)]
    stores = [pltpu.make_async_copy(stored[i], news[i], out_sem.at[i]) for i in range(15)]
    for item in (gets[0], *loads[:3], *gets[1:]):
        item.start()
    for take in takes:
        take.start()
    for load in loads[3:]:
        load.start()
    grad_norm = gs_ref[pl.ds(0, 1), pl.ds(0, 1)]
    norm_ref[...] = grad_norm
    factor = jnp.minimum(1.0, clip_limit / (grad_norm + 1e-06))
    for p in range(5):
        if got[p] is not None:
            gets[got[p]].wait()
        for i in range(3):
            loads[3 * p + i].wait()
        weight, first, second = loaded[3 * p : 3 * p + 3]
        results = adam_step(weight[...], grads[p][...] * factor, first[...], second[...])
        for i in range(3):
            stored[3 * p + i][...] = results[i]
            stores[3 * p + i].start()
        if p == 0:
            for take, move in zip(takes, moves):
                take.wait()
                move.start()
    for store in stores:
        store.wait()
    for move in moves:
        move.wait()


def adam_call(block_out, grad_input, gs, grads, olds):
    vm = pl.BlockSpec(memory_space=pltpu.VMEM)
    anywhere = pl.BlockSpec(memory_space=pl.ANY)
    S = jax.ShapeDtypeStruct
    like = [S(o.shape, o.dtype) for o in olds]
    return pl.pallas_call(
        adam_kernel,
        out_shape=(
            S(block_out.shape, block_out.dtype), S(grad_input.shape, grad_input.dtype), S((1, 1), F32), *like
        ),
        in_specs=[anywhere] * 2 + [vm] + [anywhere] * 19,
        out_specs=(anywhere, anywhere, vm, *[anywhere] * 15),
        scratch_shapes=[pltpu.VMEM(o.shape, o.dtype) for o in olds] * 2
        + [pltpu.VMEM(block_out.shape, block_out.dtype), pltpu.VMEM(grad_input.shape, grad_input.dtype)]
        + [pltpu.VMEM(g.shape, g.dtype) for g in grads]
        + [pltpu.SemaphoreType.DMA((15,)), pltpu.SemaphoreType.DMA((15,)), pltpu.SemaphoreType.DMA((2, 2)), pltpu.SemaphoreType.DMA((4,))],
        compiler_params=pltpu.CompilerParams(vmem_limit_bytes=63 << 20),
        name="adam",
    )(block_out, grad_input, gs, *grads, *olds)


def fast_local(
    n_dp, n_tp,
    inputs, cotangent, item_ids, timestep, qkv_weight, out_weight, up_weight, down_weight, norm_params,
    qkv_first, out_first, up_first, down_first, norm_first,
    qkv_second, out_second, up_second, down_second, norm_second,
):
    def turned(qkv, out, up, down, norms):
        return (jnp.moveaxis(qkv, 1, 0), out, up, down.T, norms)

    weights = turned(qkv_weight, out_weight, up_weight, down_weight, norm_params)
    firsts = turned(qkv_first, out_first, up_first, down_first, norm_first)
    seconds = turned(qkv_second, out_second, up_second, down_second, norm_second)
    block_out, grad_input, ga, go, gb, gn, gs = layer_call(
        n_dp, n_tp, inputs, cotangent, item_ids, timestep.T, *weights
    )
    olds = [item for p in range(5) for item in (weights[p], firsts[p], seconds[p])]
    block_out, grad_input, grad_norm, *news = adam_call(block_out, grad_input, gs, (ga, go, gb, gn), olds)
    for i in range(3):
        news[i] = jnp.moveaxis(news[i], 0, 1)
        news[9 + i] = news[9 + i].T
    return (block_out, grad_input, grad_norm[0, 0], *news)


def layer_norm(values, gain_row, bias_row):
    centre = values - jnp.mean(values, axis=-1, keepdims=True)
    spread = jnp.mean(centre * centre, axis=-1, keepdims=True)
    return centre * lax.rsqrt(spread + norm_eps) * gain_row + bias_row


def masked_scores(query_rows, key_rows, same_item, score_scale):
    scores = (
        jnp.einsum("thd,shd->hts", query_rows, key_rows, preferred_element_type=jnp.float32)
        * score_scale
    )
    return jnp.where(same_item, scores, -1e30)


def one_micro(gathered, stream_in, upstream, labels, embed_row):
    qkv_mat, out_mat, up_mat, down_mat, norm_rows = gathered
    tokens_here = stream_in.shape[0]
    local_width = out_mat.shape[0]
    heads_here = local_width // HEAD_DIM
    score_scale = 1.0 / math.sqrt(HEAD_DIM)
    split_shape = (tokens_here, heads_here, HEAD_DIM)
    norm_gains = norm_rows.astype(jnp.float32)
    gain_one = 1.0 + norm_gains[0]
    gain_two = 1.0 + norm_gains[2]
    stream = stream_in.astype(jnp.float32) + embed_row[None, :]
    normed_f, norm_one_back = jax.vjp(layer_norm, stream, gain_one, norm_gains[1])
    normed = normed_f.astype(jnp.bfloat16)
    triple = jnp.einsum("td,dje->jte", normed, qkv_mat, preferred_element_type=jnp.float32).astype(
        jnp.bfloat16
    )
    query_rows = triple[0].reshape(split_shape)
    key_rows = triple[1].reshape(split_shape)
    value_rows = triple[2].reshape(split_shape)
    same_item = (labels[:, None] == labels[None, :])[None]
    scores = masked_scores(query_rows, key_rows, same_item, score_scale)
    row_top = jnp.max(scores, axis=-1, keepdims=True)
    exp_scores = jnp.exp(scores - row_top)
    row_total = jnp.sum(exp_scores, axis=-1, keepdims=True)
    probs_soft = exp_scores / row_total
    log_total = row_top + jnp.log(row_total)
    context = (
        jnp.einsum(
            "hts,shd->thd",
            probs_soft.astype(jnp.bfloat16),
            value_rows,
            preferred_element_type=jnp.float32,
        )
        .reshape(tokens_here, local_width)
        .astype(jnp.bfloat16)
    )
    attn_out = lax.psum(jnp.dot(context, out_mat, preferred_element_type=jnp.float32), "tp")
    middle = stream + attn_out
    normed_two_f, norm_two_back = jax.vjp(layer_norm, middle, gain_two, norm_gains[3])
    normed_two = normed_two_f.astype(jnp.bfloat16)
    hidden_pre = jnp.dot(normed_two, up_mat, preferred_element_type=jnp.float32)
    hidden_f, gelu_back = jax.vjp(partial(jax.nn.gelu, approximate=False), hidden_pre)
    hidden = hidden_f.astype(jnp.bfloat16)
    branch = lax.psum(
        jnp.dot(hidden, down_mat, preferred_element_type=jnp.float32).astype(jnp.bfloat16), "tp"
    ).astype(jnp.float32)
    block_out = (middle + branch).astype(jnp.bfloat16)
    grad_down = jnp.einsum("tf,td->fd", hidden, upstream, preferred_element_type=jnp.float32)
    grad_hidden = jnp.einsum("td,fd->tf", upstream, down_mat, preferred_element_type=jnp.float32)
    grad_pre = gelu_back(grad_hidden)[0].astype(jnp.bfloat16)
    grad_up = jnp.einsum("td,tf->df", normed_two, grad_pre, preferred_element_type=jnp.float32)
    grad_normed_two = lax.psum(
        jnp.einsum("tf,df->td", grad_pre, up_mat, preferred_element_type=jnp.float32), "tp"
    )
    grad_middle_norm, grad_gain_two, grad_bias_two = norm_two_back(grad_normed_two)
    grad_middle = upstream.astype(jnp.float32) + grad_middle_norm
    grad_attn = grad_middle.astype(jnp.bfloat16)
    grad_outmat = jnp.einsum("tc,td->cd", context, grad_attn, preferred_element_type=jnp.float32)
    grad_context = (
        jnp.einsum("td,cd->tc", grad_attn, out_mat, preferred_element_type=jnp.float32)
        .astype(jnp.bfloat16)
        .reshape(split_shape)
    )
    probs_again = jnp.exp(masked_scores(query_rows, key_rows, same_item, score_scale) - log_total)
    grad_values = jnp.einsum(
        "hts,thd->shd",
        probs_again.astype(jnp.bfloat16),
        grad_context,
        preferred_element_type=jnp.float32,
    )
    grad_probs = jnp.einsum(
        "thd,shd->hts", grad_context, value_rows, preferred_element_type=jnp.float32
    )
    inner_sum = jnp.sum(grad_probs * probs_again, axis=-1, keepdims=True)
    grad_scores = (probs_again * (grad_probs - inner_sum)).astype(jnp.bfloat16)
    grad_query = (
        jnp.einsum("hts,shd->thd", grad_scores, key_rows, preferred_element_type=jnp.float32)
        * score_scale
    )
    grad_key = (
        jnp.einsum("hts,thd->shd", grad_scores, query_rows, preferred_element_type=jnp.float32)
        * score_scale
    )
    grad_triple = (
        jnp.stack([grad_query, grad_key, grad_values])
        .reshape(3, tokens_here, local_width)
        .astype(jnp.bfloat16)
    )
    grad_qkv = jnp.einsum("td,jte->dje", normed, grad_triple, preferred_element_type=jnp.float32)
    grad_normed = lax.psum(
        jnp.einsum("jte,dje->td", grad_triple, qkv_mat, preferred_element_type=jnp.float32).astype(
            jnp.bfloat16
        ),
        "tp",
    ).astype(jnp.float32)
    grad_stream_norm, grad_gain_one, grad_bias_one = norm_one_back(grad_normed)
    grad_input = grad_middle + grad_stream_norm
    grad_norms = jnp.stack([grad_gain_one, grad_bias_one, grad_gain_two, grad_bias_two])
    return (block_out, grad_input, (grad_qkv, grad_outmat, grad_up, grad_down, grad_norms))


def local(
    inputs,
    cotangent,
    item_ids,
    timestep,
    qkv_weight,
    out_weight,
    up_weight,
    down_weight,
    norm_params,
    qkv_first,
    out_first,
    up_first,
    down_first,
    norm_first,
    qkv_second,
    out_second,
    up_second,
    down_second,
    norm_second,
):
    micro_count = inputs.shape[0]
    embeds = time_embed(timestep[:, 0], inputs.shape[2])
    qkv_low = qkv_weight.astype(jnp.bfloat16)
    out_low = out_weight.astype(jnp.bfloat16)
    up_low = up_weight.astype(jnp.bfloat16)
    down_low = down_weight.astype(jnp.bfloat16)
    norm_low = norm_params.astype(jnp.bfloat16)
    block_list = []
    input_list = []
    for number in range(micro_count):
        gathered = (
            lax.all_gather(qkv_low, "dp", axis=0, tiled=True),
            lax.all_gather(out_low, "dp", axis=1, tiled=True),
            lax.all_gather(up_low, "dp", axis=0, tiled=True),
            lax.all_gather(down_low, "dp", axis=1, tiled=True),
            lax.all_gather(norm_low, "dp", axis=1, tiled=True),
        )
        block_out, grad_input, grad_list = one_micro(
            gathered, inputs[number], cotangent[number], item_ids[number], embeds[number]
        )
        owned_grads = (
            lax.psum_scatter(grad_list[0], "dp", scatter_dimension=0, tiled=True),
            lax.psum_scatter(grad_list[1], "dp", scatter_dimension=1, tiled=True),
            lax.psum_scatter(grad_list[2], "dp", scatter_dimension=0, tiled=True),
            lax.psum_scatter(grad_list[3], "dp", scatter_dimension=1, tiled=True),
            lax.psum_scatter(grad_list[4], "dp", scatter_dimension=1, tiled=True),
        )
        if number == 0:
            totals = tuple(owned_grads)
        else:
            totals = tuple((left + right for left, right in zip(totals, owned_grads)))
        block_list.append(block_out)
        input_list.append(grad_input)
    own_squares = jnp.sum(totals[0] * totals[0]) + jnp.sum(totals[1] * totals[1])
    own_squares = own_squares + jnp.sum(totals[2] * totals[2]) + jnp.sum(totals[3] * totals[3])
    norm_squares = jnp.sum(totals[4] * totals[4])
    own_squares = own_squares + jnp.where(
        lax.axis_index("tp") == 0, norm_squares, jnp.zeros_like(norm_squares)
    )
    grad_norm = jnp.sqrt(lax.psum(own_squares, ("dp", "tp")))
    factor = jnp.minimum(1.0, clip_limit / (grad_norm + 1e-06))
    weights = (qkv_weight, out_weight, up_weight, down_weight, norm_params)
    firsts = (qkv_first, out_first, up_first, down_first, norm_first)
    seconds = (qkv_second, out_second, up_second, down_second, norm_second)
    result = [
        adam_step(weights[index], totals[index] * factor, firsts[index], seconds[index])
        for index in range(5)
    ]
    return (
        jnp.stack(block_list),
        jnp.stack(input_list),
        grad_norm,
        result[0][0],
        result[0][1],
        result[0][2],
        result[1][0],
        result[1][1],
        result[1][2],
        result[2][0],
        result[2][1],
        result[2][2],
        result[3][0],
        result[3][1],
        result[3][2],
        result[4][0],
        result[4][1],
        result[4][2],
    )


def solution(mesh):
    n_dp, n_tp = mesh.shape["dp"], mesh.shape["tp"]

    def step(*args):
        micro, tok, width = args[0].shape
        own_rows, _, local_width = args[4].shape
        fits = n_tp == 4 and n_dp == 8 and micro == 2 and tok == 512 and own_rows == 96
        if fits and local_width == 3 * HEAD_DIM and width % 256 == 0 and args[6].shape[1] % 256 == 0:
            return fast_local(n_dp, n_tp, *args)
        return local(*args)

    return jax.shard_map(
        step,
        mesh=mesh,
        in_specs=(
            P(None, "dp", None),
            P(None, "dp", None),
            P(None, "dp"),
            P(None, "dp"),
            P("dp", None, "tp"),
            P("tp", "dp"),
            P("dp", "tp"),
            P("tp", "dp"),
            P(None, "dp"),
            P("dp", None, "tp"),
            P("tp", "dp"),
            P("dp", "tp"),
            P("tp", "dp"),
            P(None, "dp"),
            P("dp", None, "tp"),
            P("tp", "dp"),
            P("dp", "tp"),
            P("tp", "dp"),
            P(None, "dp"),
        ),
        out_specs=(
            P(None, "dp", None),
            P(None, "dp", None),
            P(),
            P("dp", None, "tp"),
            P("dp", None, "tp"),
            P("dp", None, "tp"),
            P("tp", "dp"),
            P("tp", "dp"),
            P("tp", "dp"),
            P("dp", "tp"),
            P("dp", "tp"),
            P("dp", "tp"),
            P("tp", "dp"),
            P("tp", "dp"),
            P("tp", "dp"),
            P(None, "dp"),
            P(None, "dp"),
            P(None, "dp"),
        ),
        check_vma=False,
    )
```
